128 devices in a mesh: gx: 16 (over y, x_hi, core), gy: 8 (over z, x_lo).
Axes of the slice: x: 4 (x_hi: 2, x_lo: 2; x = x_hi * 2 + x_lo), y: 4, z: 4, core: 2. Of those that a mesh axis runs over, the one named last changes fastest.
Arguments:
- forces: float32 [3, 24, 32, 64, 128], P(None, None, 'gx', 'gy'), may hold values from -6 to 6
- levels: int32 [32, 64, 128], P('gx', 'gy'), may hold values from 0 to 15
- supports: int32 [32, 64, 128], P('gx', 'gy'), may hold values 0 or 1
Outputs:
- filtered: float32 [32, 64, 128], P('gx', 'gy')
The draws below stay inside these ranges and needn't reach their ends.
All inputs are finite; a program needn't handle non-finite values. No bound on the sum of `supports` on one device may be relied on, other than what follows from the above.
Results may differ from the reference program's by a relative error of at most 0.0001.
Values sent between devices are 32-bit elements; how exact they have to be, the bound alone decides.
A program may use at most 128 MiB of HBM per device.

```python
import math
import jax
import jax.numpy as jnp
import numpy as np
from jax import lax

NZ = 128
CASES = 24
LEVELS = 16
ITERS = 2
NX = 32
NY = 64


def place_ends(values, own_key, least, largest):
    dims = values.shape
    place = [jax.random.randint(jax.random.fold_in(own_key, axis), (), 0, dims[axis]) for axis in range(len(dims))]
    values = values.at[tuple(place)].set(least)
    longest = dims.index(max(dims))
    place[longest] = (place[longest] + 1) % dims[longest]
    return values.at[tuple(place)].set(largest)


def shard_levels(key, shape, shards, low, top_value):
    def one(dim, blocks):
        steps = jax.random.uniform(jax.random.fold_in(jax.random.fold_in(key, 6), dim), (blocks,), jnp.float32, low / len(shards), top_value / len(shards))
        return jnp.repeat(jnp.exp(steps), shape[dim] // blocks).reshape((-1,) + (1,) * (len(shape) - dim - 1))

    level = one(*shards[0])
    for cut in shards[1:]:
        level = level * one(*cut)
    return level


def noise(stream_key, dims, deviation, limit, shards=(), held_as=jnp.bfloat16):
    array = jax.random.normal(stream_key, dims, jnp.float32) * deviation
    if len(shards) > 0:
        array = shard_levels(stream_key, dims, shards, -0.22, 0.18) * array
    return jnp.clip(array, min=-limit, max=limit).astype(held_as)


def setup_inputs(seed: int = 0) -> dict:
    splits = jax.random.split(jax.random.key(seed), 4)
    return {
        "forces": noise(splits[0], (3, CASES, NX, NY, NZ), 1.0, 6.0, ((2, 16), (3, 8)), jnp.float32),
        "levels": place_ends(jax.random.randint(splits[1], (NX, NY, NZ), 0, LEVELS), jax.random.fold_in(splits[1], 1), 0, LEVELS - 1).astype(jnp.int32),
        "supports": place_ends((jax.random.randint(splits[2], (NX, NY, NZ), 0, 16) < 1).astype(jnp.int32), jax.random.fold_in(splits[2], 1), 0, 1),
    }


load_factor = 0.2

def element_matrix():
    poisson = 0.3
    lame_first = poisson / ((1.0 + poisson) * (1.0 - 2.0 * poisson))
    lame_shear = 1.0 / (2.0 * (1.0 + poisson))
    elastic = np.zeros((6, 6))
    elastic[:3, :3] = lame_first
    for position in range(3):
        elastic[position, position] += 2.0 * lame_shear
        elastic[position + 3, position + 3] = lame_shear
    points = [0.5 - 0.5 / math.sqrt(3.0), 0.5 + 0.5 / math.sqrt(3.0)]
    matrix = np.zeros((24, 24))
    for point_x in points:
        for point_y in points:
            for point_z in points:
                coords = (point_x, point_y, point_z)
                strain = np.zeros((6, 24))
                for corner in range(8):
                    corner_bits = (corner >> 2 & 1, corner >> 1 & 1, corner & 1)
                    shape_values = [coords[axis_n] if corner_bits[axis_n] else 1.0 - coords[axis_n] for axis_n in range(3)]
                    slopes = [1.0 if corner_bits[axis_n] else -1.0 for axis_n in range(3)]
                    slope_x = slopes[0] * shape_values[1] * shape_values[2]
                    slope_y = shape_values[0] * slopes[1] * shape_values[2]
                    slope_z = shape_values[0] * shape_values[1] * slopes[2]
                    offset = 3 * corner
                    strain[0, offset] = slope_x
                    strain[1, offset + 1] = slope_y
                    strain[2, offset + 2] = slope_z
                    strain[3, offset] = slope_y
                    strain[3, offset + 1] = slope_x
                    strain[4, offset + 1] = slope_z
                    strain[4, offset + 2] = slope_y
                    strain[5, offset] = slope_z
                    strain[5, offset + 2] = slope_x
                matrix = matrix + strain.T @ elastic @ strain / 8.0
    return matrix

def corner_stack(field_in, lead_in, span_x, span_y, span_z):
    pieces = []
    for corner in range(8):
        step_x, step_y, step_z = (corner >> 2 & 1, corner >> 1 & 1, corner & 1)
        pieces.append(field_in[:, :, lead_in + step_x:lead_in + step_x + span_x, lead_in + step_y:lead_in + step_y + span_y, lead_in + step_z:lead_in + step_z + span_z])
    stacked = jnp.stack(pieces, 0)
    return stacked.reshape((24,) + stacked.shape[2:])

def element_forces(extended, stiff_ext, element_stiff):
    span_x, span_y, span_z = (extended.shape[2] - 2, extended.shape[3] - 2, extended.shape[4] - 2)
    outputs = []
    for first_case in range(0, extended.shape[1], 6):
        case_group = extended[:, first_case:first_case + 6]
        gathered = corner_stack(case_group, 0, span_x + 1, span_y + 1, span_z + 1)
        product = jnp.einsum('ab,bcxyz->acxyz', element_stiff, gathered, precision=lax.Precision.HIGHEST) * stiff_ext
        product = product.reshape((8, 3) + product.shape[1:])
        summed = jnp.zeros((3, case_group.shape[1], span_x, span_y, span_z), jnp.float32)
        for corner in range(8):
            step_x, step_y, step_z = (corner >> 2 & 1, corner >> 1 & 1, corner & 1)
            summed = summed + product[corner][:, :, 1 - step_x:1 - step_x + span_x, 1 - step_y:1 - step_y + span_y, 1 - step_z:1 - step_z + span_z]
        outputs.append(summed)
    return jnp.concatenate(outputs, 1)

def element_energy(extended, element_stiff):
    span_x, span_y, span_z = (extended.shape[2] - 2, extended.shape[3] - 2, extended.shape[4] - 2)
    summed = jnp.zeros((span_x, span_y, span_z), jnp.float32)
    for first_case in range(0, extended.shape[1], 6):
        case_group = extended[:, first_case:first_case + 6]
        gathered = corner_stack(case_group, 1, span_x, span_y, span_z)
        product = jnp.einsum('ab,bcxyz->acxyz', element_stiff, gathered, precision=lax.Precision.HIGHEST)
        summed = summed + lax.optimization_barrier(jnp.sum(gathered * product, axis=(0, 1)))
    return summed

def node_diagonal(stiff_ext, free_mask, element_stiff):
    span_x, span_y, span_z = free_mask.shape
    parts = []
    for component in range(3):
        summed = jnp.zeros((span_x, span_y, span_z), jnp.float32)
        for corner in range(8):
            step_x, step_y, step_z = (corner >> 2 & 1, corner >> 1 & 1, corner & 1)
            summed = summed + stiff_ext[1 - step_x:1 - step_x + span_x, 1 - step_y:1 - step_y + span_y, 1 - step_z:1 - step_z + span_z] * element_stiff[3 * corner + component, 3 * corner + component]
        parts.append(summed)
    diagonal = jnp.stack(parts, 0)[:, None]
    return 1.0 / (free_mask * diagonal + (1.0 - free_mask))

def block_gram(first_field, second_field):
    return jnp.einsum('kcxyz,kdxyz->cd', first_field, second_field, precision=lax.Precision.HIGHEST)

def combine(field_in, mixing):
    return jnp.einsum('kcxyz,cd->kdxyz', field_in, mixing, precision=lax.Precision.HIGHEST)

def cone_filter(rimmed, density):
    span_x, span_y, span_z = density.shape
    numerator = jnp.zeros((span_x, span_y, span_z), jnp.float32)
    denominator = jnp.zeros((span_x, span_y, span_z), jnp.float32)
    for shift_x in range(-2, 3):
        for shift_y in range(-2, 3):
            for shift_z in range(-2, 3):
                weight = 2.5 - math.sqrt(shift_x * shift_x + shift_y * shift_y + shift_z * shift_z)
                if weight > 0.0:
                    window = rimmed[:, 2 + shift_x:2 + shift_x + span_x, 2 + shift_y:2 + shift_y + span_y, 2 + shift_z:2 + shift_z + span_z]
                    numerator = numerator + weight * window[0]
                    denominator = denominator + weight * window[1]
    return numerator / (density * denominator)

def reference(forces, levels, supports):
    element_stiff = jnp.asarray(element_matrix(), jnp.float32)
    free_mask = (1 - supports).astype(jnp.float32)
    density = 0.3 + 0.7 * levels.astype(jnp.float32) / (LEVELS - 1)
    stiffness = density ** 3
    stiff_ext = jnp.pad(stiffness, ((1, 0), (1, 0), (1, 0)))
    inverse = node_diagonal(stiff_ext, free_mask, element_stiff)

    def operate(field_in):
        extended = jnp.pad(free_mask * field_in, ((0, 0), (0, 0), (1, 1), (1, 1), (1, 1)))
        return free_mask * element_forces(extended, stiff_ext, element_stiff) + (1.0 - free_mask) * field_in
    load_field = load_factor * free_mask * forces
    solution = jnp.zeros_like(load_field)
    residual = load_field
    direction = inverse * residual
    for iteration in range(ITERS):
        image_field = operate(direction)
        curvature = block_gram(direction, image_field)
        factor = jnp.linalg.cholesky(curvature)
        step_alpha = jax.scipy.linalg.cho_solve((factor, True), block_gram(direction, residual))
        solution = solution + combine(direction, step_alpha)
        residual = residual - combine(image_field, step_alpha)
        if iteration + 1 < ITERS:
            scaled_res = inverse * residual
            step_beta = -jax.scipy.linalg.cho_solve((factor, True), block_gram(image_field, scaled_res))
            direction = scaled_res + combine(direction, step_beta)
    extended = jnp.pad(free_mask * solution, ((0, 0), (0, 0), (1, 1), (1, 1), (1, 1)))
    energy = element_energy(extended, element_stiff)
    sensitivity = -3.0 * density ** 2 * energy / CASES
    stacked = jnp.stack([density * sensitivity, jnp.ones_like(density)], 0)
    rimmed = jnp.pad(stacked, ((0, 0), (2, 2), (2, 2), (2, 2)))
    return cone_filter(rimmed, density)
```

```python
import functools
import math

import jax
import jax.numpy as jnp
import numpy as np
from jax import lax
from jax.experimental import pallas as pl
from jax.experimental.pallas import tpu as pltpu
from jax.sharding import PartitionSpec as P

MESH = pl.DeviceIdType.MESH
CASES = 24
LEVELS = 16
LOAD = 0.2
BX, BY, NZ = 2, 8, 128
CT = 3


def element_matrix():
    poisson = 0.3
    lame_first = poisson / ((1.0 + poisson) * (1.0 - 2.0 * poisson))
    lame_shear = 1.0 / (2.0 * (1.0 + poisson))
    elastic = np.zeros((6, 6))
    elastic[:3, :3] = lame_first
    for position in range(3):
        elastic[position, position] += 2.0 * lame_shear
        elastic[position + 3, position + 3] = lame_shear
    points = [0.5 - 0.5 / math.sqrt(3.0), 0.5 + 0.5 / math.sqrt(3.0)]
    matrix = np.zeros((24, 24))
    for point_x in points:
        for point_y in points:
            for point_z in points:
                coords = (point_x, point_y, point_z)
                strain = np.zeros((6, 24))
                for corner in range(8):
                    bits = (corner >> 2 & 1, corner >> 1 & 1, corner & 1)
                    shape = [coords[n] if bits[n] else 1.0 - coords[n] for n in range(3)]
                    slopes = [1.0 if bits[n] else -1.0 for n in range(3)]
                    slope_x = slopes[0] * shape[1] * shape[2]
                    slope_y = shape[0] * slopes[1] * shape[2]
                    slope_z = shape[0] * shape[1] * slopes[2]
                    o = 3 * corner
                    strain[0, o] = slope_x
                    strain[1, o + 1] = slope_y
                    strain[2, o + 2] = slope_z
                    strain[3, o] = slope_y
                    strain[3, o + 1] = slope_x
                    strain[4, o + 1] = slope_z
                    strain[4, o + 2] = slope_y
                    strain[5, o] = slope_z
                    strain[5, o + 2] = slope_x
                matrix = matrix + strain.T @ elastic @ strain / 8.0
    return matrix


KE = element_matrix()
DIAG = float(KE[0, 0])


def parity_matrix():
    walsh = np.ones((8, 8))
    for mode in range(8):
        for corner in range(8):
            for n in range(3):
                if mode >> n & 1:
                    walsh[mode, corner] *= 2 * (corner >> n & 1) - 1
    big = np.kron(walsh, np.eye(3))
    return big @ KE @ big.T / 64.0


KP = parity_matrix()
UNIT = ((1, 0, 0), (0, 1, 0), (0, 0, 1))


def _flip(p, k):
    return tuple(a ^ b for a, b in zip(p, UNIT[k]))


def _kp(m, n):
    at = [3 * (4 * p[0] + 2 * p[1] + p[2]) + k for k, p in (m, n)]
    return float(KP[at[0], at[1]])


NORMAL = [(k, UNIT[k]) for k in range(3)]
BEND = [(k, _flip((1, 1, 1), k)) for k in range(3)]
PAIRS = [[(k, _flip(UNIT[s], k)) for k in range(3) if k != s] for s in range(3)]
SHEAR = []
TWIST = []
for _s in range(3):
    _a, _b = [k for k in range(3) if k != _s]
    SHEAR.append([(_a, UNIT[_b]), (_b, UNIT[_a])])
    TWIST.append((_s, (1, 1, 1)))
N_OFF = _kp(NORMAL[0], NORMAL[1])
N_DIA = _kp(NORMAL[0], NORMAL[0]) - N_OFF
P_OFF = _kp(PAIRS[0][0], PAIRS[0][1])
P_DIA = _kp(PAIRS[0][0], PAIRS[0][0]) - P_OFF
S_ALL = _kp(SHEAR[0][0], SHEAR[0][0])
T_ALL = _kp(TWIST[0], TWIST[0])
B_OFF = _kp(BEND[0], BEND[1])
B_DIA = _kp(BEND[0], BEND[0]) - B_OFF


def _span(d, low, high, size):
    a = max(0, low + d * size)
    b = min(size, high + 1 + d * size)
    return a, a - d * size, b - a


NEIGHBOURS = [(dx, dy) for dx in (-1, 0, 1) for dy in (-1, 0, 1) if dx or dy]


def _shift(x, by):
    lane = lax.broadcasted_iota(jnp.int32, x.shape, x.ndim - 1)
    r = pltpu.roll(x, (-by) % NZ, axis=x.ndim - 1)
    ok = lane < NZ - by if by > 0 else lane >= -by
    return jnp.where(ok, r, 0.0)


def _stage(u_at, ex, y, ct):
    out = {}
    for k in range(3):
        u0, u1 = u_at(k, ex, y, ct), u_at(k, ex + 1, y, ct)
        for px, b in ((0, u0 + u1), (1, u1 - u0)):
            up = _shift(b, 1)
            out[k, px, 0] = b + up
            out[k, px, 1] = up - b
    return out


KEYS = [(k, px, pz) for k in range(3) for px in (0, 1) for pz in (0, 1)]


def _modes(s0, s1):
    out = {}
    for k, px, pz in KEYS:
        if (px, pz) != (0, 0):
            out[k, (px, 0, pz)] = s0[k, px, pz] + s1[k, px, pz]
        out[k, (px, 1, pz)] = s1[k, px, pz] - s0[k, px, pz]
    return out


def _stress(u, e):
    g = {}
    total = (u[NORMAL[0]] + u[NORMAL[1]] + u[NORMAL[2]]) * (e * N_OFF)
    dia = e * N_DIA
    for m in NORMAL:
        g[m] = u[m] * dia + total
    total = u[BEND[0]] + u[BEND[1]] + u[BEND[2]]
    total = total * (e * B_OFF)
    dia = e * B_DIA
    for m in BEND:
        g[m] = u[m] * dia + total
    off, dia = e * P_OFF, e * P_DIA
    for a, b in PAIRS:
        total = (u[a] + u[b]) * off
        g[a] = u[a] * dia + total
        g[b] = u[b] * dia + total
    both = e * S_ALL
    for a, b in SHEAR:
        g[a] = g[b] = (u[a] + u[b]) * both
    alone = e * T_ALL
    for m in TWIST:
        g[m] = u[m] * alone
    return g


def _density_of_energy(u):
    def sq(x):
        return x * x

    e = N_OFF * sq(u[NORMAL[0]] + u[NORMAL[1]] + u[NORMAL[2]])
    e = e + N_DIA * (sq(u[NORMAL[0]]) + sq(u[NORMAL[1]]) + sq(u[NORMAL[2]]))
    e = e + B_OFF * sq(u[BEND[0]] + u[BEND[1]] + u[BEND[2]])
    e = e + B_DIA * (sq(u[BEND[0]]) + sq(u[BEND[1]]) + sq(u[BEND[2]]))
    off = dia = she = twi = 0.0
    for a, b in PAIRS:
        off = off + sq(u[a] + u[b])
        dia = dia + sq(u[a]) + sq(u[b])
    for a, b in SHEAR:
        she = she + sq(u[a] + u[b])
    for m in TWIST:
        twi = twi + sq(u[m])
    return e + P_OFF * off + P_DIA * dia + S_ALL * she + T_ALL * twi


def _apply(u_at, e_at, add, layers, y_low, columns, close, unroll=2):
    def tile(ct, _):
        for ex in layers:
            first = _stage(u_at, ex, y_low, ct)
            zero = jnp.zeros((8, NZ), jnp.float32)

            def emit(y, h, ex=ex):
                for k in range(3):
                    p = []
                    for px in (0, 1):
                        s, d = h[k, px, 0], h[k, px, 1]
                        p.append((s - d) + _shift(s + d, -1))
                    add(k, ex, ex, y, ct, p[0] - p[1])
                    add(k, ex, ex + 1, y, ct, p[0] + p[1])

            def step(t, state, ex=ex):
                s0 = dict(zip(KEYS, state[0]))
                carry = dict(zip(KEYS, state[1]))
                y = y_low + t
                s1 = _stage(u_at, ex, y + 1, ct)
                g = _stress(_modes(s0, s1), e_at(ex, y))
                h, later = {}, {}
                for key in KEYS:
                    k, px, pz = key
                    g1 = g[k, (px, 1, pz)]
                    g0 = g.get((k, (px, 0, pz)))
                    if g0 is None:
                        h[key] = carry[key] - g1
                        later[key] = g1
                    else:
                        h[key] = carry[key] + (g0 - g1)
                        later[key] = g0 + g1
                emit(y, h)
                return tuple(s1[key] for key in KEYS), tuple(later[key] for key in KEYS)

            state = (tuple(first[key] for key in KEYS), (zero,) * len(KEYS))
            state = lax.fori_loop(0, columns, step, state, unroll=unroll)
            if close:
                emit(y_low + columns, dict(zip(KEYS, state[1])))
        return 0

    lax.fori_loop(0, CT, tile, 0)


def _split(x):
    scaled = x * 65537.0
    high = scaled - (scaled - x)
    return high.astype(jnp.bfloat16), (x - high).astype(jnp.bfloat16)


def _rows(x):
    return x.reshape(CASES, NZ)


def _nt(a, b):
    return lax.dot_general(a, b, (((1,), (1,)), ((), ())), preferred_element_type=jnp.float32)


def _solve(table):
    lane = lax.broadcasted_iota(jnp.int32, (CASES, NZ), 1)

    def left(x, by):
        return pltpu.roll(x, (-by) % NZ, axis=1)

    def join(a, b):
        return jnp.where(lane < 24, a, jnp.where(lane < 48, b, 0.0))

    blocks = [
        join(table, left(table, 24)),
        join(left(table, 48), left(table, 72)),
        join(left(table, 24), left(table, 48)),
    ]
    tiles = [b[8 * i : 8 * i + 8] for b in blocks for i in range(3)]
    lane8 = lax.broadcasted_iota(jnp.int32, (1, NZ), 1)
    scales = jnp.zeros((1, NZ), jnp.float32)
    for j in range(48):
        own = tiles[j // 8]
        row = own[j % 8 : j % 8 + 1]
        pivot = row[:, j : j + 1]
        scale = 1.0 / pivot
        factor = jnp.where(lane8 == j, 0.0, row * scale)
        scales = jnp.where(lane8 == j, scale, scales)
        live = range((j + 1) // 8, 9)
        for t in live:
            tiles[t] = tiles[t] - tiles[t][:, j : j + 1] * factor
    return jnp.concatenate(tiles[6:], 0) * scales


WEIGHT = {}
for _dx in range(-2, 3):
    for _dy in range(-2, 3):
        for _dz in range(3):
            _w = 2.5 - math.sqrt(_dx * _dx + _dy * _dy + _dz * _dz)
            if _w > 0.0:
                WEIGHT[_dx, _dy, _dz] = _w


def _cone(planes):
    result = []
    for xo in range(BX):
        total = jnp.zeros((BY, NZ), jnp.float32)
        for (dx, dy, dz), w in WEIGHT.items():
            total = total + w * planes(xo + 2 + dx, dy, dz)
        result.append(total)
    return result


def _kernel(nx, ny, phases, forces, levels, supports, out, nat, lev, sup, stiff, stiffz, inv, free, field, dire, masked,
            image, qf, qm, wf, split, disp, energy, vals, zsum, gram_send, gram_recv, local_sem, l_send, l_recv, s_send,
            s_recv, f_send, f_recv, v_send, v_recv, g_send, g_recv):
    i, j = lax.axis_index("gx"), lax.axis_index("gy")

    def there(dx, dy):
        return lax.rem(i + dx + nx, nx), lax.rem(j + dy + ny, ny)

    peers = [there(dx, dy) for dx, dy in NEIGHBOURS]
    for phase in phases:
        for ox, oy in phase:
            peers.append((i ^ ox, j ^ oy))

    c_nat = pltpu.make_async_copy(forces, nat, local_sem.at[0])
    c_lev = pltpu.make_async_copy(levels, lev.at[2 : 2 + BX, 2 : 2 + BY], local_sem.at[1])
    c_sup = pltpu.make_async_copy(supports, sup.at[1 : 1 + BX, 1 : 1 + BY], local_sem.at[2])
    c_nat.start()
    c_lev.start()
    c_sup.start()

    barrier = pltpu.get_barrier_semaphore()
    for peer in peers:
        pl.semaphore_signal(barrier, inc=1, device_id=peer, device_id_type=MESH)

    c_nat.wait()

    def arrange(t, _):
        k = t // (BX * BY)
        x = (t // BY) % BX
        y = t % BY
        rows = nat[pl.ds(k * (CASES * BX * BY) + x * BY + y, CASES, stride=BX * BY), :]
        field[k, 1 + x, 1 + y] = rows.reshape(CT, 8, NZ)
        return 0

    lax.fori_loop(0, 3 * BX * BY, arrange, 0, unroll=4)
    c_lev.wait()
    c_sup.wait()

    pl.semaphore_wait(barrier, len(peers))

    copies = []
    for n, (dx, dy) in enumerate(NEIGHBOURS):
        peer = there(dx, dy)
        (a, b, c), (d, e, f) = _span(dx, -2, 3, BX), _span(dy, -2, 9, BY)
        copies.append(pltpu.make_async_remote_copy(
            levels.at[a : a + c, d : d + f], lev.at[b + 2 : b + 2 + c, e + 2 : e + 2 + f],
            l_send.at[n], l_recv.at[n], device_id=peer, device_id_type=MESH))
        (a, b, c), (d, e, f) = _span(dx, -1, 3, BX), _span(dy, -1, 9, BY)
        copies.append(pltpu.make_async_remote_copy(
            supports.at[a : a + c, d : d + f], sup.at[b + 1 : b + 1 + c, e + 1 : e + 1 + f],
            s_send.at[n], s_recv.at[n], device_id=peer, device_id_type=MESH))
        copies.append(pltpu.make_async_remote_copy(
            field.at[:, a + 1 : a + 1 + c, d + 1 : d + 1 + f], field.at[:, b + 1 : b + 1 + c, e + 1 : e + 1 + f],
            f_send.at[n], f_recv.at[n], device_id=peer, device_id_type=MESH))
    for n in (0, 1):
        for copy in copies[n::3]:
            copy.start()
    for copy in copies[2::3]:
        copy.start()
    for n in (0, 1):
        for copy in copies[n::3]:
            copy.wait()

    def inside(x, y):
        gx, gy = i * BX + x, j * BY + y
        ok = (gx >= 0) & (gx < nx * BX) & (gy >= 0) & (gy < ny * BY)
        return jnp.where(ok, 1.0, 0.0).astype(jnp.float32)

    def moduli(t, _):
        x, y = t // (BY + 4), t % (BY + 4)
        level = jnp.broadcast_to(lev[x, y], (8, NZ)).astype(jnp.float32)
        rho = 0.3 + 0.7 * level / (LEVELS - 1)
        e = rho * rho * rho * inside(x - 2, y - 2)
        stiff[x, y] = e
        stiffz[x, y] = e + _shift(e, -1)
        return 0

    lax.fori_loop(0, (BX + 4) * (BY + 4), moduli, 0, unroll=2)

    def nodal(t, _):
        x, y = t // (BY + 3), t % (BY + 3)
        fr = (1 - jnp.broadcast_to(sup[x, y], (8, NZ))).astype(jnp.float32) * inside(x - 1, y - 1)
        total = stiffz[x, y] + stiffz[x + 1, y] + stiffz[x, y + 1] + stiffz[x + 1, y + 1]
        free[x, y] = fr
        inv[x, y] = 1.0 / (fr * (DIAG * total) + (1.0 - fr))
        return 0

    lax.fori_loop(0, (BX + 3) * (BY + 3), nodal, 0, unroll=2)

    for copy in copies[2::3]:
        copy.wait()

    def search(t, _):
        x, y = t // (BY + 3), t % (BY + 3)
        fr, iv = free[x, y], inv[x, y]
        for k in range(3):
            d = iv * (LOAD * fr * field[k, x, y])
            dire[k, x, y] = d
            masked[k, x, y] = fr * d
        return 0

    lax.fori_loop(0, (BX + 3) * (BY + 3), search, 0)

    def u_at(k, x, y, ct):
        return masked[k, x + 1, y + 1, ct]

    def e_at(x, y):
        return stiff[x + 2, y + 2]

    def add_image(k, ex, x, y, ct, value):
        if x < 0 or x > BX:
            return
        if x == ex:
            image[k, x, y + 1, ct] += value
        else:
            image[k, x, y + 1, ct] = value

    _apply(u_at, e_at, add_image, range(-1, BX + 1), -1, BY + 2, False)

    def above(x, y):
        fr, iv = free[x + 1, y + 1], inv[x + 1, y + 1]
        out = []
        for k in range(3):
            d = dire[k, x + 1, y + 1]
            im = fr * image[k, x, y + 1] + (1.0 - fr) * d
            q = iv * im
            qf[k, x, y] = q
            qm[k, x, y] = fr * q
            both = jnp.concatenate([_rows(d), _rows(q)], 0)
            high, low = _split(both)
            hl = jnp.concatenate([high, low], 0)
            split[k, x, y] = hl
            out.append((hl, im, fr))
        return out

    gap = jnp.zeros((16, NZ), jnp.bfloat16)

    def first_gram(t, acc):
        x, y = t // BY, t % BY
        for k, (hl, im, fr) in enumerate(above(x, y)):
            r0 = LOAD * fr * field[k, x + 1, y + 1]
            high, low = _split(jnp.concatenate([_rows(im), _rows(r0)], 0))
            acc = acc + _nt(hl, jnp.concatenate([high, gap, low, gap], 0))
        return acc

    acc = lax.fori_loop(0, BX * BY, first_gram, jnp.zeros((96, NZ), jnp.float32))

    def edge_x(y, _):
        above(BX, y)
        return 0

    def edge_y(x, _):
        above(x, BY)
        return 0

    lax.fori_loop(0, BY + 1, edge_x, 0)
    lax.fori_loop(0, BX, edge_y, 0)

    def q_at(k, x, y, ct):
        return qm[k, x, y, ct]

    def add_w(k, ex, x, y, ct, value):
        if x == ex and ex > 0:
            wf[k, x, y, ct] += value
        else:
            wf[k, x, y, ct] = value

    _apply(q_at, e_at, add_w, range(BX), 0, BY, True)

    gap8 = jnp.zeros((8, NZ), jnp.float32)
    gap32 = jnp.zeros((32, NZ), jnp.bfloat16)

    def second_gram(t, acc):
        x, y = t // (BY + 1), t % (BY + 1)
        fr = free[x + 1, y + 1]
        mine = jnp.where((x < BX) & (y < BY), 1.0, 0.0).astype(jnp.float32)
        for k in range(3):
            w = fr * wf[k, x, y] + (mine * (1.0 - fr)) * qf[k, x, y]
            high, low = _split(jnp.concatenate([_rows(w), gap8], 0))
            acc = acc + _nt(split[k, x, y], jnp.concatenate([high, gap32, low, gap32], 0))
        return acc

    acc2 = lax.fori_loop(0, (BX + 1) * (BY + 1), second_gram, jnp.zeros((96, NZ), jnp.float32))

    lane = lax.broadcasted_iota(jnp.int32, (CASES, NZ), 1)
    both = acc[:48] + acc[48:]
    both = both + pltpu.roll(both, 64, axis=1)
    last = acc2[24:48] + acc2[72:]
    last = last + pltpu.roll(last, 64, axis=1)
    table = jnp.where(
        lane < 48, both[:24], jnp.where(lane < 96, pltpu.roll(both[24:], 48, axis=1), pltpu.roll(last, 96, axis=1)))

    slot = 0
    for n, phase in enumerate(phases):
        gram_send[n] = table
        group = []
        for m, (ox, oy) in enumerate(phase):
            group.append(pltpu.make_async_remote_copy(
                gram_send.at[n], gram_recv.at[slot + m], g_send.at[slot + m], g_recv.at[slot + m],
                device_id=(i ^ ox, j ^ oy), device_id_type=MESH))
        for copy in group:
            copy.start()
        for copy in group:
            copy.wait()
        terms = [table] + [gram_recv[slot + m] for m in range(len(phase))]
        while len(terms) > 1:
            terms = [terms[t] + terms[t + 1] for t in range(0, len(terms), 2)]
        table = terms[0]
        slot += len(phase)

    mix = _solve(table)
    half = jnp.where(lane < 48, mix, 0.0)
    mix = half + pltpu.roll(half, 48, axis=1)
    mix = jnp.concatenate([mix, gap8], 0)
    high, low = _split(mix)
    coefs = jnp.concatenate([high, low], 0)[:, :96]

    def combine(t, _):
        x, y = t // (BY + 1), t % (BY + 1)
        fr = free[x + 1, y + 1]
        for k in range(3):
            u = jnp.dot(coefs, split[k, x, y], preferred_element_type=jnp.float32)
            u = u[:24] + u[32:56]
            disp[k, x, y] = fr * u.reshape(CT, 8, NZ)
        return 0

    lax.fori_loop(0, (BX + 1) * (BY + 1), combine, 0)

    def s_at(k, x, y, ct):
        return disp[k, x, y, ct]

    for x in range(BX):
        energy[x] = jnp.zeros((BY, 8, NZ), jnp.float32)

    def energies(ct, _):
        for x in range(BX):
            first = _stage(s_at, x, 0, ct)

            def step(y, state, x=x):
                s1 = _stage(s_at, x, y + 1, ct)
                energy[x, y] += _density_of_energy(_modes(dict(zip(KEYS, state)), s1))
                return tuple(s1[key] for key in KEYS)

            lax.fori_loop(0, BY, step, tuple(first[key] for key in KEYS), unroll=2)
        return 0

    lax.fori_loop(0, CT, energies, 0)

    rho = [0.3 + 0.7 * lev[2 + x, 2 : 2 + BY, 0, :].astype(jnp.float32) / (LEVELS - 1) for x in range(BX)]
    for x in range(BX):
        sens = -3.0 * rho[x] * rho[x] * jnp.sum(energy[x], axis=1) / CASES
        vals[2 + x, BY : 2 * BY] = rho[x] * sens
    group = []
    for n, (dx, dy) in enumerate(NEIGHBOURS):
        mine = vals.at[2 : 2 + BX, BY : 2 * BY]
        at_x, at_y = 2 - BX * dx, BY - BY * dy
        group.append(pltpu.make_async_remote_copy(
            mine, vals.at[at_x : at_x + BX, at_y : at_y + BY], v_send.at[n], v_recv.at[n],
            device_id=there(dx, dy), device_id_type=MESH))
    for copy in group:
        copy.start()

    grid_y = j * BY - BY + lax.broadcasted_iota(jnp.int32, (3 * BY, NZ), 0)
    ok_y = (grid_y >= 0) & (grid_y < ny * BY)

    def present(p):
        gx = i * BX + p - 2
        return jnp.where(ok_y & (gx >= 0) & (gx < nx * BX), 1.0, 0.0).astype(jnp.float32)

    def spread(p, v):
        zsum[p, 0] = v
        zsum[p, 1] = _shift(v, 1) + _shift(v, -1)
        zsum[p, 2] = _shift(v, 2) + _shift(v, -2)

    def near(p, dy, dz):
        return zsum[p, dz, BY + dy : 2 * BY + dy]

    for p in range(BX + 4):
        spread(p, present(p))
    weights = _cone(near)
    for copy in group:
        copy.wait()
    for p in range(BX + 4):
        spread(p, jnp.where(present(p) > 0.0, vals[p], 0.0))
    sums = _cone(near)
    for x in range(BX):
        out[x] = sums[x] / (rho[x] * weights[x])


def _phases(nx, ny):
    groups = [[(1, 0)], [(2, 0), (0, 1), (2, 1)]]
    groups.append([(4 * o, 0) for o in range(1, nx // 4)])
    groups.append([(0, 2 * o) for o in range(1, ny // 2)])
    return [g for g in groups if g]


def solution(mesh):
    nx, ny = mesh.shape["gx"], mesh.shape["gy"]
    phases = _phases(nx, ny)
    slots = sum(len(g) for g in phases)
    f32 = jnp.float32
    dma = pltpu.SemaphoreType.DMA
    any_space = pl.BlockSpec(memory_space=pl.ANY)

    def local(forces, levels, supports):
        return pl.pallas_call(
            functools.partial(_kernel, nx, ny, phases),
            out_shape=jax.ShapeDtypeStruct((BX, BY, NZ), f32),
            in_specs=[any_space] * 3,
            out_specs=pl.BlockSpec(memory_space=pltpu.VMEM),
            scratch_shapes=[
                pltpu.VMEM((3 * CASES * BX * BY, NZ), f32),
                pltpu.VMEM((BX + 4, BY + 4, 1, NZ), jnp.int32),
                pltpu.VMEM((BX + 3, BY + 3, 1, NZ), jnp.int32),
                pltpu.VMEM((BX + 4, BY + 4, 8, NZ), f32),
                pltpu.VMEM((BX + 4, BY + 4, 8, NZ), f32),
                pltpu.VMEM((BX + 3, BY + 3, 8, NZ), f32),
                pltpu.VMEM((BX + 3, BY + 3, 8, NZ), f32),
                pltpu.VMEM((3, BX + 3, BY + 3, CT, 8, NZ), f32),
                pltpu.VMEM((3, BX + 3, BY + 3, CT, 8, NZ), f32),
                pltpu.VMEM((3, BX + 3, BY + 3, CT, 8, NZ), f32),
                pltpu.VMEM((3, BX + 1, BY + 2, CT, 8, NZ), f32),
                pltpu.VMEM((3, BX + 1, BY + 1, CT, 8, NZ), f32),
                pltpu.VMEM((3, BX + 1, BY + 1, CT, 8, NZ), f32),
                pltpu.VMEM((3, BX + 1, BY + 1, CT, 8, NZ), f32),
                pltpu.VMEM((3, BX + 1, BY + 1, 96, NZ), jnp.bfloat16),
                pltpu.VMEM((3, BX + 1, BY + 1, CT, 8, NZ), f32),
                pltpu.VMEM((BX, BY, 8, NZ), f32),
                pltpu.VMEM((BX + 4, 3 * BY, NZ), f32),
                pltpu.VMEM((BX + 4, 3, 3 * BY, NZ), f32),
                pltpu.VMEM((len(phases), CASES, NZ), f32),
                pltpu.VMEM((slots, CASES, NZ), f32),
                dma((3,)),
                dma((8,)), dma((8,)), dma((8,)), dma((8,)), dma((8,)), dma((8,)), dma((8,)), dma((8,)),
                dma((slots,)), dma((slots,)),
            ],
            compiler_params=pltpu.CompilerParams(collective_id=0, has_side_effects=True),
        )(
            forces.reshape(3 * CASES * BX * BY, NZ),
            levels.reshape(BX, BY, 1, NZ),
            supports.reshape(BX, BY, 1, NZ),
        )

    return jax.shard_map(
        local,
        mesh=mesh,
        in_specs=(P(None, None, "gx", "gy", None), P("gx", "gy", None), P("gx", "gy", None)),
        out_specs=P("gx", "gy", None),
        check_vma=False,
    )
```

```python
import functools
import math

import jax
import jax.numpy as jnp
import numpy as np
from jax import lax
from jax.experimental import pallas as pl
from jax.experimental.pallas import tpu as pltpu
from jax.sharding import PartitionSpec as P

MESH = pl.DeviceIdType.MESH
CASES = 24
LEVELS = 16
LOAD = 0.2
BX, BY, NZ = 2, 8, 128
CT = 3


def element_matrix():
    poisson = 0.3
    lame_first = poisson / ((1.0 + poisson) * (1.0 - 2.0 * poisson))
    lame_shear = 1.0 / (2.0 * (1.0 + poisson))
    elastic = np.zeros((6, 6))
    elastic[:3, :3] = lame_first
    for position in range(3):
        elastic[position, position] += 2.0 * lame_shear
        elastic[position + 3, position + 3] = lame_shear
    points = [0.5 - 0.5 / math.sqrt(3.0), 0.5 + 0.5 / math.sqrt(3.0)]
    matrix = np.zeros((24, 24))
    for point_x in points:
        for point_y in points:
            for point_z in points:
                coords = (point_x, point_y, point_z)
                strain = np.zeros((6, 24))
                for corner in range(8):
                    bits = (corner >> 2 & 1, corner >> 1 & 1, corner & 1)
                    shape = [coords[n] if bits[n] else 1.0 - coords[n] for n in range(3)]
                    slopes = [1.0 if bits[n] else -1.0 for n in range(3)]
                    slope_x = slopes[0] * shape[1] * shape[2]
                    slope_y = shape[0] * slopes[1] * shape[2]
                    slope_z = shape[0] * shape[1] * slopes[2]
                    o = 3 * corner
                    strain[0, o] = slope_x
                    strain[1, o + 1] = slope_y
                    strain[2, o + 2] = slope_z
                    strain[3, o] = slope_y
                    strain[3, o + 1] = slope_x
                    strain[4, o + 1] = slope_z
                    strain[4, o + 2] = slope_y
                    strain[5, o] = slope_z
                    strain[5, o + 2] = slope_x
                matrix = matrix + strain.T @ elastic @ strain / 8.0
    return matrix


KE = element_matrix()
DIAG = float(KE[0, 0])


def parity_matrix():
    walsh = np.ones((8, 8))
    for mode in range(8):
        for corner in range(8):
            for n in range(3):
                if mode >> n & 1:
                    walsh[mode, corner] *= 2 * (corner >> n & 1) - 1
    big = np.kron(walsh, np.eye(3))
    return big @ KE @ big.T / 64.0


KP = parity_matrix()
UNIT = ((1, 0, 0), (0, 1, 0), (0, 0, 1))


def _flip(p, k):
    return tuple(a ^ b for a, b in zip(p, UNIT[k]))


def _kp(m, n):
    at = [3 * (4 * p[0] + 2 * p[1] + p[2]) + k for k, p in (m, n)]
    return float(KP[at[0], at[1]])


NORMAL = [(k, UNIT[k]) for k in range(3)]
BEND = [(k, _flip((1, 1, 1), k)) for k in range(3)]
PAIRS = [[(k, _flip(UNIT[s], k)) for k in range(3) if k != s] for s in range(3)]
SHEAR = []
TWIST = []
for _s in range(3):
    _a, _b = [k for k in range(3) if k != _s]
    SHEAR.append([(_a, UNIT[_b]), (_b, UNIT[_a])])
    TWIST.append((_s, (1, 1, 1)))
N_OFF = _kp(NORMAL[0], NORMAL[1])
N_DIA = _kp(NORMAL[0], NORMAL[0]) - N_OFF
P_OFF = _kp(PAIRS[0][0], PAIRS[0][1])
P_DIA = _kp(PAIRS[0][0], PAIRS[0][0]) - P_OFF
S_ALL = _kp(SHEAR[0][0], SHEAR[0][0])
T_ALL = _kp(TWIST[0], TWIST[0])
B_OFF = _kp(BEND[0], BEND[1])
B_DIA = _kp(BEND[0], BEND[0]) - B_OFF


def _span(d, low, high, size):
    a = max(0, low + d * size)
    b = min(size, high + 1 + d * size)
    return a, a - d * size, b - a


NEIGHBOURS = [(dx, dy) for dx in (-1, 0, 1) for dy in (-1, 0, 1) if dx or dy]


def _shift(x, by):
    lane = lax.broadcasted_iota(jnp.int32, x.shape, x.ndim - 1)
    r = pltpu.roll(x, (-by) % NZ, axis=x.ndim - 1)
    ok = lane < NZ - by if by > 0 else lane >= -by
    return jnp.where(ok, r, 0.0)


def _stage(u_at, ex, y, ct):
    out = {}
    for k in range(3):
        for pz in (0, 1):
            u0, u1 = u_at(k, pz, ex, y, ct), u_at(k, pz, ex + 1, y, ct)
            out[k, 0, pz] = u0 + u1
            out[k, 1, pz] = u1 - u0
    return out


KEYS = [(k, px, pz) for k in range(3) for px in (0, 1) for pz in (0, 1)]


def _modes(s0, s1):
    out = {}
    for k, px, pz in KEYS:
        if (px, pz) != (0, 0):
            out[k, (px, 0, pz)] = s0[k, px, pz] + s1[k, px, pz]
        out[k, (px, 1, pz)] = s1[k, px, pz] - s0[k, px, pz]
    return out


SCALES = sorted({np.float32(c) for c in (N_OFF, N_DIA, P_OFF, P_DIA, S_ALL, T_ALL, B_OFF, B_DIA)})


def _stress(u, e_at):
    def e(c):
        return e_at(SCALES.index(np.float32(c)))

    g = {}
    for group, off, dia in ((NORMAL, N_OFF, N_DIA), (BEND, B_OFF, B_DIA)):
        total = (u[group[0]] + u[group[1]] + u[group[2]]) * e(off)
        for m in group:
            g[m] = u[m] * e(dia) + total
    for a, b in PAIRS:
        total = (u[a] + u[b]) * e(P_OFF)
        g[a] = u[a] * e(P_DIA) + total
        g[b] = u[b] * e(P_DIA) + total
    for a, b in SHEAR:
        g[a] = g[b] = (u[a] + u[b]) * e(S_ALL)
    for m in TWIST:
        g[m] = u[m] * e(T_ALL)
    return g


def _density_of_energy(u):
    def sq(x):
        return x * x

    e = N_OFF * sq(u[NORMAL[0]] + u[NORMAL[1]] + u[NORMAL[2]])
    e = e + N_DIA * (sq(u[NORMAL[0]]) + sq(u[NORMAL[1]]) + sq(u[NORMAL[2]]))
    e = e + B_OFF * sq(u[BEND[0]] + u[BEND[1]] + u[BEND[2]])
    e = e + B_DIA * (sq(u[BEND[0]]) + sq(u[BEND[1]]) + sq(u[BEND[2]]))
    off = dia = she = twi = 0.0
    for a, b in PAIRS:
        off = off + sq(u[a] + u[b])
        dia = dia + sq(u[a]) + sq(u[b])
    for a, b in SHEAR:
        she = she + sq(u[a] + u[b])
    for m in TWIST:
        twi = twi + sq(u[m])
    return e + P_OFF * off + P_DIA * dia + S_ALL * she + T_ALL * twi


def _apply(u_at, e_at, add, layers, y_low, columns, close, unroll=2):
    def tile(ct, _):
        for ex in layers:
            first = _stage(u_at, ex, y_low, ct)
            zero = jnp.zeros((8, NZ), jnp.float32)

            def emit(y, h, ex=ex):
                for k in range(3):
                    for pz in (0, 1):
                        p0, p1 = h[k, 0, pz], h[k, 1, pz]
                        add(k, pz, ex, ex, y, ct, p0, p1)
                        add(k, pz, ex, ex + 1, y, ct, p0, p1)

            def step(t, state, ex=ex):
                s0 = dict(zip(KEYS, state[0]))
                carry = dict(zip(KEYS, state[1]))
                y = y_low + t
                s1 = _stage(u_at, ex, y + 1, ct)
                g = _stress(_modes(s0, s1), functools.partial(e_at, ex, y))
                h, later = {}, {}
                for key in KEYS:
                    k, px, pz = key
                    g1 = g[k, (px, 1, pz)]
                    g0 = g.get((k, (px, 0, pz)))
                    if g0 is None:
                        h[key] = carry[key] - g1
                        later[key] = g1
                    else:
                        h[key] = carry[key] + (g0 - g1)
                        later[key] = g0 + g1
                emit(y, h)
                return tuple(s1[key] for key in KEYS), tuple(later[key] for key in KEYS)

            state = (tuple(first[key] for key in KEYS), (zero,) * len(KEYS))
            if columns == 1:
                state = step(0, state)
            else:
                state = lax.fori_loop(0, columns, step, state, unroll=unroll)
            if close:
                emit(y_low + columns, dict(zip(KEYS, state[1])))
        return 0

    lax.fori_loop(0, CT, tile, 0)


def _sum_diff(u):
    up = _shift(u, 1)
    return u + up, up - u


def _gather_z(s, d):
    return (s - d) + _shift(s + d, -1)


def _loop2(xs, ys, body, state=0, unroll=1):
    def outer(x, state):
        return lax.fori_loop(ys[0], ys[1], lambda y, st: body(x, y, st), state, unroll=unroll)

    return lax.fori_loop(xs[0], xs[1], outer, state)


def _split(x):
    scaled = x * 65537.0
    high = scaled - (scaled - x)
    return high.astype(jnp.bfloat16), (x - high).astype(jnp.bfloat16)


def _rows(x):
    return x.reshape(CASES, NZ)


def _nt(a, b):
    return lax.dot_general(a, b, (((1,), (1,)), ((), ())), preferred_element_type=jnp.float32)


def _system(table):
    lane = lax.broadcasted_iota(jnp.int32, (CASES, NZ), 1)

    def left(x, by):
        return pltpu.roll(x, (-by) % NZ, axis=1)

    def join(a, b):
        return jnp.where(lane < 24, a, jnp.where(lane < 48, b, 0.0))

    blocks = [
        join(table, left(table, 24)),
        join(left(table, 48), jnp.zeros_like(table)),
        join(left(table, 24), left(table, 48)),
    ]
    return [b[8 * i : 8 * i + 8] for b in blocks for i in range(3)]


def _eliminate(tiles, scales, steps):
    lane = lax.broadcasted_iota(jnp.int32, (1, NZ), 1)
    for j in steps:
        row = tiles[j // 8][j % 8 : j % 8 + 1]
        scale = 1.0 / row[:, j : j + 1]
        factor = jnp.where(lane == j, 0.0, row * scale)
        scales = jnp.where(lane == j, scale, scales)
        for t in range((j + 1) // 8, 9):
            tiles[t] = tiles[t] - tiles[t][:, j : j + 1] * factor
    return tiles, scales


WEIGHT = {}
for _dx in range(-2, 3):
    for _dy in range(-2, 3):
        for _dz in range(3):
            _w = 2.5 - math.sqrt(_dx * _dx + _dy * _dy + _dz * _dz)
            if _w > 0.0:
                WEIGHT[_dx, _dy, _dz] = _w


def _cone(planes):
    result = []
    for xo in range(BX):
        total = jnp.zeros((BY, NZ), jnp.float32)
        for (dx, dy, dz), w in WEIGHT.items():
            total = total + w * planes(xo + 2 + dx, dy, dz)
        result.append(total)
    return result


SET_A = [(dx, dy, _span(dx, -1, 2, BX), _span(dy, -1, 8, BY)) for dx, dy in NEIGHBOURS]
SET_B = [
    (-1, 0, (1, 3, 1), (0, 0, BY)),
    (0, -1, (0, 0, BX), (1, 9, 1)),
    (-1, 1, (1, 3, 1), (7, -1, 1)),
    (-1, -1, (1, 3, 1), (0, 8, 2)),
    (-1, -1, (0, 2, 1), (1, 9, 1)),
    (1, -1, (1, -1, 1), (1, 9, 1)),
]


def _kernel(nx, ny, phases, forces, levels, supports, out, nat, lev, sup, stiff, stiffz, inv, free, field, dire, masked,
            image, qf, qm, wf, split, disp, energy, vals, zsum, gram_send, gram_recv, local_sem, l_send, l_recv, s_send,
            s_recv, f_send, f_recv, v_send, v_recv, g_send, g_recv):
    i, j = lax.axis_index("gx"), lax.axis_index("gy")

    def there(dx, dy):
        return lax.rem(i + dx + nx, nx), lax.rem(j + dy + ny, ny)

    peers = [there(dx, dy) for dx, dy in NEIGHBOURS]
    for phase in phases:
        for ox, oy in phase:
            peers.append((i ^ ox, j ^ oy))

    c_nat = pltpu.make_async_copy(forces, nat, local_sem.at[0])
    c_lev = pltpu.make_async_copy(levels, lev.at[2 : 2 + BX, 2 : 2 + BY], local_sem.at[1])
    c_sup = pltpu.make_async_copy(supports, sup.at[1 : 1 + BX, 1 : 1 + BY], local_sem.at[2])
    c_nat.start()
    c_lev.start()
    c_sup.start()

    barrier = pltpu.get_barrier_semaphore()
    for peer in peers:
        pl.semaphore_signal(barrier, inc=1, device_id=peer, device_id_type=MESH)

    c_nat.wait()

    def arrange(k, _):
        for x in range(BX):
            for y in range(BY):
                rows = nat[pl.ds(k * (CASES * BX * BY) + x * BY + y, CASES, stride=BX * BY), :]
                field[k, 1 + x, 1 + y] = rows.reshape(CT, 8, NZ)
        return 0

    lax.fori_loop(0, 3, arrange, 0)
    c_lev.wait()
    c_sup.wait()

    pl.semaphore_wait(barrier, len(peers))

    small, set_a, set_b = [], [], []
    for n, (dx, dy) in enumerate(NEIGHBOURS):
        (a, b, c), (d, e, f) = _span(dx, -2, 3, BX), _span(dy, -2, 9, BY)
        small.append(pltpu.make_async_remote_copy(
            levels.at[a : a + c, d : d + f], lev.at[b + 2 : b + 2 + c, e + 2 : e + 2 + f],
            l_send.at[n], l_recv.at[n], device_id=there(dx, dy), device_id_type=MESH))
        (a, b, c), (d, e, f) = _span(dx, -1, 3, BX), _span(dy, -1, 9, BY)
        small.append(pltpu.make_async_remote_copy(
            supports.at[a : a + c, d : d + f], sup.at[b + 1 : b + 1 + c, e + 1 : e + 1 + f],
            s_send.at[n], s_recv.at[n], device_id=there(dx, dy), device_id_type=MESH))
    for n, (dx, dy, (a, b, c), (d, e, f)) in enumerate(SET_A + SET_B):
        (set_a if n < len(SET_A) else set_b).append(pltpu.make_async_remote_copy(
            field.at[:, a + 1 : a + 1 + c, d + 1 : d + 1 + f], field.at[:, b + 1 : b + 1 + c, e + 1 : e + 1 + f],
            f_send.at[n], f_recv.at[n], device_id=there(dx, dy), device_id_type=MESH))
    for copy in small + set_a + set_b:
        copy.start()
    for copy in small:
        copy.wait_recv()

    def inside(x, y):
        gx, gy = i * BX + x, j * BY + y
        ok = (gx >= 0) & (gx < nx * BX) & (gy >= 0) & (gy < ny * BY)
        return jnp.where(ok, 1.0, 0.0).astype(jnp.float32)

    def moduli(x, y, _):
        level = jnp.broadcast_to(lev[x, y], (8, NZ)).astype(jnp.float32)
        rho = 0.3 + 0.7 * level / (LEVELS - 1)
        e = rho * rho * rho * inside(x - 2, y - 2)
        for n, c in enumerate(SCALES):
            stiff[x, y, n] = e * float(c)
        stiffz[x, y] = (e + _shift(e, -1)) * DIAG
        return 0

    _loop2((0, BX + 4), (0, BY + 4), moduli, unroll=4)

    def nodal(x, y, _):
        fr = (1 - jnp.broadcast_to(sup[x, y], (8, NZ))).astype(jnp.float32) * inside(x - 1, y - 1)
        total = (stiffz[x, y] + stiffz[x + 1, y]) + (stiffz[x, y + 1] + stiffz[x + 1, y + 1])
        free[x, y] = fr
        inv[x, y] = 1.0 / (fr * total + (1.0 - fr))
        return 0

    _loop2((0, BX + 3), (0, BY + 3), nodal, unroll=3)

    def search(x, y, _):
        fr, iv = free[x, y], inv[x, y]
        for k in range(3):
            d = iv * (LOAD * fr * field[k, x, y])
            dire[k, x, y] = d
            s, t = _sum_diff(fr * d)
            masked[k, 0, x, y] = s
            masked[k, 1, x, y] = t
        return 0

    _loop2((1, 1 + BX), (1, 1 + BY), search, unroll=2)
    for copy in set_a:
        copy.wait_recv()
    _loop2((0, 1), (0, BY + 2), search, unroll=2)
    _loop2((BX + 1, BX + 2), (0, BY + 2), search, unroll=2)
    for y in (0, BY + 1):
        _loop2((1, 1 + BX), (y, y + 1), search)

    def u_at(k, pz, x, y, ct):
        return masked[k, pz, x + 1, y + 1, ct]

    def e_at(x, y, n):
        return stiff[x + 2, y + 2, n]

    def adder(ref, fresh, shift, planes):
        def add(k, pz, ex, x, y, ct, p0, p1):
            if x not in planes:
                return
            value = p0 - p1 if x == ex else p0 + p1
            if fresh(ex, x):
                ref[k, pz, x, y + shift, ct] = value
            else:
                ref[k, pz, x, y + shift, ct] += value
        return add

    at_nodes = range(BX + 1)
    _apply(u_at, e_at, adder(image, lambda ex, x: x == ex + 1, 1, at_nodes), range(-1, BX), -1, BY + 1, True, unroll=3)

    gap = jnp.zeros((16, NZ), jnp.bfloat16)
    gap8 = jnp.zeros((8, NZ), jnp.float32)
    gap32 = jnp.zeros((32, NZ), jnp.bfloat16)

    def above(x, y):
        fr, iv = free[x + 1, y + 1], inv[x + 1, y + 1]
        rows, images = [], []
        for k in range(3):
            d = dire[k, x + 1, y + 1]
            im = fr * _gather_z(image[k, 0, x, y + 1], image[k, 1, x, y + 1]) + (1.0 - fr) * d
            q = iv * im
            qf[k, x, y] = q
            s, t = _sum_diff(fr * q)
            qm[k, 0, x, y] = s
            qm[k, 1, x, y] = t
            high, low = _split(jnp.concatenate([_rows(d), _rows(q)], 0))
            hl = jnp.concatenate([high, low], 0)
            split[k, x, y] = hl
            rows.append(hl)
            images.append(im)
        return rows, images, fr

    def first_gram(x, y, acc):
        rows, images, fr = above(x, y)
        right = []
        for k in range(3):
            r0 = LOAD * fr * field[k, x + 1, y + 1]
            high, low = _split(jnp.concatenate([_rows(images[k]), _rows(r0)], 0))
            right.append(jnp.concatenate([high, gap, low, gap], 0))
        return acc + _nt(jnp.concatenate(rows, 1), jnp.concatenate(right, 1))

    acc = _loop2((0, BX), (0, BY), first_gram, jnp.zeros((96, NZ), jnp.float32))
    lane = lax.broadcasted_iota(jnp.int32, (CASES, NZ), 1)
    both = acc[:48] + acc[48:]
    both = both + pltpu.roll(both, 64, axis=1)
    table = jnp.where(lane < 48, both[:24], jnp.where(lane < 96, pltpu.roll(both[24:], 48, axis=1), 0.0))

    per_round = sum(len(p) for p in phases)

    def begin(turn, n, value):
        slot = turn * per_round + sum(len(p) for p in phases[:n])
        gram_send[turn * len(phases) + n] = value
        group = [pltpu.make_async_remote_copy(
            gram_send.at[turn * len(phases) + n], gram_recv.at[slot + m], g_send.at[slot + m], g_recv.at[slot + m],
            device_id=(i ^ ox, j ^ oy), device_id_type=MESH) for m, (ox, oy) in enumerate(phases[n])]
        for copy in group:
            copy.start()
        sent.extend(group)
        return value, slot, group

    def finish(going):
        value, slot, group = going
        for copy in group:
            copy.wait_recv()
        terms = [value] + [gram_recv[slot + m] for m in range(len(group))]
        while len(terms) > 1:
            terms = [terms[t] + terms[t + 1] for t in range(0, len(terms), 2)]
        return terms[0]

    sent = []
    todo = list(range(len(phases)))
    going = begin(0, todo.pop(0), table)

    for copy in set_b:
        copy.wait_recv()
    _loop2((BX + 2, BX + 3), (0, BY + 3), search, unroll=2)
    _loop2((0, BX + 2), (BY + 2, BY + 3), search, unroll=2)
    _apply(u_at, e_at, adder(image, lambda ex, x: False, 1, at_nodes), range(-1, BX), BY, 1, False)
    if todo:
        going = begin(0, todo.pop(0), finish(going))
    _apply(u_at, e_at, adder(image, lambda ex, x: False, 1, at_nodes), range(BX, BX + 1), -1, BY + 2, False, unroll=2)

    def edge(x, y, _):
        above(x, y)
        return 0

    _loop2((BX, BX + 1), (0, BY + 1), edge, unroll=3)
    _loop2((0, BX), (BY, BY + 1), edge)
    if todo:
        going = begin(0, todo.pop(0), finish(going))

    def q_at(k, pz, x, y, ct):
        return qm[k, pz, x, y, ct]

    _apply(q_at, e_at, adder(wf, lambda ex, x: x == ex + 1 or ex == 0, 0, at_nodes), range(BX), 0, BY, True, unroll=2)
    if todo:
        going = begin(0, todo.pop(0), finish(going))

    def second_gram(x, y, acc):
        fr = free[x + 1, y + 1]
        mine = jnp.where((x < BX) & (y < BY), 1.0, 0.0).astype(jnp.float32)
        right = []
        for k in range(3):
            w = fr * _gather_z(wf[k, 0, x, y], wf[k, 1, x, y]) + (mine * (1.0 - fr)) * qf[k, x, y]
            high, low = _split(jnp.concatenate([_rows(w), gap8], 0))
            right.append(jnp.concatenate([high, gap32, low, gap32], 0))
        left = jnp.concatenate([split[k, x, y] for k in range(3)], 1)
        return acc + _nt(left, jnp.concatenate(right, 1))

    acc2 = _loop2((0, BX + 1), (0, BY + 1), second_gram, jnp.zeros((96, NZ), jnp.float32), unroll=3)
    last = acc2[24:48] + acc2[72:]
    last = last + pltpu.roll(last, 64, axis=1)
    n_going = begin(1, 0, last)
    table = finish(going)
    todo = list(range(1, len(phases)))
    if todo:
        n_going = begin(1, todo.pop(0), finish(n_going))
    tiles, scales = _eliminate(_system(table), jnp.zeros((1, NZ), jnp.float32), range(24))
    if todo:
        n_going = begin(1, todo.pop(0), finish(n_going))

    grid_y = j * BY - BY + lax.broadcasted_iota(jnp.int32, (3 * BY, NZ), 0)
    ok_y = (grid_y >= 0) & (grid_y < ny * BY)

    def present(p):
        gx = i * BX + p - 2
        return jnp.where(ok_y & (gx >= 0) & (gx < nx * BX), 1.0, 0.0).astype(jnp.float32)

    def spread(p, v):
        zsum[p, 0] = v
        zsum[p, 1] = _shift(v, 1) + _shift(v, -1)
        zsum[p, 2] = _shift(v, 2) + _shift(v, -2)

    def near(p, dy, dz):
        return zsum[p, dz, BY + dy : 2 * BY + dy]

    for p in range(BX + 4):
        spread(p, present(p))
    weights = _cone(near)
    rho = [0.3 + 0.7 * lev[2 + x, 2 : 2 + BY, 0, :].astype(jnp.float32) / (LEVELS - 1) for x in range(BX)]

    if todo:
        n_going = begin(1, todo.pop(0), finish(n_going))
    last = finish(n_going)
    last = jnp.where(lane < 24, last, 0.0)
    last = pltpu.roll(last, 24, axis=1)
    for t in range(3):
        tiles[3 + t] = tiles[3 + t] + last[8 * t : 8 * t + 8]
    tiles, scales = _eliminate(tiles, scales, range(24, 48))
    half = jnp.concatenate(tiles[6:], 0) * scales
    mix = half + pltpu.roll(half, 48, axis=1)
    mix = jnp.concatenate([mix, gap8], 0)
    high, low = _split(mix)
    coefs = jnp.concatenate([high, low], 0)[:, :96]

    def combine(x, y, _):
        fr = free[x + 1, y + 1]
        for k in range(3):
            u = jnp.dot(coefs, split[k, x, y], preferred_element_type=jnp.float32)
            u = u[:24] + u[32:56]
            s, t = _sum_diff(fr * u.reshape(CT, 8, NZ))
            disp[k, 0, x, y] = s
            disp[k, 1, x, y] = t
        return 0

    _loop2((0, BX + 1), (0, BY + 1), combine, unroll=3)

    def s_at(k, pz, x, y, ct):
        return disp[k, pz, x, y, ct]

    for x in range(BX):
        energy[x] = jnp.zeros((BY, 8, NZ), jnp.float32)

    def energies(ct, _):
        for x in range(BX):
            first = _stage(s_at, x, 0, ct)

            def step(y, state, x=x):
                s1 = _stage(s_at, x, y + 1, ct)
                energy[x, y] += _density_of_energy(_modes(dict(zip(KEYS, state)), s1))
                return tuple(s1[key] for key in KEYS)

            lax.fori_loop(0, BY, step, tuple(first[key] for key in KEYS), unroll=2)
        return 0

    lax.fori_loop(0, CT, energies, 0)

    for x in range(BX):
        sens = -3.0 * rho[x] * rho[x] * jnp.sum(energy[x], axis=1) / CASES
        vals[2 + x, BY : 2 * BY] = rho[x] * sens
    group = []
    for n, (dx, dy) in enumerate(NEIGHBOURS):
        at_x, at_y = 2 - BX * dx, BY - BY * dy
        group.append(pltpu.make_async_remote_copy(
            vals.at[2 : 2 + BX, BY : 2 * BY], vals.at[at_x : at_x + BX, at_y : at_y + BY], v_send.at[n], v_recv.at[n],
            device_id=there(dx, dy), device_id_type=MESH))
    for copy in group:
        copy.start()
    for copy in small + set_a + set_b + sent:
        copy.wait_send()
    for copy in group:
        copy.wait_recv()
    for p in range(BX + 4):
        spread(p, jnp.where(present(p) > 0.0, vals[p], 0.0))
    sums = _cone(near)
    for x in range(BX):
        out[x] = sums[x] / (rho[x] * weights[x])
    for copy in group:
        copy.wait_send()


def _phases(nx, ny):
    groups = [[(1, 0)], [(2, 0), (0, 1), (2, 1)]]
    groups.append([(4 * o, 0) for o in range(1, nx // 4)])
    groups.append([(0, 2 * o) for o in range(1, ny // 2)])
    return [g for g in groups if g]


def solution(mesh):
    nx, ny = mesh.shape["gx"], mesh.shape["gy"]
    phases = _phases(nx, ny)
    slots = sum(len(g) for g in phases)
    f32 = jnp.float32
    dma = pltpu.SemaphoreType.DMA
    any_space = pl.BlockSpec(memory_space=pl.ANY)

    def local(forces, levels, supports):
        return pl.pallas_call(
            functools.partial(_kernel, nx, ny, phases),
            out_shape=jax.ShapeDtypeStruct((BX, BY, NZ), f32),
            in_specs=[any_space] * 3,
            out_specs=pl.BlockSpec(memory_space=pltpu.VMEM),
            scratch_shapes=[
                pltpu.VMEM((3 * CASES * BX * BY, NZ), f32),
                pltpu.VMEM((BX + 4, BY + 4, 1, NZ), jnp.int32),
                pltpu.VMEM((BX + 3, BY + 3, 1, NZ), jnp.int32),
                pltpu.VMEM((BX + 4, BY + 4, len(SCALES), 8, NZ), f32),
                pltpu.VMEM((BX + 4, BY + 4, 8, NZ), f32),
                pltpu.VMEM((BX + 3, BY + 3, 8, NZ), f32),
                pltpu.VMEM((BX + 3, BY + 3, 8, NZ), f32),
                pltpu.VMEM((3, BX + 3, BY + 3, CT, 8, NZ), f32),
                pltpu.VMEM((3, BX + 3, BY + 3, CT, 8, NZ), f32),
                pltpu.VMEM((3, 2, BX + 3, BY + 3, CT, 8, NZ), f32),
                pltpu.VMEM((3, 2, BX + 1, BY + 2, CT, 8, NZ), f32),
                pltpu.VMEM((3, BX + 1, BY + 1, CT, 8, NZ), f32),
                pltpu.VMEM((3, 2, BX + 1, BY + 1, CT, 8, NZ), f32),
                pltpu.VMEM((3, 2, BX + 1, BY + 1, CT, 8, NZ), f32),
                pltpu.VMEM((3, BX + 1, BY + 1, 96, NZ), jnp.bfloat16),
                pltpu.VMEM((3, 2, BX + 1, BY + 1, CT, 8, NZ), f32),
                pltpu.VMEM((BX, BY, 8, NZ), f32),
                pltpu.VMEM((BX + 4, 3 * BY, NZ), f32),
                pltpu.VMEM((BX + 4, 3, 3 * BY, NZ), f32),
                pltpu.VMEM((2 * len(phases), CASES, NZ), f32),
                pltpu.VMEM((2 * slots, CASES, NZ), f32),
                dma((3,)),
                dma((8,)), dma((8,)), dma((8,)), dma((8,)), dma((14,)), dma((14,)), dma((8,)), dma((8,)),
                dma((2 * slots,)), dma((2 * slots,)),
            ],
            compiler_params=pltpu.CompilerParams(collective_id=0, has_side_effects=True),
        )(
            forces.reshape(3 * CASES * BX * BY, NZ),
            levels.reshape(BX, BY, 1, NZ),
            supports.reshape(BX, BY, 1, NZ),
        )

    return jax.shard_map(
        local,
        mesh=mesh,
        in_specs=(P(None, None, "gx", "gy", None), P("gx", "gy", None), P("gx", "gy", None)),
        out_specs=P("gx", "gy", None),
        check_vma=False,
    )
```

```python
import functools
import math

import jax
import jax.numpy as jnp
import numpy as np
from jax import lax
from jax.experimental import pallas as pl
from jax.experimental.pallas import tpu as pltpu
from jax.sharding import PartitionSpec as P

MESH = pl.DeviceIdType.MESH
CASES = 24
LEVELS = 16
LOAD = 0.2
BX, BY, NZ = 2, 8, 128
CT = 3


def element_matrix():
    poisson = 0.3
    lame_first = poisson / ((1.0 + poisson) * (1.0 - 2.0 * poisson))
    lame_shear = 1.0 / (2.0 * (1.0 + poisson))
    elastic = np.zeros((6, 6))
    elastic[:3, :3] = lame_first
    for position in range(3):
        elastic[position, position] += 2.0 * lame_shear
        elastic[position + 3, position + 3] = lame_shear
    points = [0.5 - 0.5 / math.sqrt(3.0), 0.5 + 0.5 / math.sqrt(3.0)]
    matrix = np.zeros((24, 24))
    for point_x in points:
        for point_y in points:
            for point_z in points:
                coords = (point_x, point_y, point_z)
                strain = np.zeros((6, 24))
                for corner in range(8):
                    bits = (corner >> 2 & 1, corner >> 1 & 1, corner & 1)
                    shape = [coords[n] if bits[n] else 1.0 - coords[n] for n in range(3)]
                    slopes = [1.0 if bits[n] else -1.0 for n in range(3)]
                    slope_x = slopes[0] * shape[1] * shape[2]
                    slope_y = shape[0] * slopes[1] * shape[2]
                    slope_z = shape[0] * shape[1] * slopes[2]
                    o = 3 * corner
                    strain[0, o] = slope_x
                    strain[1, o + 1] = slope_y
                    strain[2, o + 2] = slope_z
                    strain[3, o] = slope_y
                    strain[3, o + 1] = slope_x
                    strain[4, o + 1] = slope_z
                    strain[4, o + 2] = slope_y
                    strain[5, o] = slope_z
                    strain[5, o + 2] = slope_x
                matrix = matrix + strain.T @ elastic @ strain / 8.0
    return matrix


KE = element_matrix()
DIAG = float(KE[0, 0])


def parity_matrix():
    walsh = np.ones((8, 8))
    for mode in range(8):
        for corner in range(8):
            for n in range(3):
                if mode >> n & 1:
                    walsh[mode, corner] *= 2 * (corner >> n & 1) - 1
    big = np.kron(walsh, np.eye(3))
    return big @ KE @ big.T / 64.0


KP = parity_matrix()
UNIT = ((1, 0, 0), (0, 1, 0), (0, 0, 1))


def _flip(p, k):
    return tuple(a ^ b for a, b in zip(p, UNIT[k]))


def _kp(m, n):
    at = [3 * (4 * p[0] + 2 * p[1] + p[2]) + k for k, p in (m, n)]
    return float(KP[at[0], at[1]])


NORMAL = [(k, UNIT[k]) for k in range(3)]
BEND = [(k, _flip((1, 1, 1), k)) for k in range(3)]
PAIRS = [[(k, _flip(UNIT[s], k)) for k in range(3) if k != s] for s in range(3)]
SHEAR = []
TWIST = []
for _s in range(3):
    _a, _b = [k for k in range(3) if k != _s]
    SHEAR.append([(_a, UNIT[_b]), (_b, UNIT[_a])])
    TWIST.append((_s, (1, 1, 1)))
N_OFF = _kp(NORMAL[0], NORMAL[1])
N_DIA = _kp(NORMAL[0], NORMAL[0]) - N_OFF
P_OFF = _kp(PAIRS[0][0], PAIRS[0][1])
P_DIA = _kp(PAIRS[0][0], PAIRS[0][0]) - P_OFF
S_ALL = _kp(SHEAR[0][0], SHEAR[0][0])
T_ALL = _kp(TWIST[0], TWIST[0])
B_OFF = _kp(BEND[0], BEND[1])
B_DIA = _kp(BEND[0], BEND[0]) - B_OFF


def _span(d, low, high, size):
    a = max(0, low + d * size)
    b = min(size, high + 1 + d * size)
    return a, a - d * size, b - a


NEIGHBOURS = [(dx, dy) for dx in (-1, 0, 1) for dy in (-1, 0, 1) if dx or dy]


def _shift(x, by):
    lane = lax.broadcasted_iota(jnp.int32, x.shape, x.ndim - 1)
    r = pltpu.roll(x, (-by) % NZ, axis=x.ndim - 1)
    ok = lane < NZ - by if by > 0 else lane >= -by
    return jnp.where(ok, r, 0.0)


def _stage(u_at, ex, y, ct):
    out = {}
    for k in range(3):
        for pz in (0, 1):
            u0, u1 = u_at(k, pz, ex, y, ct), u_at(k, pz, ex + 1, y, ct)
            out[k, 0, pz] = u0 + u1
            out[k, 1, pz] = u1 - u0
    return out


KEYS = [(k, px, pz) for k in range(3) for px in (0, 1) for pz in (0, 1)]


def _modes(s0, s1):
    out = {}
    for k, px, pz in KEYS:
        if (px, pz) != (0, 0):
            out[k, (px, 0, pz)] = s0[k, px, pz] + s1[k, px, pz]
        out[k, (px, 1, pz)] = s1[k, px, pz] - s0[k, px, pz]
    return out


SCALES = sorted({np.float32(c) for c in (N_OFF, N_DIA, P_OFF, P_DIA, S_ALL, T_ALL, B_OFF, B_DIA)})


def _stress(u, e_at):
    def e(c):
        return e_at(SCALES.index(np.float32(c)))

    g = {}
    for group, off, dia in ((NORMAL, N_OFF, N_DIA), (BEND, B_OFF, B_DIA)):
        total = (u[group[0]] + u[group[1]] + u[group[2]]) * e(off)
        for m in group:
            g[m] = u[m] * e(dia) + total
    for a, b in PAIRS:
        total = (u[a] + u[b]) * e(P_OFF)
        g[a] = u[a] * e(P_DIA) + total
        g[b] = u[b] * e(P_DIA) + total
    for a, b in SHEAR:
        g[a] = g[b] = (u[a] + u[b]) * e(S_ALL)
    for m in TWIST:
        g[m] = u[m] * e(T_ALL)
    return g


def _density_of_energy(u):
    def sq(x):
        return x * x

    e = N_OFF * sq(u[NORMAL[0]] + u[NORMAL[1]] + u[NORMAL[2]])
    e = e + N_DIA * (sq(u[NORMAL[0]]) + sq(u[NORMAL[1]]) + sq(u[NORMAL[2]]))
    e = e + B_OFF * sq(u[BEND[0]] + u[BEND[1]] + u[BEND[2]])
    e = e + B_DIA * (sq(u[BEND[0]]) + sq(u[BEND[1]]) + sq(u[BEND[2]]))
    off = dia = she = twi = 0.0
    for a, b in PAIRS:
        off = off + sq(u[a] + u[b])
        dia = dia + sq(u[a]) + sq(u[b])
    for a, b in SHEAR:
        she = she + sq(u[a] + u[b])
    for m in TWIST:
        twi = twi + sq(u[m])
    return e + P_OFF * off + P_DIA * dia + S_ALL * she + T_ALL * twi


def _apply(u_at, e_at, add, layers, y_low, columns, close, unroll=2):
    def tile(ct, _):
        for ex in layers:
            first = _stage(u_at, ex, y_low, ct)
            zero = jnp.zeros((8, NZ), jnp.float32)

            def emit(y, h, ex=ex):
                for k in range(3):
                    for pz in (0, 1):
                        p0, p1 = h[k, 0, pz], h[k, 1, pz]
                        add(k, pz, ex, ex, y, ct, p0, p1)
                        add(k, pz, ex, ex + 1, y, ct, p0, p1)

            def step(t, state, ex=ex):
                s0 = dict(zip(KEYS, state[0]))
                carry = dict(zip(KEYS, state[1]))
                y = y_low + t
                s1 = _stage(u_at, ex, y + 1, ct)
                g = _stress(_modes(s0, s1), functools.partial(e_at, ex, y))
                h, later = {}, {}
                for key in KEYS:
                    k, px, pz = key
                    g1 = g[k, (px, 1, pz)]
                    g0 = g.get((k, (px, 0, pz)))
                    if g0 is None:
                        h[key] = carry[key] - g1
                        later[key] = g1
                    else:
                        h[key] = carry[key] + (g0 - g1)
                        later[key] = g0 + g1
                emit(y, h)
                return tuple(s1[key] for key in KEYS), tuple(later[key] for key in KEYS)

            state = (tuple(first[key] for key in KEYS), (zero,) * len(KEYS))
            if columns == 1:
                state = step(0, state)
            else:
                state = lax.fori_loop(0, columns, step, state, unroll=unroll)
            if close:
                emit(y_low + columns, dict(zip(KEYS, state[1])))
        return 0

    lax.fori_loop(0, CT, tile, 0)


def _sum_diff(u):
    up = _shift(u, 1)
    return u + up, up - u


def _gather_z(s, d):
    return (s - d) + _shift(s + d, -1)


def _loop2(xs, ys, body, state=0, unroll=1):
    def outer(x, state):
        return lax.fori_loop(ys[0], ys[1], lambda y, st: body(x, y, st), state, unroll=unroll)

    return lax.fori_loop(xs[0], xs[1], outer, state)


def _split(x):
    scaled = x * 65537.0
    high = scaled - (scaled - x)
    return high.astype(jnp.bfloat16), (x - high).astype(jnp.bfloat16)


def _rows(x):
    return x.reshape(CASES, NZ)


def _nt(a, b):
    return lax.dot_general(a, b, (((1,), (1,)), ((), ())), preferred_element_type=jnp.float32)


def _system(table):
    lane = lax.broadcasted_iota(jnp.int32, (CASES, NZ), 1)

    def left(x, by):
        return pltpu.roll(x, (-by) % NZ, axis=1)

    def join(a, b):
        return jnp.where(lane < 24, a, jnp.where(lane < 48, b, 0.0))

    blocks = [
        join(table, left(table, 24)),
        join(left(table, 48), jnp.zeros_like(table)),
        join(left(table, 24), left(table, 48)),
    ]
    return [b[8 * i : 8 * i + 8] for b in blocks for i in range(3)]


def _eliminate(tiles, scales, steps):
    lane = lax.broadcasted_iota(jnp.int32, (1, NZ), 1)
    for j in steps:
        row = tiles[j // 8][j % 8 : j % 8 + 1]
        scale = 1.0 / row[:, j : j + 1]
        factor = jnp.where(lane == j, 0.0, row * scale)
        scales = jnp.where(lane == j, scale, scales)
        for t in range((j + 1) // 8, 9):
            tiles[t] = tiles[t] - tiles[t][:, j : j + 1] * factor
    return tiles, scales


def _weight(dx, dy, dz):
    return max(0.0, 2.5 - math.sqrt(dx * dx + dy * dy + dz * dz))


def _cone(planes):
    by_row = {}
    for p in range(BX + 4):
        by_row[p, 0] = planes[p, BY : 2 * BY]
        for dy in (1, 2):
            by_row[p, dy] = planes[p, BY + dy : 2 * BY + dy] + planes[p, BY - dy : 2 * BY - dy]
    result = []
    for xo in range(BX):
        total = None
        for dz in range(3):
            part = jnp.zeros((BY, NZ), jnp.float32)
            for dx in range(-2, 3):
                for dy in range(3):
                    w = _weight(dx, dy, dz)
                    if w > 0.0:
                        part = part + w * by_row[xo + 2 + dx, dy]
            total = part if dz == 0 else total + (_shift(part, dz) + _shift(part, -dz))
        result.append(total)
    return result


SET_A = [(dx, dy, _span(dx, -1, 2, BX), _span(dy, -1, 8, BY)) for dx, dy in NEIGHBOURS]
SET_B = [
    (-1, 0, (1, 3, 1), (0, 0, BY)),
    (0, -1, (0, 0, BX), (1, 9, 1)),
    (-1, 1, (1, 3, 1), (7, -1, 1)),
    (-1, -1, (1, 3, 1), (0, 8, 2)),
    (-1, -1, (0, 2, 1), (1, 9, 1)),
    (1, -1, (1, -1, 1), (1, 9, 1)),
]


def _kernel(nx, ny, phases, phases2, forces, levels, supports, out, nat, lev, sup, stiff, stiffz, inv, free, field, dire, masked,
            image, qf, qm, wf, split, disp, energy, vals, rim, gram_send, gram_recv, last_send, last_recv, local_sem, l_send, l_recv, s_send,
            s_recv, f_send, f_recv, v_send, v_recv, g_send, g_recv, n_send, n_recv):
    i, j = lax.axis_index("gx"), lax.axis_index("gy")

    def there(dx, dy):
        return lax.rem(i + dx + nx, nx), lax.rem(j + dy + ny, ny)

    peers = [there(dx, dy) for dx, dy in NEIGHBOURS]
    for phase in phases:
        for ox, oy in phase:
            peers.append((i ^ ox, j ^ oy))

    c_nat = pltpu.make_async_copy(forces, nat, local_sem.at[0])
    c_lev = pltpu.make_async_copy(levels, lev.at[2 : 2 + BX, 2 : 2 + BY], local_sem.at[1])
    c_sup = pltpu.make_async_copy(supports, sup.at[1 : 1 + BX, 1 : 1 + BY], local_sem.at[2])
    c_nat.start()
    c_lev.start()
    c_sup.start()

    barrier = pltpu.get_barrier_semaphore()
    for peer in peers:
        pl.semaphore_signal(barrier, inc=1, device_id=peer, device_id_type=MESH)

    c_nat.wait()

    def arrange(k, _):
        for x in range(BX):
            for y in range(BY):
                rows = nat[pl.ds(k * (CASES * BX * BY) + x * BY + y, CASES, stride=BX * BY), :]
                field[k, 1 + x, 1 + y] = rows.reshape(CT, 8, NZ)
        return 0

    lax.fori_loop(0, 3, arrange, 0)
    c_lev.wait()
    c_sup.wait()

    pl.semaphore_wait(barrier, len(peers))

    small, set_a, set_b = [], [], []
    for n, (dx, dy) in enumerate(NEIGHBOURS):
        (a, b, c), (d, e, f) = _span(dx, -2, 3, BX), _span(dy, -2, 9, BY)
        small.append(pltpu.make_async_remote_copy(
            levels.at[a : a + c, d : d + f], lev.at[b + 2 : b + 2 + c, e + 2 : e + 2 + f],
            l_send.at[n], l_recv.at[n], device_id=there(dx, dy), device_id_type=MESH))
        (a, b, c), (d, e, f) = _span(dx, -1, 3, BX), _span(dy, -1, 9, BY)
        small.append(pltpu.make_async_remote_copy(
            supports.at[a : a + c, d : d + f], sup.at[b + 1 : b + 1 + c, e + 1 : e + 1 + f],
            s_send.at[n], s_recv.at[n], device_id=there(dx, dy), device_id_type=MESH))
    for n, (dx, dy, (a, b, c), (d, e, f)) in enumerate(SET_A + SET_B):
        (set_a if n < len(SET_A) else set_b).append(pltpu.make_async_remote_copy(
            field.at[:, a + 1 : a + 1 + c, d + 1 : d + 1 + f], field.at[:, b + 1 : b + 1 + c, e + 1 : e + 1 + f],
            f_send.at[n], f_recv.at[n], device_id=there(dx, dy), device_id_type=MESH))
    for copy in small + set_a + set_b:
        copy.start()
    for copy in small:
        copy.wait_recv()

    def inside(x, y):
        gx, gy = i * BX + x, j * BY + y
        ok = (gx >= 0) & (gx < nx * BX) & (gy >= 0) & (gy < ny * BY)
        return jnp.where(ok, 1.0, 0.0).astype(jnp.float32)

    def moduli(x, y, _):
        level = jnp.broadcast_to(lev[x, y], (8, NZ)).astype(jnp.float32)
        rho = 0.3 + 0.7 * level / (LEVELS - 1)
        e = rho * rho * rho * inside(x - 2, y - 2)
        for n, c in enumerate(SCALES):
            stiff[x, y, n] = e * float(c)
        stiffz[x, y] = (e + _shift(e, -1)) * DIAG
        return 0

    _loop2((0, BX + 4), (0, BY + 4), moduli, unroll=4)

    def nodal(x, y, _):
        fr = (1 - jnp.broadcast_to(sup[x, y], (8, NZ))).astype(jnp.float32) * inside(x - 1, y - 1)
        total = (stiffz[x, y] + stiffz[x + 1, y]) + (stiffz[x, y + 1] + stiffz[x + 1, y + 1])
        free[x, y] = fr
        inv[x, y] = 1.0 / (fr * total + (1.0 - fr))
        return 0

    _loop2((0, BX + 3), (0, BY + 3), nodal, unroll=3)

    def search(x, y, _):
        fr, iv = free[x, y], inv[x, y]
        for k in range(3):
            d = iv * (LOAD * fr * field[k, x, y])
            dire[k, x, y] = d
            s, t = _sum_diff(fr * d)
            masked[k, 0, x, y] = s
            masked[k, 1, x, y] = t
        return 0

    _loop2((1, 1 + BX), (1, 1 + BY), search, unroll=2)
    for copy in set_a:
        copy.wait_recv()
    _loop2((0, 1), (0, BY + 2), search, unroll=2)
    _loop2((BX + 1, BX + 2), (0, BY + 2), search, unroll=2)
    for y in (0, BY + 1):
        _loop2((1, 1 + BX), (y, y + 1), search)

    def u_at(k, pz, x, y, ct):
        return masked[k, pz, x + 1, y + 1, ct]

    def e_at(x, y, n):
        return stiff[x + 2, y + 2, n]

    def adder(ref, fresh, shift, planes):
        def add(k, pz, ex, x, y, ct, p0, p1):
            if x not in planes:
                return
            value = p0 - p1 if x == ex else p0 + p1
            if fresh(ex, x):
                ref[k, pz, x, y + shift, ct] = value
            else:
                ref[k, pz, x, y + shift, ct] += value
        return add

    at_nodes = range(BX + 1)
    _apply(u_at, e_at, adder(image, lambda ex, x: x == ex + 1, 1, at_nodes), range(-1, BX), -1, BY + 1, True, unroll=3)

    gap = jnp.zeros((16, NZ), jnp.bfloat16)
    gap8 = jnp.zeros((8, NZ), jnp.float32)
    gap32 = jnp.zeros((32, NZ), jnp.bfloat16)

    def above(x, y):
        fr, iv = free[x + 1, y + 1], inv[x + 1, y + 1]
        nodes = []
        for k in range(3):
            d = dire[k, x + 1, y + 1]
            im = fr * _gather_z(image[k, 0, x, y + 1], image[k, 1, x, y + 1]) + (1.0 - fr) * d
            q = iv * im
            s, t = _sum_diff(fr * q)
            qm[k, 0, x, y] = s
            qm[k, 1, x, y] = t
            nodes.append((d, im, q))
        return nodes, fr

    def first_gram(x, y, acc):
        nodes, fr = above(x, y)
        left, right = [], []
        for k, (d, im, q) in enumerate(nodes):
            qf[k, x, y] = q
            r0 = LOAD * fr * field[k, x + 1, y + 1]
            left.append(jnp.concatenate(_split(jnp.concatenate([_rows(d), _rows(q)], 0)), 0))
            high, low = _split(jnp.concatenate([_rows(im), _rows(r0)], 0))
            right.append(jnp.concatenate([high, gap, low, gap], 0))
        return acc + _nt(jnp.concatenate(left, 1), jnp.concatenate(right, 1))

    acc = _loop2((0, BX), (0, BY), first_gram, jnp.zeros((96, NZ), jnp.float32))
    lane = lax.broadcasted_iota(jnp.int32, (CASES, NZ), 1)
    both = acc[:48] + acc[48:]
    both = both + pltpu.roll(both, 64, axis=1)
    table = jnp.where(lane < 48, both[:24], jnp.where(lane < 96, pltpu.roll(both[24:], 48, axis=1), 0.0))

    sent = []

    def begin(n, value, groups, source, target, send_sem, recv_sem):
        slot = sum(len(p) for p in groups[:n])
        source[n] = value
        group = [pltpu.make_async_remote_copy(
            source.at[n], target.at[slot + m], send_sem.at[slot + m], recv_sem.at[slot + m],
            device_id=(i ^ ox, j ^ oy), device_id_type=MESH) for m, (ox, oy) in enumerate(groups[n])]
        for copy in group:
            copy.start()
        sent.extend(group)
        return value, slot, group, target

    def begin1(n, value):
        return begin(n, value, phases, gram_send, gram_recv, g_send, g_recv)

    def begin2(n, value):
        return begin(n, value, phases2, last_send, last_recv, n_send, n_recv)

    def finish(going):
        value, slot, group, target = going
        for copy in group:
            copy.wait_recv()
        terms = [value] + [target[slot + m] for m in range(len(group))]
        while len(terms) > 1:
            terms = [terms[t] + terms[t + 1] for t in range(0, len(terms), 2)]
        return terms[0]

    todo = list(range(len(phases)))
    going = begin1(todo.pop(0), table)

    def pair(left, right, acc):
        a, b = [], []
        for u, v in zip(left, right):
            a.append(jnp.concatenate(_split(jnp.concatenate([_rows(u), gap8], 0)), 0))
            high, low = _split(jnp.concatenate([_rows(v), gap8], 0))
            b.append(jnp.concatenate([high, gap32, low, gap32], 0))
        return acc + _nt(jnp.concatenate(a, 1), jnp.concatenate(b, 1))

    def clamped(x, y, acc):
        fr = free[x + 1, y + 1]
        q = [qf[k, x, y] for k in range(3)]
        return pair(q, [(1.0 - fr) * v for v in q], acc)

    acc2 = _loop2((0, BX), (0, BY), clamped, jnp.zeros((64, NZ), jnp.float32), unroll=4)

    for copy in set_b:
        copy.wait_recv()
    _loop2((BX + 2, BX + 3), (0, BY + 3), search, unroll=2)
    _loop2((0, BX + 2), (BY + 2, BY + 3), search, unroll=2)
    _apply(u_at, e_at, adder(image, lambda ex, x: False, 1, at_nodes), range(-1, BX), BY, 1, False)
    _apply(u_at, e_at, adder(image, lambda ex, x: False, 1, at_nodes), range(BX, BX + 1), -1, BY + 2, False, unroll=2)

    def edge(x, y, _):
        above(x, y)
        return 0

    _loop2((BX, BX + 1), (0, BY + 1), edge, unroll=3)
    _loop2((0, BX), (BY, BY + 1), edge)
    if todo:
        going = begin1(todo.pop(0), finish(going))

    def q_at(k, pz, x, y, ct):
        return qm[k, pz, x, y, ct]

    _apply(q_at, e_at, adder(wf, lambda ex, x: x == ex + 1 or ex == 0, 0, at_nodes), range(BX), 0, BY, True, unroll=2)

    def second_gram(x, y, acc):
        at = [(k, pz) for k in range(3) for pz in (0, 1)]
        return pair([qm[k, pz, x, y] for k, pz in at], [wf[k, pz, x, y] for k, pz in at], acc)

    acc2 = _loop2((0, BX + 1), (0, BY + 1), second_gram, acc2, unroll=3)
    last = acc2[:24] + acc2[32:56]
    last = last + pltpu.roll(last, 64, axis=1)
    last = jnp.where(lane < 24, last, 0.0)
    last = last[:8] + pltpu.roll(last[8:16], 24, axis=1) + pltpu.roll(last[16:], 48, axis=1)
    n_going = begin2(0, last)
    while todo:
        going = begin1(todo.pop(0), finish(going))
    n_todo = list(range(1, len(phases2)))
    if n_todo:
        n_going = begin2(n_todo.pop(0), finish(n_going))
    table = finish(going)
    tiles, scales = _eliminate(_system(table), jnp.zeros((1, NZ), jnp.float32), range(24))

    def prepare(x, y, _):
        for k in range(3):
            for pz in (0, 1):
                both = jnp.concatenate([_rows(masked[k, pz, x + 1, y + 1]), _rows(qm[k, pz, x, y])], 0)
                split[k, x, y, :, pz * NZ : pz * NZ + NZ] = jnp.concatenate(_split(both), 0)
        return 0

    _loop2((0, BX + 1), (0, BY + 1), prepare)

    def block(p, t):
        return inside(BX * ((p - 2) // BX), BY * (t - 1))

    for p in range(BX + 4):
        for t in range(3):
            rim[p, BY * t : BY * t + BY] = jnp.zeros((BY, NZ), jnp.float32) + block(p, t)
    weights = _cone(rim)
    rho = [0.3 + 0.7 * lev[2 + x, 2 : 2 + BY, 0, :].astype(jnp.float32) / (LEVELS - 1) for x in range(BX)]

    last = finish(n_going)
    lane8 = lax.broadcasted_iota(jnp.int32, (8, NZ), 1)
    for t in range(3):
        rows = last if t == 1 else pltpu.roll(last, (24 * (1 - t)) % NZ, axis=1)
        tiles[3 + t] = tiles[3 + t] + jnp.where((lane8 >= 24) & (lane8 < 48), rows, 0.0)
    tiles, scales = _eliminate(tiles, scales, range(24, 48))
    half = jnp.concatenate(tiles[6:], 0) * scales
    mix = half + pltpu.roll(half, 48, axis=1)
    mix = jnp.concatenate([mix, gap8], 0)
    high, low = _split(mix)
    coefs = jnp.concatenate([high, low], 0)[:, :96]

    def combine(x, y, _):
        for k in range(3):
            u = jnp.dot(coefs, split[k, x, y], preferred_element_type=jnp.float32)
            u = u[:24] + u[32:56]
            for pz in (0, 1):
                disp[k, pz, x, y] = u[:, pz * NZ : pz * NZ + NZ].reshape(CT, 8, NZ)
        return 0

    _loop2((0, BX + 1), (0, BY + 1), combine, unroll=3)

    def s_at(k, pz, x, y, ct):
        return disp[k, pz, x, y, ct]

    for x in range(BX):
        energy[x] = jnp.zeros((BY, 8, NZ), jnp.float32)

    def energies(ct, _):
        for x in range(BX):
            first = _stage(s_at, x, 0, ct)

            def step(y, state, x=x):
                s1 = _stage(s_at, x, y + 1, ct)
                energy[x, y] += _density_of_energy(_modes(dict(zip(KEYS, state)), s1))
                return tuple(s1[key] for key in KEYS)

            lax.fori_loop(0, BY, step, tuple(first[key] for key in KEYS), unroll=2)
        return 0

    lax.fori_loop(0, CT, energies, 0)

    for x in range(BX):
        sens = -3.0 * rho[x] * rho[x] * jnp.sum(energy[x], axis=1) / CASES
        vals[2 + x, BY : 2 * BY] = rho[x] * sens
    group = []
    for n, (dx, dy) in enumerate(NEIGHBOURS):
        at_x, at_y = 2 - BX * dx, BY - BY * dy
        group.append(pltpu.make_async_remote_copy(
            vals.at[2 : 2 + BX, BY : 2 * BY], vals.at[at_x : at_x + BX, at_y : at_y + BY], v_send.at[n], v_recv.at[n],
            device_id=there(dx, dy), device_id_type=MESH))
    for copy in group:
        copy.start()
    for copy in small + set_a + set_b + sent:
        copy.wait_send()
    for copy in group:
        copy.wait_recv()
    for p in range(BX + 4):
        for t in range(3):
            rim[p, BY * t : BY * t + BY] = vals[p, BY * t : BY * t + BY] * block(p, t)
    sums = _cone(rim)
    for x in range(BX):
        out[x] = sums[x] / (rho[x] * weights[x])
    for copy in group:
        copy.wait_send()


def _phases(nx, ny):
    core, along_x = [(1, 0)], [(2, 0), (0, 1), (2, 1)]
    along_y = [(4 * o, 0) for o in range(1, nx // 4)]
    along_z = [(0, 2 * o) for o in range(1, ny // 2)]

    def product(fast, slow):
        return [(a ^ c, b ^ d) for c, d in [(0, 0)] + slow for a, b in [(0, 0)] + fast][1:]

    first = [product(core, along_x), along_y, along_z]
    second = [product(core, along_x), product(along_y, along_z)]
    return [g for g in first if g], [g for g in second if g]


def solution(mesh):
    nx, ny = mesh.shape["gx"], mesh.shape["gy"]
    phases, phases2 = _phases(nx, ny)
    slots, slots2 = (sum(len(g) for g in p) for p in (phases, phases2))
    f32 = jnp.float32
    dma = pltpu.SemaphoreType.DMA
    any_space = pl.BlockSpec(memory_space=pl.ANY)

    def local(forces, levels, supports):
        return pl.pallas_call(
            functools.partial(_kernel, nx, ny, phases, phases2),
            out_shape=jax.ShapeDtypeStruct((BX, BY, NZ), f32),
            in_specs=[any_space] * 3,
            out_specs=pl.BlockSpec(memory_space=pltpu.VMEM),
            scratch_shapes=[
                pltpu.VMEM((3 * CASES * BX * BY, NZ), f32),
                pltpu.VMEM((BX + 4, BY + 4, 1, NZ), jnp.int32),
                pltpu.VMEM((BX + 3, BY + 3, 1, NZ), jnp.int32),
                pltpu.VMEM((BX + 4, BY + 4, len(SCALES), 8, NZ), f32),
                pltpu.VMEM((BX + 4, BY + 4, 8, NZ), f32),
                pltpu.VMEM((BX + 3, BY + 3, 8, NZ), f32),
                pltpu.VMEM((BX + 3, BY + 3, 8, NZ), f32),
                pltpu.VMEM((3, BX + 3, BY + 3, CT, 8, NZ), f32),
                pltpu.VMEM((3, BX + 3, BY + 3, CT, 8, NZ), f32),
                pltpu.VMEM((3, 2, BX + 3, BY + 3, CT, 8, NZ), f32),
                pltpu.VMEM((3, 2, BX + 1, BY + 2, CT, 8, NZ), f32),
                pltpu.VMEM((3, BX + 1, BY + 1, CT, 8, NZ), f32),
                pltpu.VMEM((3, 2, BX + 1, BY + 1, CT, 8, NZ), f32),
                pltpu.VMEM((3, 2, BX + 1, BY + 1, CT, 8, NZ), f32),
                pltpu.VMEM((3, BX + 1, BY + 1, 96, 2 * NZ), jnp.bfloat16),
                pltpu.VMEM((3, 2, BX + 1, BY + 1, CT, 8, NZ), f32),
                pltpu.VMEM((BX, BY, 8, NZ), f32),
                pltpu.VMEM((BX + 4, 3 * BY, NZ), f32),
                pltpu.VMEM((BX + 4, 3 * BY, NZ), f32),
                pltpu.VMEM((len(phases), CASES, NZ), f32),
                pltpu.VMEM((slots, CASES, NZ), f32),
                pltpu.VMEM((len(phases2), 8, NZ), f32),
                pltpu.VMEM((slots2, 8, NZ), f32),
                dma((3,)),
                dma((8,)), dma((8,)), dma((8,)), dma((8,)), dma((14,)), dma((14,)), dma((8,)), dma((8,)),
                dma((slots,)), dma((slots,)), dma((slots2,)), dma((slots2,)),
            ],
            compiler_params=pltpu.CompilerParams(collective_id=0, has_side_effects=True),
        )(
            forces.reshape(3 * CASES * BX * BY, NZ),
            levels.reshape(BX, BY, 1, NZ),
            supports.reshape(BX, BY, 1, NZ),
        )

    return jax.shard_map(
        local,
        mesh=mesh,
        in_specs=(P(None, None, "gx", "gy", None), P("gx", "gy", None), P("gx", "gy", None)),
        out_specs=P("gx", "gy", None),
        check_vma=False,
    )
```

```python
import functools
import math

import jax
import jax.numpy as jnp
import numpy as np
from jax import lax
from jax.experimental import pallas as pl
from jax.experimental.pallas import tpu as pltpu
from jax.sharding import PartitionSpec as P

MESH = pl.DeviceIdType.MESH
CASES = 24
LEVELS = 16
LOAD = 0.2
BX, BY, NZ = 2, 8, 128
CT = 3


def element_matrix():
    poisson = 0.3
    lame_first = poisson / ((1.0 + poisson) * (1.0 - 2.0 * poisson))
    lame_shear = 1.0 / (2.0 * (1.0 + poisson))
    elastic = np.zeros((6, 6))
    elastic[:3, :3] = lame_first
    for position in range(3):
        elastic[position, position] += 2.0 * lame_shear
        elastic[position + 3, position + 3] = lame_shear
    points = [0.5 - 0.5 / math.sqrt(3.0), 0.5 + 0.5 / math.sqrt(3.0)]
    matrix = np.zeros((24, 24))
    for point_x in points:
        for point_y in points:
            for point_z in points:
                coords = (point_x, point_y, point_z)
                strain = np.zeros((6, 24))
                for corner in range(8):
                    bits = (corner >> 2 & 1, corner >> 1 & 1, corner & 1)
                    shape = [coords[n] if bits[n] else 1.0 - coords[n] for n in range(3)]
                    slopes = [1.0 if bits[n] else -1.0 for n in range(3)]
                    slope_x = slopes[0] * shape[1] * shape[2]
                    slope_y = shape[0] * slopes[1] * shape[2]
                    slope_z = shape[0] * shape[1] * slopes[2]
                    o = 3 * corner
                    strain[0, o] = slope_x
                    strain[1, o + 1] = slope_y
                    strain[2, o + 2] = slope_z
                    strain[3, o] = slope_y
                    strain[3, o + 1] = slope_x
                    strain[4, o + 1] = slope_z
                    strain[4, o + 2] = slope_y
                    strain[5, o] = slope_z
                    strain[5, o + 2] = slope_x
                matrix = matrix + strain.T @ elastic @ strain / 8.0
    return matrix


KE = element_matrix()
DIAG = float(KE[0, 0])


def parity_matrix():
    walsh = np.ones((8, 8))
    for mode in range(8):
        for corner in range(8):
            for n in range(3):
                if mode >> n & 1:
                    walsh[mode, corner] *= 2 * (corner >> n & 1) - 1
    big = np.kron(walsh, np.eye(3))
    return big @ KE @ big.T / 64.0


KP = parity_matrix()
UNIT = ((1, 0, 0), (0, 1, 0), (0, 0, 1))


def _flip(p, k):
    return tuple(a ^ b for a, b in zip(p, UNIT[k]))


def _kp(m, n):
    at = [3 * (4 * p[0] + 2 * p[1] + p[2]) + k for k, p in (m, n)]
    return float(KP[at[0], at[1]])


NORMAL = [(k, UNIT[k]) for k in range(3)]
BEND = [(k, _flip((1, 1, 1), k)) for k in range(3)]
PAIRS = [[(k, _flip(UNIT[s], k)) for k in range(3) if k != s] for s in range(3)]
SHEAR = []
TWIST = []
for _s in range(3):
    _a, _b = [k for k in range(3) if k != _s]
    SHEAR.append([(_a, UNIT[_b]), (_b, UNIT[_a])])
    TWIST.append((_s, (1, 1, 1)))
N_OFF = _kp(NORMAL[0], NORMAL[1])
N_DIA = _kp(NORMAL[0], NORMAL[0]) - N_OFF
P_OFF = _kp(PAIRS[0][0], PAIRS[0][1])
P_DIA = _kp(PAIRS[0][0], PAIRS[0][0]) - P_OFF
S_ALL = _kp(SHEAR[0][0], SHEAR[0][0])
T_ALL = _kp(TWIST[0], TWIST[0])
B_OFF = _kp(BEND[0], BEND[1])
B_DIA = _kp(BEND[0], BEND[0]) - B_OFF


def _span(d, low, high, size):
    a = max(0, low + d * size)
    b = min(size, high + 1 + d * size)
    return a, a - d * size, b - a


NEIGHBOURS = [(dx, dy) for dx in (-1, 0, 1) for dy in (-1, 0, 1) if dx or dy]


def _shift(x, by):
    lane = lax.broadcasted_iota(jnp.int32, x.shape, x.ndim - 1)
    r = pltpu.roll(x, (-by) % NZ, axis=x.ndim - 1)
    ok = lane < NZ - by if by > 0 else lane >= -by
    return jnp.where(ok, r, 0.0)


def _stage(u_at, ex, y, ct):
    out = {}
    for k in range(3):
        for pz in (0, 1):
            u0, u1 = u_at(k, pz, ex, y, ct), u_at(k, pz, ex + 1, y, ct)
            out[k, 0, pz] = u0 + u1
            out[k, 1, pz] = u1 - u0
    return out


KEYS = [(k, px, pz) for k in range(3) for px in (0, 1) for pz in (0, 1)]


def _modes(s0, s1):
    out = {}
    for k, px, pz in KEYS:
        if (px, pz) != (0, 0):
            out[k, (px, 0, pz)] = s0[k, px, pz] + s1[k, px, pz]
        out[k, (px, 1, pz)] = s1[k, px, pz] - s0[k, px, pz]
    return out


SCALES = sorted({np.float32(c) for c in (N_OFF, N_DIA, P_OFF, P_DIA, S_ALL, T_ALL, B_OFF, B_DIA)})


def _stress(u, e_at):
    def e(c):
        return e_at(SCALES.index(np.float32(c)))

    g = {}
    for group, off, dia in ((NORMAL, N_OFF, N_DIA), (BEND, B_OFF, B_DIA)):
        total = (u[group[0]] + u[group[1]] + u[group[2]]) * e(off)
        for m in group:
            g[m] = u[m] * e(dia) + total
    for a, b in PAIRS:
        total = (u[a] + u[b]) * e(P_OFF)
        g[a] = u[a] * e(P_DIA) + total
        g[b] = u[b] * e(P_DIA) + total
    for a, b in SHEAR:
        g[a] = g[b] = (u[a] + u[b]) * e(S_ALL)
    for m in TWIST:
        g[m] = u[m] * e(T_ALL)
    return g


def _density_of_energy(u):
    def sq(x):
        return x * x

    e = N_OFF * sq(u[NORMAL[0]] + u[NORMAL[1]] + u[NORMAL[2]])
    e = e + N_DIA * (sq(u[NORMAL[0]]) + sq(u[NORMAL[1]]) + sq(u[NORMAL[2]]))
    e = e + B_OFF * sq(u[BEND[0]] + u[BEND[1]] + u[BEND[2]])
    e = e + B_DIA * (sq(u[BEND[0]]) + sq(u[BEND[1]]) + sq(u[BEND[2]]))
    off = dia = she = twi = 0.0
    for a, b in PAIRS:
        off = off + sq(u[a] + u[b])
        dia = dia + sq(u[a]) + sq(u[b])
    for a, b in SHEAR:
        she = she + sq(u[a] + u[b])
    for m in TWIST:
        twi = twi + sq(u[m])
    return e + P_OFF * off + P_DIA * dia + S_ALL * she + T_ALL * twi


def _apply(u_at, e_at, add, layers, y_low, columns, close, unroll=2):
    def tile(ct, _):
        for ex in layers:
            first = _stage(u_at, ex, y_low, ct)
            zero = jnp.zeros((8, NZ), jnp.float32)

            def emit(y, h, ex=ex):
                for k in range(3):
                    for pz in (0, 1):
                        p0, p1 = h[k, 0, pz], h[k, 1, pz]
                        add(k, pz, ex, ex, y, ct, p0, p1)
                        add(k, pz, ex, ex + 1, y, ct, p0, p1)

            def step(t, state, ex=ex):
                s0 = dict(zip(KEYS, state[0]))
                carry = dict(zip(KEYS, state[1]))
                y = y_low + t
                s1 = _stage(u_at, ex, y + 1, ct)
                g = _stress(_modes(s0, s1), functools.partial(e_at, ex, y))
                h, later = {}, {}
                for key in KEYS:
                    k, px, pz = key
                    g1 = g[k, (px, 1, pz)]
                    g0 = g.get((k, (px, 0, pz)))
                    if g0 is None:
                        h[key] = carry[key] - g1
                        later[key] = g1
                    else:
                        h[key] = carry[key] + (g0 - g1)
                        later[key] = g0 + g1
                emit(y, h)
                return tuple(s1[key] for key in KEYS), tuple(later[key] for key in KEYS)

            state = (tuple(first[key] for key in KEYS), (zero,) * len(KEYS))
            if columns == 1:
                state = step(0, state)
            else:
                state = lax.fori_loop(0, columns, step, state, unroll=unroll)
            if close:
                emit(y_low + columns, dict(zip(KEYS, state[1])))
        return 0

    lax.fori_loop(0, CT, tile, 0)


def _sum_diff(u):
    up = _shift(u, 1)
    return u + up, up - u


def _gather_z(s, d):
    return (s - d) + _shift(s + d, -1)


def _loop2(xs, ys, body, state=0, unroll=1):
    def outer(x, state):
        return lax.fori_loop(ys[0], ys[1], lambda y, st: body(x, y, st), state, unroll=unroll)

    return lax.fori_loop(xs[0], xs[1], outer, state)


def _split(x):
    scaled = x * 65537.0
    high = scaled - (scaled - x)
    return high.astype(jnp.bfloat16), (x - high).astype(jnp.bfloat16)


def _rows(x):
    return x.reshape(CASES, NZ)


def _nt(a, b):
    return lax.dot_general(a, b, (((1,), (1,)), ((), ())), preferred_element_type=jnp.float32)


def _system(table):
    lane = lax.broadcasted_iota(jnp.int32, (CASES, NZ), 1)

    def left(x, by):
        return pltpu.roll(x, (-by) % NZ, axis=1)

    def join(a, b):
        return jnp.where(lane < 24, a, jnp.where(lane < 48, b, 0.0))

    blocks = [
        join(table, left(table, 24)),
        join(left(table, 48), jnp.zeros_like(table)),
        join(left(table, 24), left(table, 48)),
    ]
    return [b[8 * i : 8 * i + 8] for b in blocks for i in range(3)]


def _eliminate(tiles, scales, steps, width=4):
    lane = lax.broadcasted_iota(jnp.int32, (8, NZ), 1)

    def one_row(x, r):
        return jnp.broadcast_to(x[r : r + 1], (8, NZ))

    for first in range(steps.start, steps.stop, width):
        own, at = first // 8, first % 8
        live = range(own, 9)
        cols = [{t: jnp.broadcast_to(tiles[t][:, first + m : first + m + 1], (8, NZ)) for t in live} for m in range(width)]
        rows = [one_row(tiles[own], at + m) for m in range(width)]
        factors = []
        for m in range(width):
            scale = 1.0 / one_row(cols[m][own], at + m)
            factor = jnp.where(lane == first + m, 0.0, rows[m] * scale)
            scales = jnp.where(lane == first + m, scale, scales)
            factors.append(factor)
            for later in range(m + 1, width):
                share = one_row(cols[later][own], at + m) * scale
                rows[later] = rows[later] - one_row(cols[m][own], at + later) * factor
                for t in live:
                    cols[later][t] = cols[later][t] - cols[m][t] * share
        for t in live:
            for m in range(width):
                tiles[t] = tiles[t] - cols[m][t] * factors[m]
    return tiles, scales


def _weight(dx, dy, dz):
    return max(0.0, 2.5 - math.sqrt(dx * dx + dy * dy + dz * dz))


def _cone(planes):
    by_row = {}
    for p in range(BX + 4):
        by_row[p, 0] = planes[p, BY : 2 * BY]
        for dy in (1, 2):
            by_row[p, dy] = planes[p, BY + dy : 2 * BY + dy] + planes[p, BY - dy : 2 * BY - dy]
    result = []
    for xo in range(BX):
        total = None
        for dz in range(3):
            part = jnp.zeros((BY, NZ), jnp.float32)
            for dx in range(-2, 3):
                for dy in range(3):
                    w = _weight(dx, dy, dz)
                    if w > 0.0:
                        part = part + w * by_row[xo + 2 + dx, dy]
            total = part if dz == 0 else total + (_shift(part, dz) + _shift(part, -dz))
        result.append(total)
    return result


EDGE_Y = [(0, dy, (0, 0, BX), _span(dy, -1, 8, BY)) for dy in (-1, 1)]
EDGE_X = [(dx, 0, _span(dx, -1, 2, BX), (0, 0, BY)) for dx in (-1, 1)]
CORNERS = [(dx, dy, _span(dx, -1, 2, BX), _span(dy, -1, 8, BY)) for dx in (-1, 1) for dy in (-1, 1)]
FAR_Y = [(0, -1, (0, 0, BX), (1, 9, 1))]
FAR_X = [(-1, 0, (1, 3, 1), (0, 0, BY))]
FAR_CORNERS = [
    (-1, 1, (1, 3, 1), (7, -1, 1)),
    (-1, -1, (1, 3, 1), (0, 8, 2)),
    (-1, -1, (0, 2, 1), (1, 9, 1)),
    (1, -1, (1, -1, 1), (1, 9, 1)),
]
HALO = [EDGE_Y, EDGE_X, CORNERS, FAR_Y, FAR_X, FAR_CORNERS]


def _kernel(nx, ny, phases, phases2, forces, levels, supports, out, nat, lev, sup, stiff, stiffz, inv, free, field, dire, masked,
            image, qf, qm, wf, split, disp, energy, vals, rim, gram_send, gram_recv, last_send, last_recv, local_sem, l_send, l_recv, s_send,
            s_recv, f_send, f_recv, v_send, v_recv, g_send, g_recv, n_send, n_recv):
    i, j = lax.axis_index("gx"), lax.axis_index("gy")

    def there(dx, dy):
        return lax.rem(i + dx + nx, nx), lax.rem(j + dy + ny, ny)

    peers = [there(dx, dy) for dx, dy in NEIGHBOURS]
    for phase in phases:
        for ox, oy in phase:
            peers.append((i ^ ox, j ^ oy))

    c_nat = pltpu.make_async_copy(forces, nat, local_sem.at[0])
    c_lev = pltpu.make_async_copy(levels, lev.at[2 : 2 + BX, 2 : 2 + BY], local_sem.at[1])
    c_sup = pltpu.make_async_copy(supports, sup.at[1 : 1 + BX, 1 : 1 + BY], local_sem.at[2])
    c_nat.start()
    c_lev.start()
    c_sup.start()

    barrier = pltpu.get_barrier_semaphore()
    for peer in peers:
        pl.semaphore_signal(barrier, inc=1, device_id=peer, device_id_type=MESH)

    c_nat.wait()

    def arrange(k, _):
        for x in range(BX):
            for y in range(BY):
                rows = nat[pl.ds(k * (CASES * BX * BY) + x * BY + y, CASES, stride=BX * BY), :]
                field[k, 1 + x, 1 + y] = rows.reshape(CT, 8, NZ)
        return 0

    lax.fori_loop(0, 3, arrange, 0)
    c_lev.wait()
    c_sup.wait()

    pl.semaphore_wait(barrier, len(peers))

    small = []
    for n, (dx, dy) in enumerate(NEIGHBOURS):
        (a, b, c), (d, e, f) = _span(dx, -2, 3, BX), _span(dy, -2, 9, BY)
        small.append(pltpu.make_async_remote_copy(
            levels.at[a : a + c, d : d + f], lev.at[b + 2 : b + 2 + c, e + 2 : e + 2 + f],
            l_send.at[n], l_recv.at[n], device_id=there(dx, dy), device_id_type=MESH))
        (a, b, c), (d, e, f) = _span(dx, -1, 3, BX), _span(dy, -1, 9, BY)
        small.append(pltpu.make_async_remote_copy(
            supports.at[a : a + c, d : d + f], sup.at[b + 1 : b + 1 + c, e + 1 : e + 1 + f],
            s_send.at[n], s_recv.at[n], device_id=there(dx, dy), device_id_type=MESH))

    odd = lax.rem(i, 2)
    halo, n = [], 0
    for group in HALO:
        halo.append([])
        for dx, dy, (a, b, c), (d, e, f) in group:
            if dx and dy:
                direct = odd if dx > 0 else 1 - odd
                columns = pl.ds(e + 1 + direct * (d - e), f)
                peer = there(dx, direct * dy)
            else:
                columns = pl.ds(d + 1, f)
                peer = there(dx, dy)
            halo[-1].append(pltpu.make_async_remote_copy(
                field.at[:, a + 1 : a + 1 + c, columns], field.at[:, b + 1 : b + 1 + c, e + 1 : e + 1 + f],
                f_send.at[n], f_recv.at[n], device_id=peer, device_id_type=MESH))
            n += 1
    edge_y, edge_x, corners, far_y, far_x, far_corners = halo
    set_b = far_y + far_x + far_corners
    for copy in small + edge_y + edge_x:
        copy.start()
    for copy in small:
        copy.wait_recv()

    def inside(x, y):
        gx, gy = i * BX + x, j * BY + y
        ok = (gx >= 0) & (gx < nx * BX) & (gy >= 0) & (gy < ny * BY)
        return jnp.where(ok, 1.0, 0.0).astype(jnp.float32)

    def moduli(x, y, _):
        level = jnp.broadcast_to(lev[x, y], (8, NZ)).astype(jnp.float32)
        rho = 0.3 + 0.7 * level / (LEVELS - 1)
        e = rho * rho * rho * inside(x - 2, y - 2)
        for n, c in enumerate(SCALES):
            stiff[x, y, n] = e * float(c)
        stiffz[x, y] = (e + _shift(e, -1)) * DIAG
        return 0

    _loop2((0, BX + 4), (0, BY + 4), moduli, unroll=4)

    def nodal(x, y, _):
        fr = (1 - jnp.broadcast_to(sup[x, y], (8, NZ))).astype(jnp.float32) * inside(x - 1, y - 1)
        total = (stiffz[x, y] + stiffz[x + 1, y]) + (stiffz[x, y + 1] + stiffz[x + 1, y + 1])
        free[x, y] = fr
        inv[x, y] = 1.0 / (fr * total + (1.0 - fr))
        return 0

    _loop2((0, BX + 3), (0, BY + 3), nodal, unroll=3)

    def search(x, y, _):
        fr, iv = free[x, y], inv[x, y]
        for k in range(3):
            d = iv * (LOAD * fr * field[k, x, y])
            dire[k, x, y] = d
            s, t = _sum_diff(fr * d)
            masked[k, 0, x, y] = s
            masked[k, 1, x, y] = t
        return 0

    for copy in edge_y:
        copy.wait_recv()
    for copy in corners + far_y + far_x:
        copy.start()
    _loop2((1, 1 + BX), (0, BY + 2), search, unroll=2)

    def u_at(k, pz, x, y, ct):
        return masked[k, pz, x + 1, y + 1, ct]

    def e_at(x, y, n):
        return stiff[x + 2, y + 2, n]

    def adder(ref, fresh, shift, planes):
        def add(k, pz, ex, x, y, ct, p0, p1):
            if x not in planes:
                return
            value = p0 - p1 if x == ex else p0 + p1
            if fresh(ex, x):
                ref[k, pz, x, y + shift, ct] = value
            else:
                ref[k, pz, x, y + shift, ct] += value
        return add

    at_nodes = range(BX + 1)
    add_near = adder(image, lambda ex, x: ex == 0 or x == BX, 1, at_nodes)
    _apply(u_at, e_at, add_near, range(0, 1), -1, BY + 1, True, unroll=3)
    for copy in far_y:
        copy.wait_recv()
    for copy in far_corners:
        copy.start()
    for copy in edge_x + corners:
        copy.wait_recv()
    _loop2((0, 1), (0, BY + 2), search, unroll=2)
    _loop2((BX + 1, BX + 2), (0, BY + 2), search, unroll=2)
    _apply(u_at, e_at, add_near, (-1, BX - 1), -1, BY + 1, True, unroll=3)

    gap = jnp.zeros((16, NZ), jnp.bfloat16)
    gap8 = jnp.zeros((8, NZ), jnp.float32)
    gap32 = jnp.zeros((32, NZ), jnp.bfloat16)

    def above(x, y):
        fr, iv = free[x + 1, y + 1], inv[x + 1, y + 1]
        nodes = []
        for k in range(3):
            d = dire[k, x + 1, y + 1]
            im = fr * _gather_z(image[k, 0, x, y + 1], image[k, 1, x, y + 1]) + (1.0 - fr) * d
            q = iv * im
            s, t = _sum_diff(fr * q)
            qm[k, 0, x, y] = s
            qm[k, 1, x, y] = t
            nodes.append((d, im, q))
        return nodes, fr

    def first_gram(x, y, acc):
        nodes, fr = above(x, y)
        left, right = [], []
        for k, (d, im, q) in enumerate(nodes):
            qf[k, x, y] = q
            r0 = LOAD * fr * field[k, x + 1, y + 1]
            left.append(jnp.concatenate(_split(jnp.concatenate([_rows(d), _rows(q)], 0)), 0))
            high, low = _split(jnp.concatenate([_rows(im), _rows(r0)], 0))
            right.append(jnp.concatenate([high, gap, low, gap], 0))
        return acc + _nt(jnp.concatenate(left, 1), jnp.concatenate(right, 1))

    acc = _loop2((0, BX), (0, BY), first_gram, jnp.zeros((96, NZ), jnp.float32), unroll=4)
    lane = lax.broadcasted_iota(jnp.int32, (CASES, NZ), 1)
    both = acc[:48] + acc[48:]
    both = both + pltpu.roll(both, 64, axis=1)
    table = jnp.where(lane < 48, both[:24], jnp.where(lane < 96, pltpu.roll(both[24:], 48, axis=1), 0.0))

    sent = []

    def begin(n, value, groups, source, target, send_sem, recv_sem):
        slot = sum(len(p) for p in groups[:n])
        source[n] = value
        group = [pltpu.make_async_remote_copy(
            source.at[n], target.at[slot + m], send_sem.at[slot + m], recv_sem.at[slot + m],
            device_id=(i ^ ox, j ^ oy), device_id_type=MESH) for m, (ox, oy) in enumerate(groups[n])]
        for copy in group:
            copy.start()
        sent.extend(group)
        return value, slot, group, target

    def begin1(n, value):
        return begin(n, value, phases, gram_send, gram_recv, g_send, g_recv)

    def begin2(n, value):
        return begin(n, value, phases2, last_send, last_recv, n_send, n_recv)

    def finish(going):
        value, slot, group, target = going
        for copy in group:
            copy.wait_recv()
        terms = [value] + [target[slot + m] for m in range(len(group))]
        while len(terms) > 1:
            terms = [terms[t] + terms[t + 1] for t in range(0, len(terms), 2)]
        return terms[0]

    todo = list(range(len(phases)))
    going = begin1(todo.pop(0), table)

    def pair(left, right, acc):
        a, b = [], []
        for u, v in zip(left, right):
            a.append(jnp.concatenate(_split(jnp.concatenate([_rows(u), gap8], 0)), 0))
            high, low = _split(jnp.concatenate([_rows(v), gap8], 0))
            b.append(jnp.concatenate([high, gap32, low, gap32], 0))
        return acc + _nt(jnp.concatenate(a, 1), jnp.concatenate(b, 1))

    def clamped(x, y, acc):
        fr = free[x + 1, y + 1]
        q = [qf[k, x, y] for k in range(3)]
        return pair(q, [(1.0 - fr) * v for v in q], acc)

    acc2 = _loop2((0, BX), (0, BY), clamped, jnp.zeros((64, NZ), jnp.float32), unroll=4)

    for copy in far_x + far_corners:
        copy.wait_recv()
    _loop2((BX + 2, BX + 3), (0, BY + 3), search, unroll=2)
    _loop2((0, BX + 2), (BY + 2, BY + 3), search, unroll=2)
    _apply(u_at, e_at, adder(image, lambda ex, x: False, 1, at_nodes), range(-1, BX), BY, 1, False)
    _apply(u_at, e_at, adder(image, lambda ex, x: False, 1, at_nodes), range(BX, BX + 1), -1, BY + 2, False, unroll=2)

    def edge(x, y, _):
        above(x, y)
        return 0

    _loop2((BX, BX + 1), (0, BY + 1), edge, unroll=3)
    _loop2((0, BX), (BY, BY + 1), edge)
    if todo:
        going = begin1(todo.pop(0), finish(going))

    def q_at(k, pz, x, y, ct):
        return qm[k, pz, x, y, ct]

    _apply(q_at, e_at, adder(wf, lambda ex, x: x == ex + 1 or ex == 0, 0, at_nodes), range(BX), 0, BY, True, unroll=2)

    def second_gram(x, y, acc):
        at = [(k, pz) for k in range(3) for pz in (0, 1)]
        return pair([qm[k, pz, x, y] for k, pz in at], [wf[k, pz, x, y] for k, pz in at], acc)

    acc2 = _loop2((0, BX + 1), (0, BY + 1), second_gram, acc2, unroll=3)
    last = acc2[:24] + acc2[32:56]
    last = last + pltpu.roll(last, 64, axis=1)
    last = jnp.where(lane < 24, last, 0.0)
    last = last[:8] + pltpu.roll(last[8:16], 24, axis=1) + pltpu.roll(last[16:], 48, axis=1)
    n_going = begin2(0, last)
    while todo:
        going = begin1(todo.pop(0), finish(going))
    n_todo = list(range(1, len(phases2)))
    if n_todo:
        n_going = begin2(n_todo.pop(0), finish(n_going))
    table = finish(going)
    tiles, scales = _eliminate(_system(table), jnp.zeros((8, NZ), jnp.float32), range(24))

    def prepare(x, y, _):
        for k in range(3):
            for pz in (0, 1):
                both = jnp.concatenate([_rows(masked[k, pz, x + 1, y + 1]), _rows(qm[k, pz, x, y])], 0)
                split[k, x, y, :, pz * NZ : pz * NZ + NZ] = jnp.concatenate(_split(both), 0)
        return 0

    _loop2((0, BX + 1), (0, BY + 1), prepare, unroll=3)

    def block(p, t):
        return inside(BX * ((p - 2) // BX), BY * (t - 1))

    for p in range(BX + 4):
        for t in range(3):
            rim[p, BY * t : BY * t + BY] = jnp.zeros((BY, NZ), jnp.float32) + block(p, t)
    weights = _cone(rim)
    rho = [0.3 + 0.7 * lev[2 + x, 2 : 2 + BY, 0, :].astype(jnp.float32) / (LEVELS - 1) for x in range(BX)]

    last = finish(n_going)
    lane8 = lax.broadcasted_iota(jnp.int32, (8, NZ), 1)
    for t in range(3):
        rows = last if t == 1 else pltpu.roll(last, (24 * (1 - t)) % NZ, axis=1)
        tiles[3 + t] = tiles[3 + t] + jnp.where((lane8 >= 24) & (lane8 < 48), rows, 0.0)
    tiles, scales = _eliminate(tiles, scales, range(24, 48))
    half = jnp.concatenate([t * scales for t in tiles[6:]], 0)
    mix = half + pltpu.roll(half, 48, axis=1)
    mix = jnp.concatenate([mix, gap8], 0)
    high, low = _split(mix)
    coefs = jnp.concatenate([high, low], 0)[:, :96]

    def combine(x, y, _):
        for k in range(3):
            u = jnp.dot(coefs, split[k, x, y], preferred_element_type=jnp.float32)
            u = u[:24] + u[32:56]
            for pz in (0, 1):
                disp[k, pz, x, y] = u[:, pz * NZ : pz * NZ + NZ].reshape(CT, 8, NZ)
        return 0

    _loop2((0, BX + 1), (0, BY + 1), combine, unroll=3)

    def s_at(k, pz, x, y, ct):
        return disp[k, pz, x, y, ct]

    for x in range(BX):
        energy[x] = jnp.zeros((BY, 8, NZ), jnp.float32)

    def energies(ct, _):
        for x in range(BX):
            first = _stage(s_at, x, 0, ct)

            def step(y, state, x=x):
                s1 = _stage(s_at, x, y + 1, ct)
                energy[x, y] += _density_of_energy(_modes(dict(zip(KEYS, state)), s1))
                return tuple(s1[key] for key in KEYS)

            lax.fori_loop(0, BY, step, tuple(first[key] for key in KEYS), unroll=2)
        return 0

    lax.fori_loop(0, CT, energies, 0)

    for x in range(BX):
        sens = -3.0 * rho[x] * rho[x] * jnp.sum(energy[x], axis=1) / CASES
        vals[2 + x, BY : 2 * BY] = rho[x] * sens
    group = []
    for n, (dx, dy) in enumerate(NEIGHBOURS):
        at_x, at_y = 2 - BX * dx, BY - BY * dy
        group.append(pltpu.make_async_remote_copy(
            vals.at[2 : 2 + BX, BY : 2 * BY], vals.at[at_x : at_x + BX, at_y : at_y + BY], v_send.at[n], v_recv.at[n],
            device_id=there(dx, dy), device_id_type=MESH))
    for copy in group:
        copy.start()
    for copy in small + edge_y + edge_x + corners + set_b + sent:
        copy.wait_send()
    for copy in group:
        copy.wait_recv()
    for p in range(BX + 4):
        for t in range(3):
            rim[p, BY * t : BY * t + BY] = vals[p, BY * t : BY * t + BY] * block(p, t)
    sums = _cone(rim)
    for x in range(BX):
        out[x] = sums[x] / (rho[x] * weights[x])
    for copy in group:
        copy.wait_send()


def _phases(nx, ny):
    core, along_x = [(1, 0)], [(2, 0), (0, 1), (2, 1)]
    along_y = [(4 * o, 0) for o in range(1, nx // 4)]
    along_z = [(0, 2 * o) for o in range(1, ny // 2)]

    def product(fast, slow):
        return [(a ^ c, b ^ d) for c, d in [(0, 0)] + slow for a, b in [(0, 0)] + fast][1:]

    first = [product(core, along_x), along_y, along_z]
    second = [product(core, along_x), product(along_y, along_z)]
    return [g for g in first if g], [g for g in second if g]


def solution(mesh):
    nx, ny = mesh.shape["gx"], mesh.shape["gy"]
    phases, phases2 = _phases(nx, ny)
    slots, slots2 = (sum(len(g) for g in p) for p in (phases, phases2))
    f32 = jnp.float32
    dma = pltpu.SemaphoreType.DMA
    any_space = pl.BlockSpec(memory_space=pl.ANY)

    def local(forces, levels, supports):
        return pl.pallas_call(
            functools.partial(_kernel, nx, ny, phases, phases2),
            out_shape=jax.ShapeDtypeStruct((BX, BY, NZ), f32),
            in_specs=[any_space] * 3,
            out_specs=pl.BlockSpec(memory_space=pltpu.VMEM),
            scratch_shapes=[
                pltpu.VMEM((3 * CASES * BX * BY, NZ), f32),
                pltpu.VMEM((BX + 4, BY + 4, 1, NZ), jnp.int32),
                pltpu.VMEM((BX + 3, BY + 3, 1, NZ), jnp.int32),
                pltpu.VMEM((BX + 4, BY + 4, len(SCALES), 8, NZ), f32),
                pltpu.VMEM((BX + 4, BY + 4, 8, NZ), f32),
                pltpu.VMEM((BX + 3, BY + 3, 8, NZ), f32),
                pltpu.VMEM((BX + 3, BY + 3, 8, NZ), f32),
                pltpu.VMEM((3, BX + 3, BY + 3, CT, 8, NZ), f32),
                pltpu.VMEM((3, BX + 3, BY + 3, CT, 8, NZ), f32),
                pltpu.VMEM((3, 2, BX + 3, BY + 3, CT, 8, NZ), f32),
                pltpu.VMEM((3, 2, BX + 1, BY + 2, CT, 8, NZ), f32),
                pltpu.VMEM((3, BX + 1, BY + 1, CT, 8, NZ), f32),
                pltpu.VMEM((3, 2, BX + 1, BY + 1, CT, 8, NZ), f32),
                pltpu.VMEM((3, 2, BX + 1, BY + 1, CT, 8, NZ), f32),
                pltpu.VMEM((3, BX + 1, BY + 1, 96, 2 * NZ), jnp.bfloat16),
                pltpu.VMEM((3, 2, BX + 1, BY + 1, CT, 8, NZ), f32),
                pltpu.VMEM((BX, BY, 8, NZ), f32),
                pltpu.VMEM((BX + 4, 3 * BY, NZ), f32),
                pltpu.VMEM((BX + 4, 3 * BY, NZ), f32),
                pltpu.VMEM((len(phases), CASES, NZ), f32),
                pltpu.VMEM((slots, CASES, NZ), f32),
                pltpu.VMEM((len(phases2), 8, NZ), f32),
                pltpu.VMEM((slots2, 8, NZ), f32),
                dma((3,)),
                dma((8,)), dma((8,)), dma((8,)), dma((8,)), dma((14,)), dma((14,)), dma((8,)), dma((8,)),
                dma((slots,)), dma((slots,)), dma((slots2,)), dma((slots2,)),
            ],
            compiler_params=pltpu.CompilerParams(collective_id=0, has_side_effects=True),
        )(
            forces.reshape(3 * CASES * BX * BY, NZ),
            levels.reshape(BX, BY, 1, NZ),
            supports.reshape(BX, BY, 1, NZ),
        )

    return jax.shard_map(
        local,
        mesh=mesh,
        in_specs=(P(None, None, "gx", "gy", None), P("gx", "gy", None), P("gx", "gy", None)),
        out_specs=P("gx", "gy", None),
        check_vma=False,
    )
```

```python
import functools
import math

import jax
import jax.numpy as jnp
import numpy as np
from jax import lax
from jax.experimental import pallas as pl
from jax.experimental.pallas import tpu as pltpu
from jax.sharding import PartitionSpec as P

MESH = pl.DeviceIdType.MESH
CASES = 24
LEVELS = 16
LOAD = 0.2
BX, BY, NZ = 2, 8, 128
CT = 3


def element_matrix():
    poisson = 0.3
    lame_first = poisson / ((1.0 + poisson) * (1.0 - 2.0 * poisson))
    lame_shear = 1.0 / (2.0 * (1.0 + poisson))
    elastic = np.zeros((6, 6))
    elastic[:3, :3] = lame_first
    for position in range(3):
        elastic[position, position] += 2.0 * lame_shear
        elastic[position + 3, position + 3] = lame_shear
    points = [0.5 - 0.5 / math.sqrt(3.0), 0.5 + 0.5 / math.sqrt(3.0)]
    matrix = np.zeros((24, 24))
    for point_x in points:
        for point_y in points:
            for point_z in points:
                coords = (point_x, point_y, point_z)
                strain = np.zeros((6, 24))
                for corner in range(8):
                    bits = (corner >> 2 & 1, corner >> 1 & 1, corner & 1)
                    shape = [coords[n] if bits[n] else 1.0 - coords[n] for n in range(3)]
                    slopes = [1.0 if bits[n] else -1.0 for n in range(3)]
                    slope_x = slopes[0] * shape[1] * shape[2]
                    slope_y = shape[0] * slopes[1] * shape[2]
                    slope_z = shape[0] * shape[1] * slopes[2]
                    o = 3 * corner
                    strain[0, o] = slope_x
                    strain[1, o + 1] = slope_y
                    strain[2, o + 2] = slope_z
                    strain[3, o] = slope_y
                    strain[3, o + 1] = slope_x
                    strain[4, o + 1] = slope_z
                    strain[4, o + 2] = slope_y
                    strain[5, o] = slope_z
                    strain[5, o + 2] = slope_x
                matrix = matrix + strain.T @ elastic @ strain / 8.0
    return matrix


KE = element_matrix()
DIAG = float(KE[0, 0])


def parity_matrix():
    walsh = np.ones((8, 8))
    for mode in range(8):
        for corner in range(8):
            for n in range(3):
                if mode >> n & 1:
                    walsh[mode, corner] *= 2 * (corner >> n & 1) - 1
    big = np.kron(walsh, np.eye(3))
    return big @ KE @ big.T / 64.0


KP = parity_matrix()
UNIT = ((1, 0, 0), (0, 1, 0), (0, 0, 1))


def _flip(p, k):
    return tuple(a ^ b for a, b in zip(p, UNIT[k]))


def _kp(m, n):
    at = [3 * (4 * p[0] + 2 * p[1] + p[2]) + k for k, p in (m, n)]
    return float(KP[at[0], at[1]])


NORMAL = [(k, UNIT[k]) for k in range(3)]
BEND = [(k, _flip((1, 1, 1), k)) for k in range(3)]
PAIRS = [[(k, _flip(UNIT[s], k)) for k in range(3) if k != s] for s in range(3)]
SHEAR = []
TWIST = []
for _s in range(3):
    _a, _b = [k for k in range(3) if k != _s]
    SHEAR.append([(_a, UNIT[_b]), (_b, UNIT[_a])])
    TWIST.append((_s, (1, 1, 1)))
N_OFF = _kp(NORMAL[0], NORMAL[1])
N_DIA = _kp(NORMAL[0], NORMAL[0]) - N_OFF
P_OFF = _kp(PAIRS[0][0], PAIRS[0][1])
P_DIA = _kp(PAIRS[0][0], PAIRS[0][0]) - P_OFF
S_ALL = _kp(SHEAR[0][0], SHEAR[0][0])
T_ALL = _kp(TWIST[0], TWIST[0])
B_OFF = _kp(BEND[0], BEND[1])
B_DIA = _kp(BEND[0], BEND[0]) - B_OFF


def _span(d, low, high, size):
    a = max(0, low + d * size)
    b = min(size, high + 1 + d * size)
    return a, a - d * size, b - a


NEIGHBOURS = [(dx, dy) for dx in (-1, 0, 1) for dy in (-1, 0, 1) if dx or dy]


def _shift(x, by):
    lane = lax.broadcasted_iota(jnp.int32, x.shape, x.ndim - 1)
    r = pltpu.roll(x, (-by) % NZ, axis=x.ndim - 1)
    ok = lane < NZ - by if by > 0 else lane >= -by
    return jnp.where(ok, r, 0.0)


def _stage(u_at, ex, y, ct):
    out = {}
    for k in range(3):
        for pz in (0, 1):
            u0, u1 = u_at(k, pz, ex, y, ct), u_at(k, pz, ex + 1, y, ct)
            out[k, 0, pz] = u0 + u1
            out[k, 1, pz] = u1 - u0
    return out


KEYS = [(k, px, pz) for k in range(3) for px in (0, 1) for pz in (0, 1)]


def _modes(s0, s1):
    out = {}
    for k, px, pz in KEYS:
        if (px, pz) != (0, 0):
            out[k, (px, 0, pz)] = s0[k, px, pz] + s1[k, px, pz]
        out[k, (px, 1, pz)] = s1[k, px, pz] - s0[k, px, pz]
    return out


SCALES = sorted({np.float32(c) for c in (N_OFF, N_DIA, P_OFF, P_DIA, S_ALL, T_ALL, B_OFF, B_DIA)})


def _stress(u, e_at):
    def e(c):
        return e_at(SCALES.index(np.float32(c)))

    g = {}
    for group, off, dia in ((NORMAL, N_OFF, N_DIA), (BEND, B_OFF, B_DIA)):
        total = (u[group[0]] + u[group[1]] + u[group[2]]) * e(off)
        for m in group:
            g[m] = u[m] * e(dia) + total
    for a, b in PAIRS:
        total = (u[a] + u[b]) * e(P_OFF)
        g[a] = u[a] * e(P_DIA) + total
        g[b] = u[b] * e(P_DIA) + total
    for a, b in SHEAR:
        g[a] = g[b] = (u[a] + u[b]) * e(S_ALL)
    for m in TWIST:
        g[m] = u[m] * e(T_ALL)
    return g


def _density_of_energy(u):
    def sq(x):
        return x * x

    e = N_OFF * sq(u[NORMAL[0]] + u[NORMAL[1]] + u[NORMAL[2]])
    e = e + N_DIA * (sq(u[NORMAL[0]]) + sq(u[NORMAL[1]]) + sq(u[NORMAL[2]]))
    e = e + B_OFF * sq(u[BEND[0]] + u[BEND[1]] + u[BEND[2]])
    e = e + B_DIA * (sq(u[BEND[0]]) + sq(u[BEND[1]]) + sq(u[BEND[2]]))
    off = dia = she = twi = 0.0
    for a, b in PAIRS:
        off = off + sq(u[a] + u[b])
        dia = dia + sq(u[a]) + sq(u[b])
    for a, b in SHEAR:
        she = she + sq(u[a] + u[b])
    for m in TWIST:
        twi = twi + sq(u[m])
    return e + P_OFF * off + P_DIA * dia + S_ALL * she + T_ALL * twi


def _apply(u_at, e_at, add, layers, y_low, columns, close, unroll=2):
    def tile(ct, _):
        for ex in layers:
            first = _stage(u_at, ex, y_low, ct)
            zero = jnp.zeros((8, NZ), jnp.float32)

            def emit(y, h, ex=ex):
                for k in range(3):
                    for pz in (0, 1):
                        p0, p1 = h[k, 0, pz], h[k, 1, pz]
                        add(k, pz, ex, ex, y, ct, p0, p1)
                        add(k, pz, ex, ex + 1, y, ct, p0, p1)

            def step(t, state, ex=ex):
                s0 = dict(zip(KEYS, state[0]))
                carry = dict(zip(KEYS, state[1]))
                y = y_low + t
                s1 = _stage(u_at, ex, y + 1, ct)
                g = _stress(_modes(s0, s1), functools.partial(e_at, ex, y))
                h, later = {}, {}
                for key in KEYS:
                    k, px, pz = key
                    g1 = g[k, (px, 1, pz)]
                    g0 = g.get((k, (px, 0, pz)))
                    if g0 is None:
                        h[key] = carry[key] - g1
                        later[key] = g1
                    else:
                        h[key] = carry[key] + (g0 - g1)
                        later[key] = g0 + g1
                emit(y, h)
                return tuple(s1[key] for key in KEYS), tuple(later[key] for key in KEYS)

            state = (tuple(first[key] for key in KEYS), (zero,) * len(KEYS))
            if columns == 1:
                state = step(0, state)
            else:
                state = lax.fori_loop(0, columns, step, state, unroll=unroll)
            if close:
                emit(y_low + columns, dict(zip(KEYS, state[1])))
        return 0

    lax.fori_loop(0, CT, tile, 0)


def _sum_diff(u):
    up = _shift(u, 1)
    return u + up, up - u


def _gather_z(s, d):
    return (s - d) + _shift(s + d, -1)


def _loop2(xs, ys, body, state=0, unroll=1):
    def outer(x, state):
        return lax.fori_loop(ys[0], ys[1], lambda y, st: body(x, y, st), state, unroll=unroll)

    return lax.fori_loop(xs[0], xs[1], outer, state)


def _split(x):
    scaled = x * 65537.0
    high = scaled - (scaled - x)
    return high.astype(jnp.bfloat16), (x - high).astype(jnp.bfloat16)


def _rows(x):
    return x.reshape(CASES, NZ)


def _nt(a, b):
    return lax.dot_general(a, b, (((1,), (1,)), ((), ())), preferred_element_type=jnp.float32)


def _system(table):
    lane = lax.broadcasted_iota(jnp.int32, (CASES, NZ), 1)

    def left(x, by):
        return pltpu.roll(x, (-by) % NZ, axis=1)

    def join(a, b):
        return jnp.where(lane < 24, a, jnp.where(lane < 48, b, 0.0))

    blocks = [
        join(table, left(table, 24)),
        join(left(table, 48), left(table, 72)),
        join(left(table, 24), left(table, 48)),
    ]
    return [b[8 * i : 8 * i + 8] for b in blocks for i in range(3)]


def _eliminate(tiles, scales, steps, width=4):
    lane = lax.broadcasted_iota(jnp.int32, (8, NZ), 1)

    def one_row(x, r):
        return jnp.broadcast_to(x[r : r + 1], (8, NZ))

    for first in range(steps.start, steps.stop, width):
        own, at = first // 8, first % 8
        live = range(own, 9)
        cols = [{t: jnp.broadcast_to(tiles[t][:, first + m : first + m + 1], (8, NZ)) for t in live} for m in range(width)]
        rows = [one_row(tiles[own], at + m) for m in range(width)]
        factors = []
        for m in range(width):
            scale = 1.0 / one_row(cols[m][own], at + m)
            factor = jnp.where(lane == first + m, 0.0, rows[m] * scale)
            scales = jnp.where(lane == first + m, scale, scales)
            factors.append(factor)
            for later in range(m + 1, width):
                share = one_row(cols[later][own], at + m) * scale
                rows[later] = rows[later] - one_row(cols[m][own], at + later) * factor
                for t in live:
                    cols[later][t] = cols[later][t] - cols[m][t] * share
        for t in live:
            for m in range(width):
                tiles[t] = tiles[t] - cols[m][t] * factors[m]
    return tiles, scales


def _weight(dx, dy, dz):
    return max(0.0, 2.5 - math.sqrt(dx * dx + dy * dy + dz * dz))


def _cone(planes):
    by_row = {}
    for p in range(BX + 4):
        by_row[p, 0] = planes[p, BY : 2 * BY]
        for dy in (1, 2):
            by_row[p, dy] = planes[p, BY + dy : 2 * BY + dy] + planes[p, BY - dy : 2 * BY - dy]
    result = []
    for xo in range(BX):
        total = None
        for dz in range(3):
            part = jnp.zeros((BY, NZ), jnp.float32)
            for dx in range(-2, 3):
                for dy in range(3):
                    w = _weight(dx, dy, dz)
                    if w > 0.0:
                        part = part + w * by_row[xo + 2 + dx, dy]
            total = part if dz == 0 else total + (_shift(part, dz) + _shift(part, -dz))
        result.append(total)
    return result


EDGE_Y = [(0, dy, (0, 0, BX), _span(dy, -1, 8, BY)) for dy in (-1, 1)]
EDGE_X = [(dx, 0, _span(dx, -1, 2, BX), (0, 0, BY)) for dx in (-1, 1)]
CORNERS = [(dx, dy, _span(dx, -1, 2, BX), _span(dy, -1, 8, BY)) for dx in (-1, 1) for dy in (-1, 1)]
FAR_Y = [(0, -1, (0, 0, BX), (1, 9, 1))]
FAR_X = [(-1, 0, (1, 3, 1), (0, 0, BY))]
FAR_CORNERS = [
    (-1, 1, (1, 3, 1), (7, -1, 1)),
    (-1, -1, (1, 3, 1), (0, 8, 2)),
    (-1, -1, (0, 2, 1), (1, 9, 1)),
    (1, -1, (1, -1, 1), (1, 9, 1)),
]
HALO = [EDGE_Y, EDGE_X, CORNERS, FAR_Y, FAR_X, FAR_CORNERS]


def _kernel(nx, ny, phases, phases2, forces, levels, supports, out, nat, lev, sup, stiff, stiffz, inv, free, field, dire, masked,
            image, qm, wf, split, disp, energy, vals, rim, gram_send, gram_recv, last_send, last_recv, local_sem, l_send, l_recv, s_send,
            s_recv, f_send, f_recv, v_send, v_recv, g_send, g_recv, n_send, n_recv):
    i, j = lax.axis_index("gx"), lax.axis_index("gy")

    def there(dx, dy):
        return lax.rem(i + dx + nx, nx), lax.rem(j + dy + ny, ny)

    peers = [there(dx, dy) for dx, dy in NEIGHBOURS]
    for phase in phases:
        for ox, oy in phase:
            peers.append((i ^ ox, j ^ oy))

    c_nat = pltpu.make_async_copy(forces, nat, local_sem.at[0])
    c_lev = pltpu.make_async_copy(levels, lev.at[2 : 2 + BX, 2 : 2 + BY], local_sem.at[1])
    c_sup = pltpu.make_async_copy(supports, sup.at[1 : 1 + BX, 1 : 1 + BY], local_sem.at[2])
    c_nat.start()
    c_lev.start()
    c_sup.start()

    barrier = pltpu.get_barrier_semaphore()
    for peer in peers:
        pl.semaphore_signal(barrier, inc=1, device_id=peer, device_id_type=MESH)

    c_nat.wait()

    def arrange(k, _):
        for x in range(BX):
            for y in range(BY):
                rows = nat[pl.ds(k * (CASES * BX * BY) + x * BY + y, CASES, stride=BX * BY), :]
                field[k, 1 + x, 1 + y] = rows.reshape(CT, 8, NZ)
        return 0

    lax.fori_loop(0, 3, arrange, 0)
    c_lev.wait()
    c_sup.wait()

    pl.semaphore_wait(barrier, len(peers))

    small = []
    for n, (dx, dy) in enumerate(NEIGHBOURS):
        (a, b, c), (d, e, f) = _span(dx, -2, 3, BX), _span(dy, -2, 9, BY)
        small.append(pltpu.make_async_remote_copy(
            levels.at[a : a + c, d : d + f], lev.at[b + 2 : b + 2 + c, e + 2 : e + 2 + f],
            l_send.at[n], l_recv.at[n], device_id=there(dx, dy), device_id_type=MESH))
        (a, b, c), (d, e, f) = _span(dx, -1, 3, BX), _span(dy, -1, 9, BY)
        small.append(pltpu.make_async_remote_copy(
            supports.at[a : a + c, d : d + f], sup.at[b + 1 : b + 1 + c, e + 1 : e + 1 + f],
            s_send.at[n], s_recv.at[n], device_id=there(dx, dy), device_id_type=MESH))

    odd = lax.rem(i, 2)
    halo, n = [], 0
    for group in HALO:
        halo.append([])
        for dx, dy, (a, b, c), (d, e, f) in group:
            if dx and dy:
                direct = odd if dx > 0 else 1 - odd
                columns = pl.ds(e + 1 + direct * (d - e), f)
                peer = there(dx, direct * dy)
            else:
                columns = pl.ds(d + 1, f)
                peer = there(dx, dy)
            halo[-1].append(pltpu.make_async_remote_copy(
                field.at[:, a + 1 : a + 1 + c, columns], field.at[:, b + 1 : b + 1 + c, e + 1 : e + 1 + f],
                f_send.at[n], f_recv.at[n], device_id=peer, device_id_type=MESH))
            n += 1
    edge_y, edge_x, corners, far_y, far_x, far_corners = halo
    set_b = far_y + far_x + far_corners
    for copy in small + edge_y + far_y + edge_x:
        copy.start()
    for copy in small:
        copy.wait_recv()

    def inside(x, y):
        gx, gy = i * BX + x, j * BY + y
        ok = (gx >= 0) & (gx < nx * BX) & (gy >= 0) & (gy < ny * BY)
        return jnp.where(ok, 1.0, 0.0).astype(jnp.float32)

    def moduli(x, y, _):
        level = jnp.broadcast_to(lev[x, y], (8, NZ)).astype(jnp.float32)
        rho = 0.3 + 0.7 * level / (LEVELS - 1)
        e = rho * rho * rho * inside(x - 2, y - 2)
        for n, c in enumerate(SCALES):
            stiff[x, y, n] = e * float(c)
        stiffz[x, y] = (e + _shift(e, -1)) * DIAG
        return 0

    _loop2((0, BX + 4), (0, BY + 4), moduli, unroll=4)

    def nodal(x, y, _):
        fr = (1 - jnp.broadcast_to(sup[x, y], (8, NZ))).astype(jnp.float32) * inside(x - 1, y - 1)
        total = (stiffz[x, y] + stiffz[x + 1, y]) + (stiffz[x, y + 1] + stiffz[x + 1, y + 1])
        free[x, y] = fr
        inv[x, y] = 1.0 / (fr * total + (1.0 - fr))
        return 0

    _loop2((0, BX + 3), (0, BY + 3), nodal, unroll=3)

    def search(x, y, _):
        fr, iv = free[x, y], inv[x, y]
        for k in range(3):
            d = iv * (LOAD * fr * field[k, x, y])
            dire[k, x, y] = d
            s, t = _sum_diff(fr * d)
            masked[k, 0, x, y] = s
            masked[k, 1, x, y] = t
        return 0

    for copy in edge_y + far_y:
        copy.wait_recv()
    for copy in corners + far_corners + far_x:
        copy.start()
    _loop2((1, 1 + BX), (0, BY + 3), search, unroll=2)

    def u_at(k, pz, x, y, ct):
        return masked[k, pz, x + 1, y + 1, ct]

    def e_at(x, y, n):
        return stiff[x + 2, y + 2, n]

    def adder(ref, fresh, shift, planes):
        def add(k, pz, ex, x, y, ct, p0, p1):
            if x not in planes:
                return
            value = p0 - p1 if x == ex else p0 + p1
            if fresh(ex, x):
                ref[k, pz, x, y + shift, ct] = value
            else:
                ref[k, pz, x, y + shift, ct] += value
        return add

    at_nodes = range(BX + 1)
    add_near = adder(image, lambda ex, x: ex == 0 or x == BX, 1, at_nodes)
    _apply(u_at, e_at, add_near, range(0, 1), -1, BY + 1, True, unroll=3)
    for copy in edge_x + corners:
        copy.wait_recv()
    _loop2((0, 1), (0, BY + 2), search, unroll=2)
    _loop2((BX + 1, BX + 2), (0, BY + 2), search, unroll=2)
    _apply(u_at, e_at, add_near, (-1, BX - 1), -1, BY + 1, True, unroll=3)

    gap8 = jnp.zeros((8, NZ), jnp.float32)
    gap32 = jnp.zeros((32, NZ), jnp.bfloat16)

    def above(x, y):
        fr, iv = free[x + 1, y + 1], inv[x + 1, y + 1]
        nodes = []
        for k in range(3):
            d = dire[k, x + 1, y + 1]
            im = fr * _gather_z(image[k, 0, x, y + 1], image[k, 1, x, y + 1]) + (1.0 - fr) * d
            q = iv * im
            s, t = _sum_diff(fr * q)
            qm[k, 0, x, y] = s
            qm[k, 1, x, y] = t
            nodes.append((d, im, q))
        return nodes, fr

    def first_gram(x, y, acc):
        nodes, fr = above(x, y)
        left, right = [], []
        for k, (d, im, q) in enumerate(nodes):
            r0 = LOAD * fr * field[k, x + 1, y + 1]
            held = jnp.concatenate([_rows((1.0 - fr) * q), gap8], 0).astype(jnp.bfloat16)
            left.append(jnp.concatenate(_split(jnp.concatenate([_rows(d), _rows(q)], 0)), 0))
            high, low = _split(jnp.concatenate([_rows(im), _rows(r0)], 0))
            right.append(jnp.concatenate([high, held[:16], low, held[16:]], 0))
        return acc + _nt(jnp.concatenate(left, 1), jnp.concatenate(right, 1))

    acc = _loop2((0, BX), (0, BY), first_gram, jnp.zeros((96, NZ), jnp.float32), unroll=4)
    lane = lax.broadcasted_iota(jnp.int32, (CASES, NZ), 1)
    both = acc[:48] + acc[48:]
    held = both[24:]
    held = jnp.where(lane < 112, pltpu.roll(held, 48, axis=1), held)
    both = both + pltpu.roll(both, 64, axis=1)
    table = jnp.where(lane < 48, both[:24], jnp.where(lane < 96, pltpu.roll(both[24:], 48, axis=1), held))

    sent = []

    def begin(n, value, groups, source, target, send_sem, recv_sem):
        slot = sum(len(p) for p in groups[:n])
        source[n] = value
        group = [pltpu.make_async_remote_copy(
            source.at[n], target.at[slot + m], send_sem.at[slot + m], recv_sem.at[slot + m],
            device_id=(i ^ ox, j ^ oy), device_id_type=MESH) for m, (ox, oy) in enumerate(groups[n])]
        for copy in group:
            copy.start()
        sent.extend(group)
        return value, slot, group, target

    def begin1(n, value):
        return begin(n, value, phases, gram_send, gram_recv, g_send, g_recv)

    def begin2(n, value):
        return begin(n, value, phases2, last_send, last_recv, n_send, n_recv)

    def finish(going):
        value, slot, group, target = going
        for copy in group:
            copy.wait_recv()
        terms = [value] + [target[slot + m] for m in range(len(group))]
        while len(terms) > 1:
            terms = [terms[t] + terms[t + 1] for t in range(0, len(terms), 2)]
        return terms[0]

    todo = list(range(len(phases)))
    going = begin1(todo.pop(0), table)

    def pair(left, right, acc):
        a, b = [], []
        for u, v in zip(left, right):
            a.append(jnp.concatenate(_split(jnp.concatenate([_rows(u), gap8], 0)), 0))
            high, low = _split(jnp.concatenate([_rows(v), gap8], 0))
            b.append(jnp.concatenate([high, gap32, low, gap32], 0))
        return acc + _nt(jnp.concatenate(a, 1), jnp.concatenate(b, 1))

    for copy in far_x + far_corners:
        copy.wait_recv()
    _loop2((BX + 2, BX + 3), (0, BY + 3), search, unroll=2)
    _loop2((0, 1), (BY + 2, BY + 3), search)
    _loop2((BX + 1, BX + 2), (BY + 2, BY + 3), search)
    _apply(u_at, e_at, adder(image, lambda ex, x: False, 1, at_nodes), range(-1, BX), BY, 1, False)
    _apply(u_at, e_at, adder(image, lambda ex, x: False, 1, at_nodes), range(BX, BX + 1), -1, BY + 2, False, unroll=2)

    def edge(x, y, _):
        above(x, y)
        return 0

    _loop2((BX, BX + 1), (0, BY + 1), edge, unroll=3)
    _loop2((0, BX), (BY, BY + 1), edge)

    def q_at(k, pz, x, y, ct):
        return qm[k, pz, x, y, ct]

    _apply(q_at, e_at, adder(wf, lambda ex, x: x == ex + 1 or ex == 0, 0, at_nodes), range(BX), 0, BY, True, unroll=2)
    if todo:
        going = begin1(todo.pop(0), finish(going))

    def second_gram(x, y, acc):
        at = [(k, pz) for k in range(3) for pz in (0, 1)]
        return pair([qm[k, pz, x, y] for k, pz in at], [wf[k, pz, x, y] for k, pz in at], acc)

    acc2 = _loop2((0, BX + 1), (0, BY + 1), second_gram, jnp.zeros((64, NZ), jnp.float32), unroll=3)
    last = acc2[:24] + acc2[32:56]
    last = last + pltpu.roll(last, 64, axis=1)
    last = jnp.where(lane < 24, last, 0.0)
    last = last[:8] + pltpu.roll(last[8:16], 24, axis=1) + pltpu.roll(last[16:], 48, axis=1)
    n_going = begin2(0, last)
    while todo:
        going = begin1(todo.pop(0), finish(going))

    def prepare(x, y, _):
        for k in range(3):
            for pz in (0, 1):
                both = jnp.concatenate([_rows(masked[k, pz, x + 1, y + 1]), _rows(qm[k, pz, x, y])], 0)
                split[k, x, y, :, pz * NZ : pz * NZ + NZ] = jnp.concatenate(_split(both), 0)
        return 0

    _loop2((0, BX + 1), (0, BY + 1), prepare, unroll=3)

    n_todo = list(range(1, len(phases2)))
    if n_todo:
        n_going = begin2(n_todo.pop(0), finish(n_going))
    table = finish(going)
    tiles, scales = _eliminate(_system(table), jnp.zeros((8, NZ), jnp.float32), range(24))

    def block(p, t):
        return inside(BX * ((p - 2) // BX), BY * (t - 1))

    for p in range(BX + 4):
        for t in range(3):
            rim[p, BY * t : BY * t + BY] = jnp.zeros((BY, NZ), jnp.float32) + block(p, t)
    weights = _cone(rim)
    rho = [0.3 + 0.7 * lev[2 + x, 2 : 2 + BY, 0, :].astype(jnp.float32) / (LEVELS - 1) for x in range(BX)]

    last = finish(n_going)
    lane8 = lax.broadcasted_iota(jnp.int32, (8, NZ), 1)
    for t in range(3):
        rows = last if t == 1 else pltpu.roll(last, (24 * (1 - t)) % NZ, axis=1)
        tiles[3 + t] = tiles[3 + t] + jnp.where((lane8 >= 24) & (lane8 < 48), rows, 0.0)
    tiles, scales = _eliminate(tiles, scales, range(24, 48))
    half = jnp.concatenate([t * scales for t in tiles[6:]], 0)
    mix = half + pltpu.roll(half, 48, axis=1)
    mix = jnp.concatenate([mix, gap8], 0)
    high, low = _split(mix)
    coefs = jnp.concatenate([high, low], 0)[:, :96]

    def combine(x, y, _):
        for k in range(3):
            u = jnp.dot(coefs, split[k, x, y], preferred_element_type=jnp.float32)
            u = u[:24] + u[32:56]
            for pz in (0, 1):
                disp[k, pz, x, y] = u[:, pz * NZ : pz * NZ + NZ].reshape(CT, 8, NZ)
        return 0

    _loop2((0, BX + 1), (0, BY + 1), combine, unroll=9)

    def s_at(k, pz, x, y, ct):
        return disp[k, pz, x, y, ct]

    for x in range(BX):
        energy[x] = jnp.zeros((BY, 8, NZ), jnp.float32)

    def energies(ct, _):
        for x in range(BX):
            first = _stage(s_at, x, 0, ct)

            def step(y, state, x=x):
                s1 = _stage(s_at, x, y + 1, ct)
                energy[x, y] += _density_of_energy(_modes(dict(zip(KEYS, state)), s1))
                return tuple(s1[key] for key in KEYS)

            lax.fori_loop(0, BY, step, tuple(first[key] for key in KEYS), unroll=2)
        return 0

    lax.fori_loop(0, CT, energies, 0)

    for x in range(BX):
        sens = -3.0 * rho[x] * rho[x] * jnp.sum(energy[x], axis=1) / CASES
        vals[2 + x, BY : 2 * BY] = rho[x] * sens
    group = []
    for n, (dx, dy) in enumerate(NEIGHBOURS):
        at_x, at_y = 2 - BX * dx, BY - BY * dy
        group.append(pltpu.make_async_remote_copy(
            vals.at[2 : 2 + BX, BY : 2 * BY], vals.at[at_x : at_x + BX, at_y : at_y + BY], v_send.at[n], v_recv.at[n],
            device_id=there(dx, dy), device_id_type=MESH))
    for copy in group:
        copy.start()
    for copy in small + edge_y + edge_x + corners + set_b + sent:
        copy.wait_send()
    for copy in group:
        copy.wait_recv()
    for p in range(BX + 4):
        for t in range(3):
            rim[p, BY * t : BY * t + BY] = vals[p, BY * t : BY * t + BY] * block(p, t)
    sums = _cone(rim)
    for x in range(BX):
        out[x] = sums[x] / (rho[x] * weights[x])
    for copy in group:
        copy.wait_send()


def _phases(nx, ny):
    core, along_x = [(1, 0)], [(2, 0), (0, 1), (2, 1)]
    along_y = [(4 * o, 0) for o in range(1, nx // 4)]
    along_z = [(0, 2 * o) for o in range(1, ny // 2)]

    def product(fast, slow):
        return [(a ^ c, b ^ d) for c, d in [(0, 0)] + slow for a, b in [(0, 0)] + fast][1:]

    first = [product(core, along_x), along_y, along_z]
    second = [product(core, along_x), product(along_y, along_z)]
    return [g for g in first if g], [g for g in second if g]


def solution(mesh):
    nx, ny = mesh.shape["gx"], mesh.shape["gy"]
    phases, phases2 = _phases(nx, ny)
    slots, slots2 = (sum(len(g) for g in p) for p in (phases, phases2))
    f32 = jnp.float32
    dma = pltpu.SemaphoreType.DMA
    any_space = pl.BlockSpec(memory_space=pl.ANY)

    def local(forces, levels, supports):
        return pl.pallas_call(
            functools.partial(_kernel, nx, ny, phases, phases2),
            out_shape=jax.ShapeDtypeStruct((BX, BY, NZ), f32),
            in_specs=[any_space] * 3,
            out_specs=pl.BlockSpec(memory_space=pltpu.VMEM),
            scratch_shapes=[
                pltpu.VMEM((3 * CASES * BX * BY, NZ), f32),
                pltpu.VMEM((BX + 4, BY + 4, 1, NZ), jnp.int32),
                pltpu.VMEM((BX + 3, BY + 3, 1, NZ), jnp.int32),
                pltpu.VMEM((BX + 4, BY + 4, len(SCALES), 8, NZ), f32),
                pltpu.VMEM((BX + 4, BY + 4, 8, NZ), f32),
                pltpu.VMEM((BX + 3, BY + 3, 8, NZ), f32),
                pltpu.VMEM((BX + 3, BY + 3, 8, NZ), f32),
                pltpu.VMEM((3, BX + 3, BY + 3, CT, 8, NZ), f32),
                pltpu.VMEM((3, BX + 3, BY + 3, CT, 8, NZ), f32),
                pltpu.VMEM((3, 2, BX + 3, BY + 3, CT, 8, NZ), f32),
                pltpu.VMEM((3, 2, BX + 1, BY + 2, CT, 8, NZ), f32),
                pltpu.VMEM((3, 2, BX + 1, BY + 1, CT, 8, NZ), f32),
                pltpu.VMEM((3, 2, BX + 1, BY + 1, CT, 8, NZ), f32),
                pltpu.VMEM((3, BX + 1, BY + 1, 96, 2 * NZ), jnp.bfloat16),
                pltpu.VMEM((3, 2, BX + 1, BY + 1, CT, 8, NZ), f32),
                pltpu.VMEM((BX, BY, 8, NZ), f32),
                pltpu.VMEM((BX + 4, 3 * BY, NZ), f32),
                pltpu.VMEM((BX + 4, 3 * BY, NZ), f32),
                pltpu.VMEM((len(phases), CASES, NZ), f32),
                pltpu.VMEM((slots, CASES, NZ), f32),
                pltpu.VMEM((len(phases2), 8, NZ), f32),
                pltpu.VMEM((slots2, 8, NZ), f32),
                dma((3,)),
                dma((8,)), dma((8,)), dma((8,)), dma((8,)), dma((14,)), dma((14,)), dma((8,)), dma((8,)),
                dma((slots,)), dma((slots,)), dma((slots2,)), dma((slots2,)),
            ],
            compiler_params=pltpu.CompilerParams(collective_id=0, has_side_effects=True),
        )(
            forces.reshape(3 * CASES * BX * BY, NZ),
            levels.reshape(BX, BY, 1, NZ),
            supports.reshape(BX, BY, 1, NZ),
        )

    return jax.shard_map(
        local,
        mesh=mesh,
        in_specs=(P(None, None, "gx", "gy", None), P("gx", "gy", None), P("gx", "gy", None)),
        out_specs=P("gx", "gy", None),
        check_vma=False,
    )
```

```python
import functools
import math

import jax
import jax.numpy as jnp
import numpy as np
from jax import lax
from jax.experimental import pallas as pl
from jax.experimental.pallas import tpu as pltpu
from jax.sharding import PartitionSpec as P

MESH = pl.DeviceIdType.MESH
CASES = 24
LEVELS = 16
LOAD = 0.2
BX, BY, NZ = 2, 8, 128
CT = 3


def element_matrix():
    poisson = 0.3
    lame_first = poisson / ((1.0 + poisson) * (1.0 - 2.0 * poisson))
    lame_shear = 1.0 / (2.0 * (1.0 + poisson))
    elastic = np.zeros((6, 6))
    elastic[:3, :3] = lame_first
    for position in range(3):
        elastic[position, position] += 2.0 * lame_shear
        elastic[position + 3, position + 3] = lame_shear
    points = [0.5 - 0.5 / math.sqrt(3.0), 0.5 + 0.5 / math.sqrt(3.0)]
    matrix = np.zeros((24, 24))
    for point_x in points:
        for point_y in points:
            for point_z in points:
                coords = (point_x, point_y, point_z)
                strain = np.zeros((6, 24))
                for corner in range(8):
                    bits = (corner >> 2 & 1, corner >> 1 & 1, corner & 1)
                    shape = [coords[n] if bits[n] else 1.0 - coords[n] for n in range(3)]
                    slopes = [1.0 if bits[n] else -1.0 for n in range(3)]
                    slope_x = slopes[0] * shape[1] * shape[2]
                    slope_y = shape[0] * slopes[1] * shape[2]
                    slope_z = shape[0] * shape[1] * slopes[2]
                    o = 3 * corner
                    strain[0, o] = slope_x
                    strain[1, o + 1] = slope_y
                    strain[2, o + 2] = slope_z
                    strain[3, o] = slope_y
                    strain[3, o + 1] = slope_x
                    strain[4, o + 1] = slope_z
                    strain[4, o + 2] = slope_y
                    strain[5, o] = slope_z
                    strain[5, o + 2] = slope_x
                matrix = matrix + strain.T @ elastic @ strain / 8.0
    return matrix


KE = element_matrix()
DIAG = float(KE[0, 0])


def parity_matrix():
    walsh = np.ones((8, 8))
    for mode in range(8):
        for corner in range(8):
            for n in range(3):
                if mode >> n & 1:
                    walsh[mode, corner] *= 2 * (corner >> n & 1) - 1
    big = np.kron(walsh, np.eye(3))
    return big @ KE @ big.T / 64.0


KP = parity_matrix()
UNIT = ((1, 0, 0), (0, 1, 0), (0, 0, 1))


def _flip(p, k):
    return tuple(a ^ b for a, b in zip(p, UNIT[k]))


def _kp(m, n):
    at = [3 * (4 * p[0] + 2 * p[1] + p[2]) + k for k, p in (m, n)]
    return float(KP[at[0], at[1]])


NORMAL = [(k, UNIT[k]) for k in range(3)]
BEND = [(k, _flip((1, 1, 1), k)) for k in range(3)]
PAIRS = [[(k, _flip(UNIT[s], k)) for k in range(3) if k != s] for s in range(3)]
SHEAR = []
TWIST = []
for _s in range(3):
    _a, _b = [k for k in range(3) if k != _s]
    SHEAR.append([(_a, UNIT[_b]), (_b, UNIT[_a])])
    TWIST.append((_s, (1, 1, 1)))
N_OFF = _kp(NORMAL[0], NORMAL[1])
N_DIA = _kp(NORMAL[0], NORMAL[0]) - N_OFF
P_OFF = _kp(PAIRS[0][0], PAIRS[0][1])
P_DIA = _kp(PAIRS[0][0], PAIRS[0][0]) - P_OFF
S_ALL = _kp(SHEAR[0][0], SHEAR[0][0])
T_ALL = _kp(TWIST[0], TWIST[0])
B_OFF = _kp(BEND[0], BEND[1])
B_DIA = _kp(BEND[0], BEND[0]) - B_OFF


def _span(d, low, high, size):
    a = max(0, low + d * size)
    b = min(size, high + 1 + d * size)
    return a, a - d * size, b - a


NEIGHBOURS = [(dx, dy) for dx in (-1, 0, 1) for dy in (-1, 0, 1) if dx or dy]


def _shift(x, by):
    lane = lax.broadcasted_iota(jnp.int32, x.shape, x.ndim - 1)
    r = pltpu.roll(x, (-by) % NZ, axis=x.ndim - 1)
    ok = lane < NZ - by if by > 0 else lane >= -by
    return jnp.where(ok, r, 0.0)


def _stage(u_at, ex, y, ct):
    out = {}
    for k in range(3):
        for pz in (0, 1):
            u0, u1 = u_at(k, pz, ex, y, ct), u_at(k, pz, ex + 1, y, ct)
            out[k, 0, pz] = u0 + u1
            out[k, 1, pz] = u1 - u0
    return out


KEYS = [(k, px, pz) for k in range(3) for px in (0, 1) for pz in (0, 1)]


def _modes(s0, s1):
    out = {}
    for k, px, pz in KEYS:
        if (px, pz) != (0, 0):
            out[k, (px, 0, pz)] = s0[k, px, pz] + s1[k, px, pz]
        out[k, (px, 1, pz)] = s1[k, px, pz] - s0[k, px, pz]
    return out


SCALES = sorted({np.float32(c) for c in (N_OFF, N_DIA, P_OFF, P_DIA, S_ALL, T_ALL, B_OFF, B_DIA)})


def _stress(u, e_at):
    def e(c):
        return e_at(SCALES.index(np.float32(c)))

    g = {}
    for group, off, dia in ((NORMAL, N_OFF, N_DIA), (BEND, B_OFF, B_DIA)):
        total = (u[group[0]] + u[group[1]] + u[group[2]]) * e(off)
        for m in group:
            g[m] = u[m] * e(dia) + total
    for a, b in PAIRS:
        total = (u[a] + u[b]) * e(P_OFF)
        g[a] = u[a] * e(P_DIA) + total
        g[b] = u[b] * e(P_DIA) + total
    for a, b in SHEAR:
        g[a] = g[b] = (u[a] + u[b]) * e(S_ALL)
    for m in TWIST:
        g[m] = u[m] * e(T_ALL)
    return g


def _density_of_energy(u):
    def sq(x):
        return x * x

    e = N_OFF * sq(u[NORMAL[0]] + u[NORMAL[1]] + u[NORMAL[2]])
    e = e + N_DIA * (sq(u[NORMAL[0]]) + sq(u[NORMAL[1]]) + sq(u[NORMAL[2]]))
    e = e + B_OFF * sq(u[BEND[0]] + u[BEND[1]] + u[BEND[2]])
    e = e + B_DIA * (sq(u[BEND[0]]) + sq(u[BEND[1]]) + sq(u[BEND[2]]))
    off = dia = she = twi = 0.0
    for a, b in PAIRS:
        off = off + sq(u[a] + u[b])
        dia = dia + sq(u[a]) + sq(u[b])
    for a, b in SHEAR:
        she = she + sq(u[a] + u[b])
    for m in TWIST:
        twi = twi + sq(u[m])
    return e + P_OFF * off + P_DIA * dia + S_ALL * she + T_ALL * twi


def _apply(u_at, e_at, add, layers, y_low, columns, close, unroll=2):
    def tile(ct, _):
        for ex in layers:
            first = _stage(u_at, ex, y_low, ct)
            zero = jnp.zeros((8, NZ), jnp.float32)

            def emit(y, h, ex=ex):
                for k in range(3):
                    for pz in (0, 1):
                        p0, p1 = h[k, 0, pz], h[k, 1, pz]
                        add(k, pz, ex, ex, y, ct, p0, p1)
                        add(k, pz, ex, ex + 1, y, ct, p0, p1)

            def step(t, state, ex=ex):
                s0 = dict(zip(KEYS, state[0]))
                carry = dict(zip(KEYS, state[1]))
                y = y_low + t
                s1 = _stage(u_at, ex, y + 1, ct)
                g = _stress(_modes(s0, s1), functools.partial(e_at, ex, y))
                h, later = {}, {}
                for key in KEYS:
                    k, px, pz = key
                    g1 = g[k, (px, 1, pz)]
                    g0 = g.get((k, (px, 0, pz)))
                    if g0 is None:
                        h[key] = carry[key] - g1
                        later[key] = g1
                    else:
                        h[key] = carry[key] + (g0 - g1)
                        later[key] = g0 + g1
                emit(y, h)
                return tuple(s1[key] for key in KEYS), tuple(later[key] for key in KEYS)

            state = (tuple(first[key] for key in KEYS), (zero,) * len(KEYS))
            if columns == 1:
                state = step(0, state)
            else:
                state = lax.fori_loop(0, columns, step, state, unroll=unroll)
            if close:
                emit(y_low + columns, dict(zip(KEYS, state[1])))
        return 0

    lax.fori_loop(0, CT, tile, 0)


def _sum_diff(u):
    up = _shift(u, 1)
    return u + up, up - u


def _gather_z(s, d):
    return (s - d) + _shift(s + d, -1)


def _loop2(xs, ys, body, state=0, unroll=1):
    def outer(x, state):
        return lax.fori_loop(ys[0], ys[1], lambda y, st: body(x, y, st), state, unroll=unroll)

    return lax.fori_loop(xs[0], xs[1], outer, state)


def _split(x):
    scaled = x * 65537.0
    high = scaled - (scaled - x)
    return high.astype(jnp.bfloat16), (x - high).astype(jnp.bfloat16)


def _rows(x):
    return x.reshape(CASES, NZ)


def _nt(a, b):
    return lax.dot_general(a, b, (((1,), (1,)), ((), ())), preferred_element_type=jnp.float32)


def _system(table):
    lane = lax.broadcasted_iota(jnp.int32, (CASES, NZ), 1)

    def left(x, by):
        return pltpu.roll(x, (-by) % NZ, axis=1)

    def join(a, b):
        return jnp.where(lane < 24, a, jnp.where(lane < 48, b, 0.0))

    blocks = [
        join(table, left(table, 24)),
        join(left(table, 48), left(table, 72)),
        join(left(table, 24), left(table, 48)),
    ]
    return [b[8 * i : 8 * i + 8] for b in blocks for i in range(3)]


def _eliminate(tiles, scales, steps, width=4):
    lane = lax.broadcasted_iota(jnp.int32, (8, NZ), 1)

    def one_row(x, r):
        return jnp.broadcast_to(x[r : r + 1], (8, NZ))

    for first in range(steps.start, steps.stop, width):
        own, at = first // 8, first % 8
        live = range(own, 9)
        cols = [{t: jnp.broadcast_to(tiles[t][:, first + m : first + m + 1], (8, NZ)) for t in live} for m in range(width)]
        rows = [one_row(tiles[own], at + m) for m in range(width)]
        factors = []
        for m in range(width):
            scale = 1.0 / one_row(cols[m][own], at + m)
            factor = jnp.where(lane == first + m, 0.0, rows[m] * scale)
            scales = jnp.where(lane == first + m, scale, scales)
            factors.append(factor)
            for later in range(m + 1, width):
                share = one_row(cols[later][own], at + m) * scale
                rows[later] = rows[later] - one_row(cols[m][own], at + later) * factor
                for t in live:
                    cols[later][t] = cols[later][t] - cols[m][t] * share
        for t in live:
            for m in range(width):
                tiles[t] = tiles[t] - cols[m][t] * factors[m]
    return tiles, scales


def _weight(dx, dy, dz):
    return max(0.0, 2.5 - math.sqrt(dx * dx + dy * dy + dz * dz))


def _cone(planes):
    by_row = {}
    for p in range(BX + 4):
        by_row[p, 0] = planes[p, BY : 2 * BY]
        for dy in (1, 2):
            by_row[p, dy] = planes[p, BY + dy : 2 * BY + dy] + planes[p, BY - dy : 2 * BY - dy]
    result = []
    for xo in range(BX):
        total = None
        for dz in range(3):
            part = jnp.zeros((BY, NZ), jnp.float32)
            for dx in range(-2, 3):
                for dy in range(3):
                    w = _weight(dx, dy, dz)
                    if w > 0.0:
                        part = part + w * by_row[xo + 2 + dx, dy]
            total = part if dz == 0 else total + (_shift(part, dz) + _shift(part, -dz))
        result.append(total)
    return result


SET_A = [(dx, dy, _span(dx, -1, 2, BX), _span(dy, -1, 8, BY)) for dx, dy in NEIGHBOURS]
SET_B = [
    (-1, 0, (1, 3, 1), (0, 0, BY)),
    (0, -1, (0, 0, BX), (1, 9, 1)),
    (-1, 1, (1, 3, 1), (7, -1, 1)),
    (-1, -1, (1, 3, 1), (0, 8, 2)),
    (-1, -1, (0, 2, 1), (1, 9, 1)),
    (1, -1, (1, -1, 1), (1, 9, 1)),
]


def _kernel(nx, ny, phases, phases2, forces, levels, supports, out, nat, lev, sup, stiff, stiffz, inv, free, field, dire, masked,
            image, qm, wf, split, disp, energy, vals, rim, gram_send, gram_recv, last_send, last_recv, local_sem, l_send, l_recv, s_send,
            s_recv, f_send, f_recv, v_send, v_recv, g_send, g_recv, n_send, n_recv):
    i, j = lax.axis_index("gx"), lax.axis_index("gy")

    def there(dx, dy):
        return lax.rem(i + dx + nx, nx), lax.rem(j + dy + ny, ny)

    peers = [there(dx, dy) for dx, dy in NEIGHBOURS]
    for phase in phases:
        for ox, oy in phase:
            peers.append((i ^ ox, j ^ oy))

    c_nat = pltpu.make_async_copy(forces, nat, local_sem.at[0])
    c_lev = pltpu.make_async_copy(levels, lev.at[2 : 2 + BX, 2 : 2 + BY], local_sem.at[1])
    c_sup = pltpu.make_async_copy(supports, sup.at[1 : 1 + BX, 1 : 1 + BY], local_sem.at[2])
    c_nat.start()
    c_lev.start()
    c_sup.start()

    barrier = pltpu.get_barrier_semaphore()
    for peer in peers:
        pl.semaphore_signal(barrier, inc=1, device_id=peer, device_id_type=MESH)

    c_nat.wait()

    def arrange(k, _):
        for x in range(BX):
            for y in range(BY):
                rows = nat[pl.ds(k * (CASES * BX * BY) + x * BY + y, CASES, stride=BX * BY), :]
                field[k, 1 + x, 1 + y] = rows.reshape(CT, 8, NZ)
        return 0

    lax.fori_loop(0, 3, arrange, 0)
    c_lev.wait()
    c_sup.wait()

    pl.semaphore_wait(barrier, len(peers))

    small = []
    for n, (dx, dy) in enumerate(NEIGHBOURS):
        (a, b, c), (d, e, f) = _span(dx, -2, 3, BX), _span(dy, -2, 9, BY)
        small.append(pltpu.make_async_remote_copy(
            levels.at[a : a + c, d : d + f], lev.at[b + 2 : b + 2 + c, e + 2 : e + 2 + f],
            l_send.at[n], l_recv.at[n], device_id=there(dx, dy), device_id_type=MESH))
        (a, b, c), (d, e, f) = _span(dx, -1, 3, BX), _span(dy, -1, 9, BY)
        small.append(pltpu.make_async_remote_copy(
            supports.at[a : a + c, d : d + f], sup.at[b + 1 : b + 1 + c, e + 1 : e + 1 + f],
            s_send.at[n], s_recv.at[n], device_id=there(dx, dy), device_id_type=MESH))

    halo = []
    for n, (dx, dy, (a, b, c), (d, e, f)) in enumerate(SET_A + SET_B):
        halo.append(pltpu.make_async_remote_copy(
            field.at[:, a + 1 : a + 1 + c, d + 1 : d + 1 + f], field.at[:, b + 1 : b + 1 + c, e + 1 : e + 1 + f],
            f_send.at[n], f_recv.at[n], device_id=there(dx, dy), device_id_type=MESH))
    near, far = halo[: len(SET_A)], halo[len(SET_A) :]
    edge_y = [copy for copy, (dx, _, _, _) in zip(near, SET_A) if dx == 0]
    edge_x = [copy for copy, (dx, _, _, _) in zip(near, SET_A) if dx != 0]
    for copy in small + near + far:
        copy.start()
    for copy in small:
        copy.wait_recv()

    def inside(x, y):
        gx, gy = i * BX + x, j * BY + y
        ok = (gx >= 0) & (gx < nx * BX) & (gy >= 0) & (gy < ny * BY)
        return jnp.where(ok, 1.0, 0.0).astype(jnp.float32)

    def moduli(x, y, _):
        level = jnp.broadcast_to(lev[x, y], (8, NZ)).astype(jnp.float32)
        rho = 0.3 + 0.7 * level / (LEVELS - 1)
        e = rho * rho * rho * inside(x - 2, y - 2)
        for n, c in enumerate(SCALES):
            stiff[x, y, n] = e * float(c)
        stiffz[x, y] = (e + _shift(e, -1)) * DIAG
        return 0

    _loop2((0, BX + 4), (0, BY + 4), moduli, unroll=4)

    def nodal(x, y, _):
        fr = (1 - jnp.broadcast_to(sup[x, y], (8, NZ))).astype(jnp.float32) * inside(x - 1, y - 1)
        total = (stiffz[x, y] + stiffz[x + 1, y]) + (stiffz[x, y + 1] + stiffz[x + 1, y + 1])
        free[x, y] = fr
        inv[x, y] = 1.0 / (fr * total + (1.0 - fr))
        return 0

    _loop2((0, BX + 3), (0, BY + 3), nodal, unroll=3)

    def search(x, y, _):
        fr, iv = free[x, y], inv[x, y]
        for k in range(3):
            d = iv * (LOAD * fr * field[k, x, y])
            dire[k, x, y] = d
            s, t = _sum_diff(fr * d)
            masked[k, 0, x, y] = s
            masked[k, 1, x, y] = t
        return 0

    for copy in edge_y:
        copy.wait_recv()
    _loop2((1, 1 + BX), (0, BY + 2), search, unroll=2)

    def u_at(k, pz, x, y, ct):
        return masked[k, pz, x + 1, y + 1, ct]

    def e_at(x, y, n):
        return stiff[x + 2, y + 2, n]

    def adder(ref, fresh, shift, planes):
        def add(k, pz, ex, x, y, ct, p0, p1):
            if x not in planes:
                return
            value = p0 - p1 if x == ex else p0 + p1
            if fresh(ex, x):
                ref[k, pz, x, y + shift, ct] = value
            else:
                ref[k, pz, x, y + shift, ct] += value
        return add

    at_nodes = range(BX + 1)
    add_near = adder(image, lambda ex, x: ex == 0 or x == BX, 1, at_nodes)
    _apply(u_at, e_at, add_near, range(0, 1), -1, BY + 1, True, unroll=3)
    for copy in edge_x:
        copy.wait_recv()
    _loop2((0, 1), (0, BY + 2), search, unroll=2)
    _loop2((BX + 1, BX + 2), (0, BY + 2), search, unroll=2)
    _apply(u_at, e_at, add_near, (-1, BX - 1), -1, BY + 1, True, unroll=3)

    gap8 = jnp.zeros((8, NZ), jnp.float32)
    gap32 = jnp.zeros((32, NZ), jnp.bfloat16)

    def above(x, y):
        fr, iv = free[x + 1, y + 1], inv[x + 1, y + 1]
        nodes = []
        for k in range(3):
            d = dire[k, x + 1, y + 1]
            im = fr * _gather_z(image[k, 0, x, y + 1], image[k, 1, x, y + 1]) + (1.0 - fr) * d
            q = iv * im
            s, t = _sum_diff(fr * q)
            qm[k, 0, x, y] = s
            qm[k, 1, x, y] = t
            nodes.append((d, im, q))
        return nodes, fr

    def first_gram(x, y, acc):
        nodes, fr = above(x, y)
        left, right = [], []
        for k, (d, im, q) in enumerate(nodes):
            r0 = LOAD * fr * field[k, x + 1, y + 1]
            held = jnp.concatenate([_rows((1.0 - fr) * q), gap8], 0).astype(jnp.bfloat16)
            left.append(jnp.concatenate(_split(jnp.concatenate([_rows(d), _rows(q)], 0)), 0))
            high, low = _split(jnp.concatenate([_rows(im), _rows(r0)], 0))
            right.append(jnp.concatenate([high, held[:16], low, held[16:]], 0))
        return acc + _nt(jnp.concatenate(left, 1), jnp.concatenate(right, 1))

    acc = _loop2((0, BX), (0, BY), first_gram, jnp.zeros((96, NZ), jnp.float32), unroll=4)
    lane = lax.broadcasted_iota(jnp.int32, (CASES, NZ), 1)
    both = acc[:48] + acc[48:]
    held = both[24:]
    held = jnp.where(lane < 112, pltpu.roll(held, 48, axis=1), held)
    both = both + pltpu.roll(both, 64, axis=1)
    table = jnp.where(lane < 48, both[:24], jnp.where(lane < 96, pltpu.roll(both[24:], 48, axis=1), held))

    sent = []

    def begin(n, value, groups, source, target, send_sem, recv_sem):
        slot = sum(len(p) for p in groups[:n])
        source[n] = value
        group = [pltpu.make_async_remote_copy(
            source.at[n], target.at[slot + m], send_sem.at[slot + m], recv_sem.at[slot + m],
            device_id=(i ^ ox, j ^ oy), device_id_type=MESH) for m, (ox, oy) in enumerate(groups[n])]
        for copy in group:
            copy.start()
        sent.extend(group)
        return value, slot, group, target

    def begin1(n, value):
        return begin(n, value, phases, gram_send, gram_recv, g_send, g_recv)

    def begin2(n, value):
        return begin(n, value, phases2, last_send, last_recv, n_send, n_recv)

    def finish(going):
        value, slot, group, target = going
        for copy in group:
            copy.wait_recv()
        terms = [value] + [target[slot + m] for m in range(len(group))]
        while len(terms) > 1:
            terms = [terms[t] + terms[t + 1] for t in range(0, len(terms), 2)]
        return terms[0]

    todo = list(range(len(phases)))
    going = begin1(todo.pop(0), table)

    def pair(left, right, acc):
        a, b = [], []
        for u, v in zip(left, right):
            a.append(jnp.concatenate(_split(jnp.concatenate([_rows(u), gap8], 0)), 0))
            high, low = _split(jnp.concatenate([_rows(v), gap8], 0))
            b.append(jnp.concatenate([high, gap32, low, gap32], 0))
        return acc + _nt(jnp.concatenate(a, 1), jnp.concatenate(b, 1))

    for copy in far:
        copy.wait_recv()
    _loop2((BX + 2, BX + 3), (0, BY + 3), search, unroll=2)
    _loop2((0, BX + 2), (BY + 2, BY + 3), search)
    _apply(u_at, e_at, adder(image, lambda ex, x: False, 1, at_nodes), range(-1, BX), BY, 1, False)
    _apply(u_at, e_at, adder(image, lambda ex, x: False, 1, at_nodes), range(BX, BX + 1), -1, BY + 2, False, unroll=2)

    def edge(x, y, _):
        above(x, y)
        return 0

    _loop2((BX, BX + 1), (0, BY + 1), edge, unroll=3)
    _loop2((0, BX), (BY, BY + 1), edge)

    def q_at(k, pz, x, y, ct):
        return qm[k, pz, x, y, ct]

    _apply(q_at, e_at, adder(wf, lambda ex, x: x == ex + 1 or ex == 0, 0, at_nodes), range(BX), 0, BY, True, unroll=2)
    if todo:
        going = begin1(todo.pop(0), finish(going))

    def second_gram(x, y, acc):
        at = [(k, pz) for k in range(3) for pz in (0, 1)]
        return pair([qm[k, pz, x, y] for k, pz in at], [wf[k, pz, x, y] for k, pz in at], acc)

    acc2 = _loop2((0, BX + 1), (0, BY + 1), second_gram, jnp.zeros((64, NZ), jnp.float32), unroll=3)
    last = acc2[:24] + acc2[32:56]
    last = last + pltpu.roll(last, 64, axis=1)
    last = jnp.where(lane < 24, last, 0.0)
    last = last[:8] + pltpu.roll(last[8:16], 24, axis=1) + pltpu.roll(last[16:], 48, axis=1)
    n_going = begin2(0, last)
    while todo:
        going = begin1(todo.pop(0), finish(going))

    def prepare(x, y, _):
        for k in range(3):
            for pz in (0, 1):
                both = jnp.concatenate([_rows(masked[k, pz, x + 1, y + 1]), _rows(qm[k, pz, x, y])], 0)
                split[k, x, y, :, pz * NZ : pz * NZ + NZ] = jnp.concatenate(_split(both), 0)
        return 0

    _loop2((0, BX + 1), (0, BY + 1), prepare, unroll=3)

    n_todo = list(range(1, len(phases2)))
    if n_todo:
        n_going = begin2(n_todo.pop(0), finish(n_going))
    table = finish(going)
    tiles, scales = _eliminate(_system(table), jnp.zeros((8, NZ), jnp.float32), range(24))

    def block(p, t):
        return inside(BX * ((p - 2) // BX), BY * (t - 1))

    for p in range(BX + 4):
        for t in range(3):
            rim[p, BY * t : BY * t + BY] = jnp.zeros((BY, NZ), jnp.float32) + block(p, t)
    weights = _cone(rim)
    rho = [0.3 + 0.7 * lev[2 + x, 2 : 2 + BY, 0, :].astype(jnp.float32) / (LEVELS - 1) for x in range(BX)]

    last = finish(n_going)
    lane8 = lax.broadcasted_iota(jnp.int32, (8, NZ), 1)
    for t in range(3):
        rows = last if t == 1 else pltpu.roll(last, (24 * (1 - t)) % NZ, axis=1)
        tiles[3 + t] = tiles[3 + t] + jnp.where((lane8 >= 24) & (lane8 < 48), rows, 0.0)
    tiles, scales = _eliminate(tiles, scales, range(24, 48))
    half = jnp.concatenate([t * scales for t in tiles[6:]], 0)
    mix = half + pltpu.roll(half, 48, axis=1)
    mix = jnp.concatenate([mix, gap8], 0)
    high, low = _split(mix)
    coefs = jnp.concatenate([high, low], 0)[:, :96]

    def combine(x, y, _):
        for k in range(3):
            u = jnp.dot(coefs, split[k, x, y], preferred_element_type=jnp.float32)
            u = u[:24] + u[32:56]
            for pz in (0, 1):
                disp[k, pz, x, y] = u[:, pz * NZ : pz * NZ + NZ].reshape(CT, 8, NZ)
        return 0

    _loop2((0, BX + 1), (0, BY + 1), combine, unroll=9)

    def s_at(k, pz, x, y, ct):
        return disp[k, pz, x, y, ct]

    for x in range(BX):
        energy[x] = jnp.zeros((BY, 8, NZ), jnp.float32)

    def energies(ct, _):
        for x in range(BX):
            first = _stage(s_at, x, 0, ct)

            def step(y, state, x=x):
                s1 = _stage(s_at, x, y + 1, ct)
                energy[x, y] += _density_of_energy(_modes(dict(zip(KEYS, state)), s1))
                return tuple(s1[key] for key in KEYS)

            lax.fori_loop(0, BY, step, tuple(first[key] for key in KEYS), unroll=2)
        return 0

    lax.fori_loop(0, CT, energies, 0)

    for x in range(BX):
        sens = -3.0 * rho[x] * rho[x] * jnp.sum(energy[x], axis=1) / CASES
        vals[2 + x, BY : 2 * BY] = rho[x] * sens
    group = []
    for n, (dx, dy) in enumerate(NEIGHBOURS):
        at_x, at_y = 2 - BX * dx, BY - BY * dy
        group.append(pltpu.make_async_remote_copy(
            vals.at[2 : 2 + BX, BY : 2 * BY], vals.at[at_x : at_x + BX, at_y : at_y + BY], v_send.at[n], v_recv.at[n],
            device_id=there(dx, dy), device_id_type=MESH))
    for copy in group:
        copy.start()
    for copy in small + near + far + sent:
        copy.wait_send()
    for copy in group:
        copy.wait_recv()
    for p in range(BX + 4):
        for t in range(3):
            rim[p, BY * t : BY * t + BY] = vals[p, BY * t : BY * t + BY] * block(p, t)
    sums = _cone(rim)
    for x in range(BX):
        out[x] = sums[x] / (rho[x] * weights[x])
    for copy in group:
        copy.wait_send()


def _phases(nx, ny):
    core, along_x = [(1, 0)], [(2, 0), (0, 1), (2, 1)]
    along_y = [(4 * o, 0) for o in range(1, nx // 4)]
    along_z = [(0, 2 * o) for o in range(1, ny // 2)]

    def product(fast, slow):
        return [(a ^ c, b ^ d) for c, d in [(0, 0)] + slow for a, b in [(0, 0)] + fast][1:]

    first = [product(core, along_x), along_y, along_z]
    second = [product(core, along_x), product(along_y, along_z)]
    return [g for g in first if g], [g for g in second if g]


def solution(mesh):
    nx, ny = mesh.shape["gx"], mesh.shape["gy"]
    phases, phases2 = _phases(nx, ny)
    slots, slots2 = (sum(len(g) for g in p) for p in (phases, phases2))
    f32 = jnp.float32
    dma = pltpu.SemaphoreType.DMA
    any_space = pl.BlockSpec(memory_space=pl.ANY)

    def local(forces, levels, supports):
        return pl.pallas_call(
            functools.partial(_kernel, nx, ny, phases, phases2),
            out_shape=jax.ShapeDtypeStruct((BX, BY, NZ), f32),
            in_specs=[any_space] * 3,
            out_specs=pl.BlockSpec(memory_space=pltpu.VMEM),
            scratch_shapes=[
                pltpu.VMEM((3 * CASES * BX * BY, NZ), f32),
                pltpu.VMEM((BX + 4, BY + 4, 1, NZ), jnp.int32),
                pltpu.VMEM((BX + 3, BY + 3, 1, NZ), jnp.int32),
                pltpu.VMEM((BX + 4, BY + 4, len(SCALES), 8, NZ), f32),
                pltpu.VMEM((BX + 4, BY + 4, 8, NZ), f32),
                pltpu.VMEM((BX + 3, BY + 3, 8, NZ), f32),
                pltpu.VMEM((BX + 3, BY + 3, 8, NZ), f32),
                pltpu.VMEM((3, BX + 3, BY + 3, CT, 8, NZ), f32),
                pltpu.VMEM((3, BX + 3, BY + 3, CT, 8, NZ), f32),
                pltpu.VMEM((3, 2, BX + 3, BY + 3, CT, 8, NZ), f32),
                pltpu.VMEM((3, 2, BX + 1, BY + 2, CT, 8, NZ), f32),
                pltpu.VMEM((3, 2, BX + 1, BY + 1, CT, 8, NZ), f32),
                pltpu.VMEM((3, 2, BX + 1, BY + 1, CT, 8, NZ), f32),
                pltpu.VMEM((3, BX + 1, BY + 1, 96, 2 * NZ), jnp.bfloat16),
                pltpu.VMEM((3, 2, BX + 1, BY + 1, CT, 8, NZ), f32),
                pltpu.VMEM((BX, BY, 8, NZ), f32),
                pltpu.VMEM((BX + 4, 3 * BY, NZ), f32),
                pltpu.VMEM((BX + 4, 3 * BY, NZ), f32),
                pltpu.VMEM((len(phases), CASES, NZ), f32),
                pltpu.VMEM((slots, CASES, NZ), f32),
                pltpu.VMEM((len(phases2), 8, NZ), f32),
                pltpu.VMEM((slots2, 8, NZ), f32),
                dma((3,)),
                dma((8,)), dma((8,)), dma((8,)), dma((8,)), dma((14,)), dma((14,)), dma((8,)), dma((8,)),
                dma((slots,)), dma((slots,)), dma((slots2,)), dma((slots2,)),
            ],
            compiler_params=pltpu.CompilerParams(collective_id=0, has_side_effects=True),
        )(
            forces.reshape(3 * CASES * BX * BY, NZ),
            levels.reshape(BX, BY, 1, NZ),
            supports.reshape(BX, BY, 1, NZ),
        )

    return jax.shard_map(
        local,
        mesh=mesh,
        in_specs=(P(None, None, "gx", "gy", None), P("gx", "gy", None), P("gx", "gy", None)),
        out_specs=P("gx", "gy", None),
        check_vma=False,
    )
```

```python
import functools
import math

import jax
import jax.numpy as jnp
import numpy as np
from jax import lax
from jax.experimental import pallas as pl
from jax.experimental.pallas import tpu as pltpu
from jax.sharding import PartitionSpec as P

MESH = pl.DeviceIdType.MESH
CASES = 24
LEVELS = 16
LOAD = 0.2
BX, BY, NZ = 2, 8, 128
CT = 3


def element_matrix():
    poisson = 0.3
    lame_first = poisson / ((1.0 + poisson) * (1.0 - 2.0 * poisson))
    lame_shear = 1.0 / (2.0 * (1.0 + poisson))
    elastic = np.zeros((6, 6))
    elastic[:3, :3] = lame_first
    for position in range(3):
        elastic[position, position] += 2.0 * lame_shear
        elastic[position + 3, position + 3] = lame_shear
    points = [0.5 - 0.5 / math.sqrt(3.0), 0.5 + 0.5 / math.sqrt(3.0)]
    matrix = np.zeros((24, 24))
    for point_x in points:
        for point_y in points:
            for point_z in points:
                coords = (point_x, point_y, point_z)
                strain = np.zeros((6, 24))
                for corner in range(8):
                    bits = (corner >> 2 & 1, corner >> 1 & 1, corner & 1)
                    shape = [coords[n] if bits[n] else 1.0 - coords[n] for n in range(3)]
                    slopes = [1.0 if bits[n] else -1.0 for n in range(3)]
                    slope_x = slopes[0] * shape[1] * shape[2]
                    slope_y = shape[0] * slopes[1] * shape[2]
                    slope_z = shape[0] * shape[1] * slopes[2]
                    o = 3 * corner
                    strain[0, o] = slope_x
                    strain[1, o + 1] = slope_y
                    strain[2, o + 2] = slope_z
                    strain[3, o] = slope_y
                    strain[3, o + 1] = slope_x
                    strain[4, o + 1] = slope_z
                    strain[4, o + 2] = slope_y
                    strain[5, o] = slope_z
                    strain[5, o + 2] = slope_x
                matrix = matrix + strain.T @ elastic @ strain / 8.0
    return matrix


KE = element_matrix()
DIAG = float(KE[0, 0])


def parity_matrix():
    walsh = np.ones((8, 8))
    for mode in range(8):
        for corner in range(8):
            for n in range(3):
                if mode >> n & 1:
                    walsh[mode, corner] *= 2 * (corner >> n & 1) - 1
    big = np.kron(walsh, np.eye(3))
    return big @ KE @ big.T / 64.0


KP = parity_matrix()
UNIT = ((1, 0, 0), (0, 1, 0), (0, 0, 1))


def _flip(p, k):
    return tuple(a ^ b for a, b in zip(p, UNIT[k]))


def _kp(m, n):
    at = [3 * (4 * p[0] + 2 * p[1] + p[2]) + k for k, p in (m, n)]
    return float(KP[at[0], at[1]])


NORMAL = [(k, UNIT[k]) for k in range(3)]
BEND = [(k, _flip((1, 1, 1), k)) for k in range(3)]
PAIRS = [[(k, _flip(UNIT[s], k)) for k in range(3) if k != s] for s in range(3)]
SHEAR = []
TWIST = []
for _s in range(3):
    _a, _b = [k for k in range(3) if k != _s]
    SHEAR.append([(_a, UNIT[_b]), (_b, UNIT[_a])])
    TWIST.append((_s, (1, 1, 1)))
N_OFF = _kp(NORMAL[0], NORMAL[1])
N_DIA = _kp(NORMAL[0], NORMAL[0]) - N_OFF
P_OFF = _kp(PAIRS[0][0], PAIRS[0][1])
P_DIA = _kp(PAIRS[0][0], PAIRS[0][0]) - P_OFF
S_ALL = _kp(SHEAR[0][0], SHEAR[0][0])
T_ALL = _kp(TWIST[0], TWIST[0])
B_OFF = _kp(BEND[0], BEND[1])
B_DIA = _kp(BEND[0], BEND[0]) - B_OFF


def _span(d, low, high, size):
    a = max(0, low + d * size)
    b = min(size, high + 1 + d * size)
    return a, a - d * size, b - a


NEIGHBOURS = [(dx, dy) for dx in (-1, 0, 1) for dy in (-1, 0, 1) if dx or dy]


def _shift(x, by):
    lane = lax.broadcasted_iota(jnp.int32, x.shape, x.ndim - 1)
    r = pltpu.roll(x, (-by) % NZ, axis=x.ndim - 1)
    ok = lane < NZ - by if by > 0 else lane >= -by
    return jnp.where(ok, r, 0.0)


def _stage(u_at, ex, y, ct):
    out = {}
    for k in range(3):
        for pz in (0, 1):
            u0, u1 = u_at(k, pz, ex, y, ct), u_at(k, pz, ex + 1, y, ct)
            out[k, 0, pz] = u0 + u1
            out[k, 1, pz] = u1 - u0
    return out


KEYS = [(k, px, pz) for k in range(3) for px in (0, 1) for pz in (0, 1)]


def _modes(s0, s1):
    out = {}
    for k, px, pz in KEYS:
        if (px, pz) != (0, 0):
            out[k, (px, 0, pz)] = s0[k, px, pz] + s1[k, px, pz]
        out[k, (px, 1, pz)] = s1[k, px, pz] - s0[k, px, pz]
    return out


SCALES = sorted({np.float32(c) for c in (N_OFF, N_DIA, P_OFF, P_DIA, S_ALL, T_ALL, B_OFF, B_DIA)})


def _stress(u, e_at):
    def e(c):
        return e_at(SCALES.index(np.float32(c)))

    g = {}
    for group, off, dia in ((NORMAL, N_OFF, N_DIA), (BEND, B_OFF, B_DIA)):
        total = (u[group[0]] + u[group[1]] + u[group[2]]) * e(off)
        for m in group:
            g[m] = u[m] * e(dia) + total
    for a, b in PAIRS:
        total = (u[a] + u[b]) * e(P_OFF)
        g[a] = u[a] * e(P_DIA) + total
        g[b] = u[b] * e(P_DIA) + total
    for a, b in SHEAR:
        g[a] = g[b] = (u[a] + u[b]) * e(S_ALL)
    for m in TWIST:
        g[m] = u[m] * e(T_ALL)
    return g


def _density_of_energy(u):
    def sq(x):
        return x * x

    e = N_OFF * sq(u[NORMAL[0]] + u[NORMAL[1]] + u[NORMAL[2]])
    e = e + N_DIA * (sq(u[NORMAL[0]]) + sq(u[NORMAL[1]]) + sq(u[NORMAL[2]]))
    e = e + B_OFF * sq(u[BEND[0]] + u[BEND[1]] + u[BEND[2]])
    e = e + B_DIA * (sq(u[BEND[0]]) + sq(u[BEND[1]]) + sq(u[BEND[2]]))
    off = dia = she = twi = 0.0
    for a, b in PAIRS:
        off = off + sq(u[a] + u[b])
        dia = dia + sq(u[a]) + sq(u[b])
    for a, b in SHEAR:
        she = she + sq(u[a] + u[b])
    for m in TWIST:
        twi = twi + sq(u[m])
    return e + P_OFF * off + P_DIA * dia + S_ALL * she + T_ALL * twi


def _apply(u_at, e_at, add, layers, y_low, columns, close, unroll=2):
    def tile(ct, _):
        for ex in layers:
            first = _stage(u_at, ex, y_low, ct)
            zero = jnp.zeros((8, NZ), jnp.float32)

            def emit(y, h, ex=ex):
                for k in range(3):
                    for pz in (0, 1):
                        p0, p1 = h[k, 0, pz], h[k, 1, pz]
                        add(k, pz, ex, ex, y, ct, p0, p1)
                        add(k, pz, ex, ex + 1, y, ct, p0, p1)

            def step(t, state, ex=ex):
                s0 = dict(zip(KEYS, state[0]))
                carry = dict(zip(KEYS, state[1]))
                y = y_low + t
                s1 = _stage(u_at, ex, y + 1, ct)
                g = _stress(_modes(s0, s1), functools.partial(e_at, ex, y))
                h, later = {}, {}
                for key in KEYS:
                    k, px, pz = key
                    g1 = g[k, (px, 1, pz)]
                    g0 = g.get((k, (px, 0, pz)))
                    if g0 is None:
                        h[key] = carry[key] - g1
                        later[key] = g1
                    else:
                        h[key] = carry[key] + (g0 - g1)
                        later[key] = g0 + g1
                emit(y, h)
                return tuple(s1[key] for key in KEYS), tuple(later[key] for key in KEYS)

            state = (tuple(first[key] for key in KEYS), (zero,) * len(KEYS))
            if columns == 1:
                state = step(0, state)
            else:
                state = lax.fori_loop(0, columns, step, state, unroll=unroll)
            if close:
                emit(y_low + columns, dict(zip(KEYS, state[1])))
        return 0

    lax.fori_loop(0, CT, tile, 0)


def _sum_diff(u):
    up = _shift(u, 1)
    return u + up, up - u


def _gather_z(s, d):
    return (s - d) + _shift(s + d, -1)


def _loop2(xs, ys, body, state=0, unroll=1):
    def outer(x, state):
        return lax.fori_loop(ys[0], ys[1], lambda y, st: body(x, y, st), state, unroll=unroll)

    return lax.fori_loop(xs[0], xs[1], outer, state)


def _split(x):
    scaled = x * 65537.0
    high = scaled - (scaled - x)
    return high.astype(jnp.bfloat16), (x - high).astype(jnp.bfloat16)


def _rows(x):
    return x.reshape(CASES, NZ)


def _nt(a, b):
    return lax.dot_general(a, b, (((1,), (1,)), ((), ())), preferred_element_type=jnp.float32)


def _system(table):
    lane = lax.broadcasted_iota(jnp.int32, (CASES, NZ), 1)

    def left(x, by):
        return pltpu.roll(x, (-by) % NZ, axis=1)

    def join(a, b):
        return jnp.where(lane < 24, a, jnp.where(lane < 48, b, 0.0))

    blocks = [
        join(table, left(table, 24)),
        join(left(table, 48), left(table, 72)),
        join(left(table, 24), left(table, 48)),
    ]
    return [b[8 * i : 8 * i + 8] for b in blocks for i in range(3)]


def _eliminate(tiles, scales, steps, width=4):
    lane = lax.broadcasted_iota(jnp.int32, (8, NZ), 1)

    def one_row(x, r):
        return jnp.broadcast_to(x[r : r + 1], (8, NZ))

    for first in range(steps.start, steps.stop, width):
        own, at = first // 8, first % 8
        live = range(own, 9)
        cols = [{t: jnp.broadcast_to(tiles[t][:, first + m : first + m + 1], (8, NZ)) for t in live} for m in range(width)]
        rows = [one_row(tiles[own], at + m) for m in range(width)]
        factors = []
        for m in range(width):
            scale = 1.0 / one_row(cols[m][own], at + m)
            factor = jnp.where(lane == first + m, 0.0, rows[m] * scale)
            scales = jnp.where(lane == first + m, scale, scales)
            factors.append(factor)
            for later in range(m + 1, width):
                share = one_row(cols[later][own], at + m) * scale
                rows[later] = rows[later] - one_row(cols[m][own], at + later) * factor
                for t in live:
                    cols[later][t] = cols[later][t] - cols[m][t] * share
        for t in live:
            for m in range(width):
                tiles[t] = tiles[t] - cols[m][t] * factors[m]
    return tiles, scales


def _weight(dx, dy, dz):
    return max(0.0, 2.5 - math.sqrt(dx * dx + dy * dy + dz * dz))


def _cone(planes):
    by_row = {}
    for p in range(BX + 4):
        by_row[p, 0] = planes[p, BY : 2 * BY]
        for dy in (1, 2):
            by_row[p, dy] = planes[p, BY + dy : 2 * BY + dy] + planes[p, BY - dy : 2 * BY - dy]
    result = []
    for xo in range(BX):
        total = None
        for dz in range(3):
            part = jnp.zeros((BY, NZ), jnp.float32)
            for dx in range(-2, 3):
                for dy in range(3):
                    w = _weight(dx, dy, dz)
                    if w > 0.0:
                        part = part + w * by_row[xo + 2 + dx, dy]
            total = part if dz == 0 else total + (_shift(part, dz) + _shift(part, -dz))
        result.append(total)
    return result


SET_A = [(dx, dy, _span(dx, -1, 2, BX), _span(dy, -1, 8, BY)) for dx, dy in NEIGHBOURS]
SET_B = [
    (-1, 0, (1, 3, 1), (0, 0, BY)),
    (0, -1, (0, 0, BX), (1, 9, 1)),
    (-1, 1, (1, 3, 1), (7, -1, 1)),
    (-1, -1, (1, 3, 1), (0, 8, 2)),
    (-1, -1, (0, 2, 1), (1, 9, 1)),
    (1, -1, (1, -1, 1), (1, 9, 1)),
]


def _kernel(nx, ny, phases, phases2, forces, levels, supports, out, nat, lev, sup, stiff, stiffz, inv, free, field, dire, masked,
            image, qm, wf, split, disp, energy, vals, rim, gram_send, gram_recv, last_send, last_recv, local_sem, l_send, l_recv, s_send,
            s_recv, f_send, f_recv, v_send, v_recv, g_send, g_recv, n_send, n_recv):
    i, j = lax.axis_index("gx"), lax.axis_index("gy")

    def there(dx, dy):
        return lax.rem(i + dx + nx, nx), lax.rem(j + dy + ny, ny)

    peers = [there(dx, dy) for dx, dy in NEIGHBOURS]
    for phase in phases:
        for ox, oy in phase:
            peers.append((i ^ ox, j ^ oy))

    c_nat = pltpu.make_async_copy(forces, nat, local_sem.at[0])
    c_lev = pltpu.make_async_copy(levels, lev.at[2 : 2 + BX, 2 : 2 + BY], local_sem.at[1])
    c_sup = pltpu.make_async_copy(supports, sup.at[1 : 1 + BX, 1 : 1 + BY], local_sem.at[2])
    c_nat.start()
    c_lev.start()
    c_sup.start()

    barrier = pltpu.get_barrier_semaphore()
    for peer in peers:
        pl.semaphore_signal(barrier, inc=1, device_id=peer, device_id_type=MESH)

    c_nat.wait()

    def arrange(k, _):
        for x in range(BX):
            for y in range(BY):
                rows = nat[pl.ds(k * (CASES * BX * BY) + x * BY + y, CASES, stride=BX * BY), :]
                field[k, 1 + x, 1 + y] = rows.reshape(CT, 8, NZ)
        return 0

    lax.fori_loop(0, 3, arrange, 0)
    c_lev.wait()
    c_sup.wait()

    pl.semaphore_wait(barrier, len(peers))

    small = []
    for n, (dx, dy) in enumerate(NEIGHBOURS):
        (a, b, c), (d, e, f) = _span(dx, -2, 3, BX), _span(dy, -2, 9, BY)
        small.append(pltpu.make_async_remote_copy(
            levels.at[a : a + c, d : d + f], lev.at[b + 2 : b + 2 + c, e + 2 : e + 2 + f],
            l_send.at[n], l_recv.at[n], device_id=there(dx, dy), device_id_type=MESH))
        (a, b, c), (d, e, f) = _span(dx, -1, 3, BX), _span(dy, -1, 9, BY)
        small.append(pltpu.make_async_remote_copy(
            supports.at[a : a + c, d : d + f], sup.at[b + 1 : b + 1 + c, e + 1 : e + 1 + f],
            s_send.at[n], s_recv.at[n], device_id=there(dx, dy), device_id_type=MESH))

    halo = []
    for n, (dx, dy, (a, b, c), (d, e, f)) in enumerate(SET_A + SET_B):
        halo.append(pltpu.make_async_remote_copy(
            field.at[:, a + 1 : a + 1 + c, d + 1 : d + 1 + f], field.at[:, b + 1 : b + 1 + c, e + 1 : e + 1 + f],
            f_send.at[n], f_recv.at[n], device_id=there(dx, dy), device_id_type=MESH))
    near, far = halo[: len(SET_A)], halo[len(SET_A) :]
    edge_y = [copy for copy, (dx, _, _, _) in zip(near, SET_A) if dx == 0]
    edge_x = [copy for copy, (dx, _, _, _) in zip(near, SET_A) if dx != 0]
    for copy in small + near + far:
        copy.start()
    for copy in small:
        copy.wait_recv()

    def inside(x, y):
        gx, gy = i * BX + x, j * BY + y
        ok = (gx >= 0) & (gx < nx * BX) & (gy >= 0) & (gy < ny * BY)
        return jnp.where(ok, 1.0, 0.0).astype(jnp.float32)

    def moduli(x, y, _):
        level = jnp.broadcast_to(lev[x, y], (8, NZ)).astype(jnp.float32)
        rho = 0.3 + 0.7 * level / (LEVELS - 1)
        e = rho * rho * rho * inside(x - 2, y - 2)
        for n, c in enumerate(SCALES):
            stiff[x, y, n] = e * float(c)
        stiffz[x, y] = (e + _shift(e, -1)) * DIAG
        return 0

    _loop2((0, BX + 4), (0, BY + 4), moduli, unroll=4)

    def nodal(x, y, _):
        fr = (1 - jnp.broadcast_to(sup[x, y], (8, NZ))).astype(jnp.float32) * inside(x - 1, y - 1)
        total = (stiffz[x, y] + stiffz[x + 1, y]) + (stiffz[x, y + 1] + stiffz[x + 1, y + 1])
        free[x, y] = fr
        inv[x, y] = 1.0 / (fr * total + (1.0 - fr))
        return 0

    _loop2((0, BX + 3), (0, BY + 3), nodal, unroll=3)

    def search(x, y, _):
        fr, iv = free[x, y], inv[x, y]
        for k in range(3):
            d = iv * (LOAD * fr * field[k, x, y])
            dire[k, x, y] = d
            s, t = _sum_diff(fr * d)
            masked[k, 0, x, y] = s
            masked[k, 1, x, y] = t
        return 0

    for copy in edge_y:
        copy.wait_recv()
    _loop2((1, 1 + BX), (0, BY + 2), search, unroll=2)

    def u_at(k, pz, x, y, ct):
        return masked[k, pz, x + 1, y + 1, ct]

    def e_at(x, y, n):
        return stiff[x + 2, y + 2, n]

    def adder(ref, fresh, shift, planes):
        def add(k, pz, ex, x, y, ct, p0, p1):
            if x not in planes:
                return
            value = p0 - p1 if x == ex else p0 + p1
            if fresh(ex, x):
                ref[k, pz, x, y + shift, ct] = value
            else:
                ref[k, pz, x, y + shift, ct] += value
        return add

    at_nodes = range(BX + 1)
    add_near = adder(image, lambda ex, x: ex == 0 or x == BX, 1, at_nodes)
    _apply(u_at, e_at, add_near, range(0, 1), -1, BY + 1, True, unroll=3)
    for copy in edge_x:
        copy.wait_recv()
    _loop2((0, 1), (0, BY + 2), search, unroll=2)
    _loop2((BX + 1, BX + 2), (0, BY + 2), search, unroll=2)
    _apply(u_at, e_at, add_near, (-1, BX - 1), -1, BY + 1, True, unroll=3)

    gap8 = jnp.zeros((8, NZ), jnp.float32)
    gap32 = jnp.zeros((32, NZ), jnp.bfloat16)

    def above(x, y):
        fr, iv = free[x + 1, y + 1], inv[x + 1, y + 1]
        nodes = []
        for k in range(3):
            d = dire[k, x + 1, y + 1]
            im = fr * _gather_z(image[k, 0, x, y + 1], image[k, 1, x, y + 1]) + (1.0 - fr) * d
            q = iv * im
            s, t = _sum_diff(fr * q)
            qm[k, 0, x, y] = s
            qm[k, 1, x, y] = t
            nodes.append((d, im, q))
        return nodes, fr

    def first_gram(x, y, acc):
        nodes, fr = above(x, y)
        left, right = [], []
        for k, (d, im, q) in enumerate(nodes):
            r0 = LOAD * fr * field[k, x + 1, y + 1]
            held = jnp.concatenate([_rows((1.0 - fr) * q), gap8], 0).astype(jnp.bfloat16)
            left.append(jnp.concatenate(_split(jnp.concatenate([_rows(d), _rows(q)], 0)), 0))
            high, low = _split(jnp.concatenate([_rows(im), _rows(r0)], 0))
            right.append(jnp.concatenate([high, held[:16], low, held[16:]], 0))
        return acc + _nt(jnp.concatenate(left, 1), jnp.concatenate(right, 1))

    acc = _loop2((0, BX), (0, BY), first_gram, jnp.zeros((96, NZ), jnp.float32), unroll=4)
    lane = lax.broadcasted_iota(jnp.int32, (CASES, NZ), 1)
    both = acc[:48] + acc[48:]
    held = both[24:]
    held = jnp.where(lane < 112, pltpu.roll(held, 48, axis=1), held)
    both = both + pltpu.roll(both, 64, axis=1)
    table = jnp.where(lane < 48, both[:24], jnp.where(lane < 96, pltpu.roll(both[24:], 48, axis=1), held))

    sent = []

    def begin(n, value, groups, source, target, send_sem, recv_sem):
        slot = sum(len(p) for p in groups[:n])
        source[n] = value
        group = [pltpu.make_async_remote_copy(
            source.at[n], target.at[slot + m], send_sem.at[slot + m], recv_sem.at[slot + m],
            device_id=(i ^ ox, j ^ oy), device_id_type=MESH) for m, (ox, oy) in enumerate(groups[n])]
        for copy in group:
            copy.start()
        sent.extend(group)
        return value, slot, group, target

    def begin1(n, value):
        return begin(n, value, phases, gram_send, gram_recv, g_send, g_recv)

    def begin2(n, value):
        return begin(n, value, phases2, last_send, last_recv, n_send, n_recv)

    def finish(going):
        value, slot, group, target = going
        for copy in group:
            copy.wait_recv()
        terms = [value] + [target[slot + m] for m in range(len(group))]
        while len(terms) > 1:
            terms = [terms[t] + terms[t + 1] for t in range(0, len(terms), 2)]
        return terms[0]

    todo = list(range(len(phases)))
    going = begin1(todo.pop(0), table)

    def pair(left, right, acc):
        a, b = [], []
        for u, v in zip(left, right):
            a.append(jnp.concatenate(_split(jnp.concatenate([_rows(u), gap8], 0)), 0))
            high, low = _split(jnp.concatenate([_rows(v), gap8], 0))
            b.append(jnp.concatenate([high, gap32, low, gap32], 0))
        return acc + _nt(jnp.concatenate(a, 1), jnp.concatenate(b, 1))

    for copy in far:
        copy.wait_recv()
    _loop2((BX + 2, BX + 3), (0, BY + 3), search, unroll=BY + 3)
    for x in range(BX + 2):
        search(x, BY + 2, 0)
    _apply(u_at, e_at, adder(image, lambda ex, x: False, 1, at_nodes), range(-1, BX), BY, 1, False)
    _apply(u_at, e_at, adder(image, lambda ex, x: False, 1, at_nodes), range(BX, BX + 1), -1, BY + 2, False, unroll=2)

    def edge(x, y, _):
        above(x, y)
        return 0

    _loop2((BX, BX + 1), (0, BY + 1), edge, unroll=BY + 1)
    for x in range(BX):
        edge(x, BY, 0)

    def q_at(k, pz, x, y, ct):
        return qm[k, pz, x, y, ct]

    _apply(q_at, e_at, adder(wf, lambda ex, x: x == ex + 1 or ex == 0, 0, at_nodes), range(BX), 0, BY, True, unroll=2)
    if todo:
        going = begin1(todo.pop(0), finish(going))

    def second_gram(x, y, acc):
        at = [(k, pz) for k in range(3) for pz in (0, 1)]
        return pair([qm[k, pz, x, y] for k, pz in at], [wf[k, pz, x, y] for k, pz in at], acc)

    acc2 = _loop2((0, BX + 1), (0, BY + 1), second_gram, jnp.zeros((64, NZ), jnp.float32), unroll=9)
    last = acc2[:24] + acc2[32:56]
    last = last + pltpu.roll(last, 64, axis=1)
    last = jnp.where(lane < 24, last, 0.0)
    last = last[:8] + pltpu.roll(last[8:16], 24, axis=1) + pltpu.roll(last[16:], 48, axis=1)
    n_going = begin2(0, last)
    while todo:
        going = begin1(todo.pop(0), finish(going))

    def prepare(x, y, _):
        for k in range(3):
            for pz in (0, 1):
                both = jnp.concatenate([_rows(masked[k, pz, x + 1, y + 1]), _rows(qm[k, pz, x, y])], 0)
                split[k, x, y, :, pz * NZ : pz * NZ + NZ] = jnp.concatenate(_split(both), 0)
        return 0

    _loop2((0, BX + 1), (0, BY + 1), prepare, unroll=3)

    n_todo = list(range(1, len(phases2)))
    if n_todo:
        n_going = begin2(n_todo.pop(0), finish(n_going))
    table = finish(going)
    tiles, scales = _eliminate(_system(table), jnp.zeros((8, NZ), jnp.float32), range(24))

    def block(p, t):
        return inside(BX * ((p - 2) // BX), BY * (t - 1))

    for p in range(BX + 4):
        for t in range(3):
            rim[p, BY * t : BY * t + BY] = jnp.zeros((BY, NZ), jnp.float32) + block(p, t)
    weights = _cone(rim)
    rho = [0.3 + 0.7 * lev[2 + x, 2 : 2 + BY, 0, :].astype(jnp.float32) / (LEVELS - 1) for x in range(BX)]

    last = finish(n_going)
    lane8 = lax.broadcasted_iota(jnp.int32, (8, NZ), 1)
    for t in range(3):
        rows = last if t == 1 else pltpu.roll(last, (24 * (1 - t)) % NZ, axis=1)
        tiles[3 + t] = tiles[3 + t] + jnp.where((lane8 >= 24) & (lane8 < 48), rows, 0.0)
    tiles, scales = _eliminate(tiles, scales, range(24, 48))
    half = jnp.concatenate([t * scales for t in tiles[6:]], 0)
    mix = half + pltpu.roll(half, 48, axis=1)
    mix = jnp.concatenate([mix, gap8], 0)
    high, low = _split(mix)
    coefs = jnp.concatenate([high, low], 0)[:, :96]

    def combine(x, y, _):
        for k in range(3):
            u = jnp.dot(coefs, split[k, x, y], preferred_element_type=jnp.float32)
            u = u[:24] + u[32:56]
            for pz in (0, 1):
                disp[k, pz, x, y] = u[:, pz * NZ : pz * NZ + NZ].reshape(CT, 8, NZ)
        return 0

    _loop2((0, BX + 1), (0, BY + 1), combine, unroll=9)

    def s_at(k, pz, x, y, ct):
        return disp[k, pz, x, y, ct]

    for x in range(BX):
        energy[x] = jnp.zeros((BY, 8, NZ), jnp.float32)

    def energies(ct, _):
        for x in range(BX):
            first = _stage(s_at, x, 0, ct)

            def step(y, state, x=x):
                s1 = _stage(s_at, x, y + 1, ct)
                energy[x, y] += _density_of_energy(_modes(dict(zip(KEYS, state)), s1))
                return tuple(s1[key] for key in KEYS)

            lax.fori_loop(0, BY, step, tuple(first[key] for key in KEYS), unroll=2)
        return 0

    lax.fori_loop(0, CT, energies, 0)

    for x in range(BX):
        sens = -3.0 * rho[x] * rho[x] * jnp.sum(energy[x], axis=1) / CASES
        vals[2 + x, BY : 2 * BY] = rho[x] * sens
    group = []
    for n, (dx, dy) in enumerate(NEIGHBOURS):
        at_x, at_y = 2 - BX * dx, BY - BY * dy
        group.append(pltpu.make_async_remote_copy(
            vals.at[2 : 2 + BX, BY : 2 * BY], vals.at[at_x : at_x + BX, at_y : at_y + BY], v_send.at[n], v_recv.at[n],
            device_id=there(dx, dy), device_id_type=MESH))
    for copy in group:
        copy.start()
    for copy in small + near + far + sent:
        copy.wait_send()
    for copy in group:
        copy.wait_recv()
    for p in range(BX + 4):
        for t in range(3):
            rim[p, BY * t : BY * t + BY] = vals[p, BY * t : BY * t + BY] * block(p, t)
    sums = _cone(rim)
    for x in range(BX):
        out[x] = sums[x] / (rho[x] * weights[x])
    for copy in group:
        copy.wait_send()


def _phases(nx, ny):
    core, along_x = [(1, 0)], [(2, 0), (0, 1), (2, 1)]
    along_y = [(4 * o, 0) for o in range(1, nx // 4)]
    along_z = [(0, 2 * o) for o in range(1, ny // 2)]

    def product(fast, slow):
        return [(a ^ c, b ^ d) for c, d in [(0, 0)] + slow for a, b in [(0, 0)] + fast][1:]

    first = [product(core, along_x), along_y, along_z]
    second = [product(core, along_x), product(along_y, along_z)]
    return [g for g in first if g], [g for g in second if g]


def solution(mesh):
    nx, ny = mesh.shape["gx"], mesh.shape["gy"]
    phases, phases2 = _phases(nx, ny)
    slots, slots2 = (sum(len(g) for g in p) for p in (phases, phases2))
    f32 = jnp.float32
    dma = pltpu.SemaphoreType.DMA
    any_space = pl.BlockSpec(memory_space=pl.ANY)

    def local(forces, levels, supports):
        return pl.pallas_call(
            functools.partial(_kernel, nx, ny, phases, phases2),
            out_shape=jax.ShapeDtypeStruct((BX, BY, NZ), f32),
            in_specs=[any_space] * 3,
            out_specs=pl.BlockSpec(memory_space=pltpu.VMEM),
            scratch_shapes=[
                pltpu.VMEM((3 * CASES * BX * BY, NZ), f32),
                pltpu.VMEM((BX + 4, BY + 4, 1, NZ), jnp.int32),
                pltpu.VMEM((BX + 3, BY + 3, 1, NZ), jnp.int32),
                pltpu.VMEM((BX + 4, BY + 4, len(SCALES), 8, NZ), f32),
                pltpu.VMEM((BX + 4, BY + 4, 8, NZ), f32),
                pltpu.VMEM((BX + 3, BY + 3, 8, NZ), f32),
                pltpu.VMEM((BX + 3, BY + 3, 8, NZ), f32),
                pltpu.VMEM((3, BX + 3, BY + 3, CT, 8, NZ), f32),
                pltpu.VMEM((3, BX + 3, BY + 3, CT, 8, NZ), f32),
                pltpu.VMEM((3, 2, BX + 3, BY + 3, CT, 8, NZ), f32),
                pltpu.VMEM((3, 2, BX + 1, BY + 2, CT, 8, NZ), f32),
                pltpu.VMEM((3, 2, BX + 1, BY + 1, CT, 8, NZ), f32),
                pltpu.VMEM((3, 2, BX + 1, BY + 1, CT, 8, NZ), f32),
                pltpu.VMEM((3, BX + 1, BY + 1, 96, 2 * NZ), jnp.bfloat16),
                pltpu.VMEM((3, 2, BX + 1, BY + 1, CT, 8, NZ), f32),
                pltpu.VMEM((BX, BY, 8, NZ), f32),
                pltpu.VMEM((BX + 4, 3 * BY, NZ), f32),
                pltpu.VMEM((BX + 4, 3 * BY, NZ), f32),
                pltpu.VMEM((len(phases), CASES, NZ), f32),
                pltpu.VMEM((slots, CASES, NZ), f32),
                pltpu.VMEM((len(phases2), 8, NZ), f32),
                pltpu.VMEM((slots2, 8, NZ), f32),
                dma((3,)),
                dma((8,)), dma((8,)), dma((8,)), dma((8,)), dma((14,)), dma((14,)), dma((8,)), dma((8,)),
                dma((slots,)), dma((slots,)), dma((slots2,)), dma((slots2,)),
            ],
            compiler_params=pltpu.CompilerParams(collective_id=0, has_side_effects=True),
        )(
            forces.reshape(3 * CASES * BX * BY, NZ),
            levels.reshape(BX, BY, 1, NZ),
            supports.reshape(BX, BY, 1, NZ),
        )

    return jax.shard_map(
        local,
        mesh=mesh,
        in_specs=(P(None, None, "gx", "gy", None), P("gx", "gy", None), P("gx", "gy", None)),
        out_specs=P("gx", "gy", None),
        check_vma=False,
    )
```

```python
import functools
import math

import jax
import jax.numpy as jnp
import numpy as np
from jax import lax
from jax.experimental import pallas as pl
from jax.experimental.pallas import tpu as pltpu
from jax.sharding import PartitionSpec as P

MESH = pl.DeviceIdType.MESH
CASES = 24
LEVELS = 16
LOAD = 0.2
BX, BY, NZ = 2, 8, 128
CT = 3


def element_matrix():
    poisson = 0.3
    lame_first = poisson / ((1.0 + poisson) * (1.0 - 2.0 * poisson))
    lame_shear = 1.0 / (2.0 * (1.0 + poisson))
    elastic = np.zeros((6, 6))
    elastic[:3, :3] = lame_first
    for position in range(3):
        elastic[position, position] += 2.0 * lame_shear
        elastic[position + 3, position + 3] = lame_shear
    points = [0.5 - 0.5 / math.sqrt(3.0), 0.5 + 0.5 / math.sqrt(3.0)]
    matrix = np.zeros((24, 24))
    for point_x in points:
        for point_y in points:
            for point_z in points:
                coords = (point_x, point_y, point_z)
                strain = np.zeros((6, 24))
                for corner in range(8):
                    bits = (corner >> 2 & 1, corner >> 1 & 1, corner & 1)
                    shape = [coords[n] if bits[n] else 1.0 - coords[n] for n in range(3)]
                    slopes = [1.0 if bits[n] else -1.0 for n in range(3)]
                    slope_x = slopes[0] * shape[1] * shape[2]
                    slope_y = shape[0] * slopes[1] * shape[2]
                    slope_z = shape[0] * shape[1] * slopes[2]
                    o = 3 * corner
                    strain[0, o] = slope_x
                    strain[1, o + 1] = slope_y
                    strain[2, o + 2] = slope_z
                    strain[3, o] = slope_y
                    strain[3, o + 1] = slope_x
                    strain[4, o + 1] = slope_z
                    strain[4, o + 2] = slope_y
                    strain[5, o] = slope_z
                    strain[5, o + 2] = slope_x
                matrix = matrix + strain.T @ elastic @ strain / 8.0
    return matrix


KE = element_matrix()
DIAG = float(KE[0, 0])


def parity_matrix():
    walsh = np.ones((8, 8))
    for mode in range(8):
        for corner in range(8):
            for n in range(3):
                if mode >> n & 1:
                    walsh[mode, corner] *= 2 * (corner >> n & 1) - 1
    big = np.kron(walsh, np.eye(3))
    return big @ KE @ big.T / 64.0


KP = parity_matrix()
UNIT = ((1, 0, 0), (0, 1, 0), (0, 0, 1))


def _flip(p, k):
    return tuple(a ^ b for a, b in zip(p, UNIT[k]))


def _kp(m, n):
    at = [3 * (4 * p[0] + 2 * p[1] + p[2]) + k for k, p in (m, n)]
    return float(KP[at[0], at[1]])


NORMAL = [(k, UNIT[k]) for k in range(3)]
BEND = [(k, _flip((1, 1, 1), k)) for k in range(3)]
PAIRS = [[(k, _flip(UNIT[s], k)) for k in range(3) if k != s] for s in range(3)]
SHEAR = []
TWIST = []
for _s in range(3):
    _a, _b = [k for k in range(3) if k != _s]
    SHEAR.append([(_a, UNIT[_b]), (_b, UNIT[_a])])
    TWIST.append((_s, (1, 1, 1)))
N_OFF = _kp(NORMAL[0], NORMAL[1])
N_DIA = _kp(NORMAL[0], NORMAL[0]) - N_OFF
P_OFF = _kp(PAIRS[0][0], PAIRS[0][1])
P_DIA = _kp(PAIRS[0][0], PAIRS[0][0]) - P_OFF
S_ALL = _kp(SHEAR[0][0], SHEAR[0][0])
T_ALL = _kp(TWIST[0], TWIST[0])
B_OFF = _kp(BEND[0], BEND[1])
B_DIA = _kp(BEND[0], BEND[0]) - B_OFF


def _span(d, low, high, size):
    a = max(0, low + d * size)
    b = min(size, high + 1 + d * size)
    return a, a - d * size, b - a


NEIGHBOURS = [(dx, dy) for dx in (-1, 0, 1) for dy in (-1, 0, 1) if dx or dy]


def _shift(x, by):
    lane = lax.broadcasted_iota(jnp.int32, x.shape, x.ndim - 1)
    r = pltpu.roll(x, (-by) % NZ, axis=x.ndim - 1)
    ok = lane < NZ - by if by > 0 else lane >= -by
    return jnp.where(ok, r, 0.0)


def _stage(u_at, ex, y, ct):
    out = {}
    for k in range(3):
        for pz in (0, 1):
            u0, u1 = u_at(k, pz, ex, y, ct), u_at(k, pz, ex + 1, y, ct)
            out[k, 0, pz] = u0 + u1
            out[k, 1, pz] = u1 - u0
    return out


KEYS = [(k, px, pz) for k in range(3) for px in (0, 1) for pz in (0, 1)]


def _modes(s0, s1):
    out = {}
    for k, px, pz in KEYS:
        if (px, pz) != (0, 0):
            out[k, (px, 0, pz)] = s0[k, px, pz] + s1[k, px, pz]
        out[k, (px, 1, pz)] = s1[k, px, pz] - s0[k, px, pz]
    return out


SCALES = sorted({np.float32(c) for c in (N_OFF, N_DIA, P_OFF, P_DIA, S_ALL, T_ALL, B_OFF, B_DIA)})


def _stress(u, e_at):
    def e(c):
        return e_at(SCALES.index(np.float32(c)))

    g = {}
    for group, off, dia in ((NORMAL, N_OFF, N_DIA), (BEND, B_OFF, B_DIA)):
        total = (u[group[0]] + u[group[1]] + u[group[2]]) * e(off)
        for m in group:
            g[m] = u[m] * e(dia) + total
    for a, b in PAIRS:
        total = (u[a] + u[b]) * e(P_OFF)
        g[a] = u[a] * e(P_DIA) + total
        g[b] = u[b] * e(P_DIA) + total
    for a, b in SHEAR:
        g[a] = g[b] = (u[a] + u[b]) * e(S_ALL)
    for m in TWIST:
        g[m] = u[m] * e(T_ALL)
    return g


def _density_of_energy(u):
    def sq(x):
        return x * x

    e = N_OFF * sq(u[NORMAL[0]] + u[NORMAL[1]] + u[NORMAL[2]])
    e = e + N_DIA * (sq(u[NORMAL[0]]) + sq(u[NORMAL[1]]) + sq(u[NORMAL[2]]))
    e = e + B_OFF * sq(u[BEND[0]] + u[BEND[1]] + u[BEND[2]])
    e = e + B_DIA * (sq(u[BEND[0]]) + sq(u[BEND[1]]) + sq(u[BEND[2]]))
    off = dia = she = twi = 0.0
    for a, b in PAIRS:
        off = off + sq(u[a] + u[b])
        dia = dia + sq(u[a]) + sq(u[b])
    for a, b in SHEAR:
        she = she + sq(u[a] + u[b])
    for m in TWIST:
        twi = twi + sq(u[m])
    return e + P_OFF * off + P_DIA * dia + S_ALL * she + T_ALL * twi


def _apply(u_at, e_at, add, layers, y_low, columns, close, unroll=2):
    def tile(ct, _):
        for ex in layers:
            first = _stage(u_at, ex, y_low, ct)
            zero = jnp.zeros((8, NZ), jnp.float32)

            def emit(y, h, ex=ex):
                for k in range(3):
                    for pz in (0, 1):
                        p0, p1 = h[k, 0, pz], h[k, 1, pz]
                        add(k, pz, ex, ex, y, ct, p0, p1)
                        add(k, pz, ex, ex + 1, y, ct, p0, p1)

            def step(t, state, ex=ex):
                s0 = dict(zip(KEYS, state[0]))
                carry = dict(zip(KEYS, state[1]))
                y = y_low + t
                s1 = _stage(u_at, ex, y + 1, ct)
                g = _stress(_modes(s0, s1), functools.partial(e_at, ex, y))
                h, later = {}, {}
                for key in KEYS:
                    k, px, pz = key
                    g1 = g[k, (px, 1, pz)]
                    g0 = g.get((k, (px, 0, pz)))
                    if g0 is None:
                        h[key] = carry[key] - g1
                        later[key] = g1
                    else:
                        h[key] = carry[key] + (g0 - g1)
                        later[key] = g0 + g1
                emit(y, h)
                return tuple(s1[key] for key in KEYS), tuple(later[key] for key in KEYS)

            state = (tuple(first[key] for key in KEYS), (zero,) * len(KEYS))
            if columns == 1:
                state = step(0, state)
            else:
                state = lax.fori_loop(0, columns, step, state, unroll=unroll)
            if close:
                emit(y_low + columns, dict(zip(KEYS, state[1])))
        return 0

    lax.fori_loop(0, CT, tile, 0)


def _sum_diff(u):
    up = _shift(u, 1)
    return u + up, up - u


def _gather_z(s, d):
    return (s - d) + _shift(s + d, -1)


def _loop2(xs, ys, body, state=0, unroll=1, planes=1):
    def outer(x, state):
        return lax.fori_loop(ys[0], ys[1], lambda y, st: body(x, y, st), state, unroll=unroll)

    return lax.fori_loop(xs[0], xs[1], outer, state, unroll=planes)


def _split(x):
    scaled = x * 65537.0
    high = scaled - (scaled - x)
    return high.astype(jnp.bfloat16), (x - high).astype(jnp.bfloat16)


def _rows(x):
    return x.reshape(CASES, NZ)


def _nt(a, b):
    return lax.dot_general(a, b, (((1,), (1,)), ((), ())), preferred_element_type=jnp.float32)


def _system(table):
    lane = lax.broadcasted_iota(jnp.int32, (CASES, NZ), 1)

    def left(x, by):
        return pltpu.roll(x, (-by) % NZ, axis=1)

    def join(a, b):
        return jnp.where(lane < 24, a, jnp.where(lane < 48, b, 0.0))

    blocks = [
        join(table, left(table, 24)),
        join(left(table, 48), left(table, 72)),
        join(left(table, 24), left(table, 48)),
    ]
    return [b[8 * i : 8 * i + 8] for b in blocks for i in range(3)]


def _eliminate(tiles, scales, steps, width=4):
    lane = lax.broadcasted_iota(jnp.int32, (8, NZ), 1)

    def one_row(x, r):
        return jnp.broadcast_to(x[r : r + 1], (8, NZ))

    for first in range(steps.start, steps.stop, width):
        own, at = first // 8, first % 8
        live = range(own, 9)
        cols = [{t: jnp.broadcast_to(tiles[t][:, first + m : first + m + 1], (8, NZ)) for t in live} for m in range(width)]
        rows = [one_row(tiles[own], at + m) for m in range(width)]
        factors = []
        for m in range(width):
            scale = 1.0 / one_row(cols[m][own], at + m)
            factor = jnp.where(lane == first + m, 0.0, rows[m] * scale)
            scales = jnp.where(lane == first + m, scale, scales)
            factors.append(factor)
            for later in range(m + 1, width):
                share = one_row(cols[later][own], at + m) * scale
                rows[later] = rows[later] - one_row(cols[m][own], at + later) * factor
                for t in live:
                    cols[later][t] = cols[later][t] - cols[m][t] * share
        for t in live:
            for m in range(width):
                tiles[t] = tiles[t] - cols[m][t] * factors[m]
    return tiles, scales


def _weight(dx, dy, dz):
    return max(0.0, 2.5 - math.sqrt(dx * dx + dy * dy + dz * dz))


def _cone(planes):
    by_row = {}
    for p in range(BX + 4):
        by_row[p, 0] = planes[p, BY : 2 * BY]
        for dy in (1, 2):
            by_row[p, dy] = planes[p, BY + dy : 2 * BY + dy] + planes[p, BY - dy : 2 * BY - dy]
    result = []
    for xo in range(BX):
        total = None
        for dz in range(3):
            part = jnp.zeros((BY, NZ), jnp.float32)
            for dx in range(-2, 3):
                for dy in range(3):
                    w = _weight(dx, dy, dz)
                    if w > 0.0:
                        part = part + w * by_row[xo + 2 + dx, dy]
            total = part if dz == 0 else total + (_shift(part, dz) + _shift(part, -dz))
        result.append(total)
    return result


SET_A = [(dx, dy, _span(dx, -1, 2, BX), _span(dy, -1, 8, BY)) for dx, dy in NEIGHBOURS]
SET_B = [
    (-1, 0, (1, 3, 1), (0, 0, BY)),
    (0, -1, (0, 0, BX), (1, 9, 1)),
    (-1, 1, (1, 3, 1), (7, -1, 1)),
    (-1, -1, (1, 3, 1), (0, 8, 2)),
    (-1, -1, (0, 2, 1), (1, 9, 1)),
    (1, -1, (1, -1, 1), (1, 9, 1)),
]


def _kernel(nx, ny, phases, phases2, forces, levels, supports, out, nat, lev, sup, stiff, stiffz, inv, free, field, dire, masked,
            image, qm, wf, split, disp, energy, vals, rim, gram_send, gram_recv, last_send, last_recv, local_sem, l_send, l_recv, s_send,
            s_recv, f_send, f_recv, v_send, v_recv, g_send, g_recv, n_send, n_recv):
    i, j = lax.axis_index("gx"), lax.axis_index("gy")

    def there(dx, dy):
        return lax.rem(i + dx + nx, nx), lax.rem(j + dy + ny, ny)

    peers = [there(dx, dy) for dx, dy in NEIGHBOURS]
    for phase in phases:
        for ox, oy in phase:
            peers.append((i ^ ox, j ^ oy))

    c_nat = pltpu.make_async_copy(forces, nat, local_sem.at[0])
    c_lev = pltpu.make_async_copy(levels, lev.at[2 : 2 + BX, 2 : 2 + BY], local_sem.at[1])
    c_sup = pltpu.make_async_copy(supports, sup.at[1 : 1 + BX, 1 : 1 + BY], local_sem.at[2])
    c_nat.start()
    c_lev.start()
    c_sup.start()

    barrier = pltpu.get_barrier_semaphore()
    for peer in peers:
        pl.semaphore_signal(barrier, inc=1, device_id=peer, device_id_type=MESH)

    c_nat.wait()

    def arrange(k, _):
        for x in range(BX):
            for y in range(BY):
                rows = nat[pl.ds(k * (CASES * BX * BY) + x * BY + y, CASES, stride=BX * BY), :]
                field[k, 1 + x, 1 + y] = rows.reshape(CT, 8, NZ)
        return 0

    lax.fori_loop(0, 3, arrange, 0)
    c_lev.wait()
    c_sup.wait()

    pl.semaphore_wait(barrier, len(peers))

    small = []
    for n, (dx, dy) in enumerate(NEIGHBOURS):
        (a, b, c), (d, e, f) = _span(dx, -2, 3, BX), _span(dy, -2, 9, BY)
        small.append(pltpu.make_async_remote_copy(
            levels.at[a : a + c, d : d + f], lev.at[b + 2 : b + 2 + c, e + 2 : e + 2 + f],
            l_send.at[n], l_recv.at[n], device_id=there(dx, dy), device_id_type=MESH))
        (a, b, c), (d, e, f) = _span(dx, -1, 3, BX), _span(dy, -1, 9, BY)
        small.append(pltpu.make_async_remote_copy(
            supports.at[a : a + c, d : d + f], sup.at[b + 1 : b + 1 + c, e + 1 : e + 1 + f],
            s_send.at[n], s_recv.at[n], device_id=there(dx, dy), device_id_type=MESH))

    halo = []
    for n, (dx, dy, (a, b, c), (d, e, f)) in enumerate(SET_A + SET_B):
        halo.append(pltpu.make_async_remote_copy(
            field.at[:, a + 1 : a + 1 + c, d + 1 : d + 1 + f], field.at[:, b + 1 : b + 1 + c, e + 1 : e + 1 + f],
            f_send.at[n], f_recv.at[n], device_id=there(dx, dy), device_id_type=MESH))
    near, far = halo[: len(SET_A)], halo[len(SET_A) :]
    edge_y = [copy for copy, (dx, _, _, _) in zip(near, SET_A) if dx == 0]
    edge_x = [copy for copy, (dx, _, _, _) in zip(near, SET_A) if dx != 0]
    for copy in small + near + far:
        copy.start()
    for copy in small:
        copy.wait_recv()

    def inside(x, y):
        gx, gy = i * BX + x, j * BY + y
        ok = (gx >= 0) & (gx < nx * BX) & (gy >= 0) & (gy < ny * BY)
        return jnp.where(ok, 1.0, 0.0).astype(jnp.float32)

    def moduli(x, y, _):
        level = jnp.broadcast_to(lev[x, y], (8, NZ)).astype(jnp.float32)
        rho = 0.3 + 0.7 * level / (LEVELS - 1)
        e = rho * rho * rho * inside(x - 2, y - 2)
        for n, c in enumerate(SCALES):
            stiff[x, y, n] = e * float(c)
        stiffz[x, y] = (e + _shift(e, -1)) * DIAG
        return 0

    _loop2((0, BX + 4), (0, BY + 4), moduli, unroll=4)

    def nodal(x, y, _):
        fr = (1 - jnp.broadcast_to(sup[x, y], (8, NZ))).astype(jnp.float32) * inside(x - 1, y - 1)
        total = (stiffz[x, y] + stiffz[x + 1, y]) + (stiffz[x, y + 1] + stiffz[x + 1, y + 1])
        free[x, y] = fr
        inv[x, y] = 1.0 / (fr * total + (1.0 - fr))
        return 0

    _loop2((0, BX + 3), (0, BY + 3), nodal, unroll=3)

    def search(x, y, _):
        fr, iv = free[x, y], inv[x, y]
        for k in range(3):
            d = iv * (LOAD * fr * field[k, x, y])
            dire[k, x, y] = d
            s, t = _sum_diff(fr * d)
            masked[k, 0, x, y] = s
            masked[k, 1, x, y] = t
        return 0

    for copy in edge_y:
        copy.wait_recv()
    _loop2((1, 1 + BX), (0, BY + 2), search, unroll=2)

    def u_at(k, pz, x, y, ct):
        return masked[k, pz, x + 1, y + 1, ct]

    def e_at(x, y, n):
        return stiff[x + 2, y + 2, n]

    def adder(ref, fresh, shift, planes):
        def add(k, pz, ex, x, y, ct, p0, p1):
            if x not in planes:
                return
            value = p0 - p1 if x == ex else p0 + p1
            if fresh(ex, x):
                ref[k, pz, x, y + shift, ct] = value
            else:
                ref[k, pz, x, y + shift, ct] += value
        return add

    at_nodes = range(BX + 1)
    add_near = adder(image, lambda ex, x: ex == 0 or x == BX, 1, at_nodes)
    _apply(u_at, e_at, add_near, range(0, 1), -1, BY + 1, True, unroll=3)
    for copy in edge_x:
        copy.wait_recv()
    _loop2((0, 1), (0, BY + 2), search, unroll=2)
    _loop2((BX + 1, BX + 2), (0, BY + 2), search, unroll=2)
    _apply(u_at, e_at, add_near, (-1, BX - 1), -1, BY + 1, True, unroll=3)

    gap8 = jnp.zeros((8, NZ), jnp.float32)
    gap32 = jnp.zeros((32, NZ), jnp.bfloat16)

    def above(x, y):
        fr, iv = free[x + 1, y + 1], inv[x + 1, y + 1]
        nodes = []
        for k in range(3):
            d = dire[k, x + 1, y + 1]
            im = fr * _gather_z(image[k, 0, x, y + 1], image[k, 1, x, y + 1]) + (1.0 - fr) * d
            q = iv * im
            s, t = _sum_diff(fr * q)
            qm[k, 0, x, y] = s
            qm[k, 1, x, y] = t
            nodes.append((d, im, q))
        return nodes, fr

    def first_gram(x, y, acc):
        nodes, fr = above(x, y)
        left, right = [], []
        for k, (d, im, q) in enumerate(nodes):
            r0 = LOAD * fr * field[k, x + 1, y + 1]
            held = jnp.concatenate([_rows((1.0 - fr) * q), gap8], 0).astype(jnp.bfloat16)
            left.append(jnp.concatenate(_split(jnp.concatenate([_rows(d), _rows(q)], 0)), 0))
            high, low = _split(jnp.concatenate([_rows(im), _rows(r0)], 0))
            right.append(jnp.concatenate([high, held[:16], low, held[16:]], 0))
        return acc + _nt(jnp.concatenate(left, 1), jnp.concatenate(right, 1))

    acc = _loop2((0, BX), (0, BY), first_gram, jnp.zeros((96, NZ), jnp.float32), unroll=4)
    lane = lax.broadcasted_iota(jnp.int32, (CASES, NZ), 1)
    both = acc[:48] + acc[48:]
    held = both[24:]
    held = jnp.where(lane < 112, pltpu.roll(held, 48, axis=1), held)
    both = both + pltpu.roll(both, 64, axis=1)
    table = jnp.where(lane < 48, both[:24], jnp.where(lane < 96, pltpu.roll(both[24:], 48, axis=1), held))

    sent = []

    def begin(n, value, groups, source, target, send_sem, recv_sem):
        slot = sum(len(p) for p in groups[:n])
        source[n] = value
        group = [pltpu.make_async_remote_copy(
            source.at[n], target.at[slot + m], send_sem.at[slot + m], recv_sem.at[slot + m],
            device_id=(i ^ ox, j ^ oy), device_id_type=MESH) for m, (ox, oy) in enumerate(groups[n])]
        for copy in group:
            copy.start()
        sent.extend(group)
        return value, slot, group, target

    def begin1(n, value):
        return begin(n, value, phases, gram_send, gram_recv, g_send, g_recv)

    def begin2(n, value):
        return begin(n, value, phases2, last_send, last_recv, n_send, n_recv)

    def finish(going):
        value, slot, group, target = going
        for copy in group:
            copy.wait_recv()
        terms = [value] + [target[slot + m] for m in range(len(group))]
        while len(terms) > 1:
            terms = [terms[t] + terms[t + 1] for t in range(0, len(terms), 2)]
        return terms[0]

    todo = list(range(len(phases)))
    going = begin1(todo.pop(0), table)

    def pair(left, right, acc):
        a, b = [], []
        for u, v in zip(left, right):
            a.append(jnp.concatenate(_split(jnp.concatenate([_rows(u), gap8], 0)), 0))
            high, low = _split(jnp.concatenate([_rows(v), gap8], 0))
            b.append(jnp.concatenate([high, gap32, low, gap32], 0))
        return acc + _nt(jnp.concatenate(a, 1), jnp.concatenate(b, 1))

    for copy in far:
        copy.wait_recv()
    _loop2((BX + 2, BX + 3), (0, BY + 3), search, unroll=BY + 3)
    for x in range(BX + 2):
        search(x, BY + 2, 0)
    _apply(u_at, e_at, adder(image, lambda ex, x: False, 1, at_nodes), range(-1, BX), BY, 1, False)
    _apply(u_at, e_at, adder(image, lambda ex, x: False, 1, at_nodes), range(BX, BX + 1), -1, BY + 2, False, unroll=2)

    def edge(x, y, _):
        above(x, y)
        return 0

    _loop2((BX, BX + 1), (0, BY + 1), edge, unroll=BY + 1)
    for x in range(BX):
        edge(x, BY, 0)

    def q_at(k, pz, x, y, ct):
        return qm[k, pz, x, y, ct]

    _apply(q_at, e_at, adder(wf, lambda ex, x: x == ex + 1 or ex == 0, 0, at_nodes), range(BX), 0, BY, True, unroll=2)
    if todo:
        going = begin1(todo.pop(0), finish(going))

    def second_gram(x, y, acc):
        at = [(k, pz) for k in range(3) for pz in (0, 1)]
        return pair([qm[k, pz, x, y] for k, pz in at], [wf[k, pz, x, y] for k, pz in at], acc)

    acc2 = _loop2((0, BX + 1), (0, BY + 1), second_gram, jnp.zeros((64, NZ), jnp.float32), unroll=9, planes=3)
    last = acc2[:24] + acc2[32:56]
    last = last + pltpu.roll(last, 64, axis=1)
    last = jnp.where(lane < 24, last, 0.0)
    last = last[:8] + pltpu.roll(last[8:16], 24, axis=1) + pltpu.roll(last[16:], 48, axis=1)
    n_going = begin2(0, last)
    while todo:
        going = begin1(todo.pop(0), finish(going))

    def prepare(x, y, _):
        for k in range(3):
            for pz in (0, 1):
                both = jnp.concatenate([_rows(masked[k, pz, x + 1, y + 1]), _rows(qm[k, pz, x, y])], 0)
                split[k, x, y, :, pz * NZ : pz * NZ + NZ] = jnp.concatenate(_split(both), 0)
        return 0

    _loop2((0, BX + 1), (0, BY + 1), prepare, unroll=3)

    n_todo = list(range(1, len(phases2)))
    if n_todo:
        n_going = begin2(n_todo.pop(0), finish(n_going))
    table = finish(going)
    tiles, scales = _eliminate(_system(table), jnp.zeros((8, NZ), jnp.float32), range(24))

    def block(p, t):
        return inside(BX * ((p - 2) // BX), BY * (t - 1))

    for p in range(BX + 4):
        for t in range(3):
            rim[p, BY * t : BY * t + BY] = jnp.zeros((BY, NZ), jnp.float32) + block(p, t)
    weights = _cone(rim)
    rho = [0.3 + 0.7 * lev[2 + x, 2 : 2 + BY, 0, :].astype(jnp.float32) / (LEVELS - 1) for x in range(BX)]

    last = finish(n_going)
    lane8 = lax.broadcasted_iota(jnp.int32, (8, NZ), 1)
    for t in range(3):
        rows = last if t == 1 else pltpu.roll(last, (24 * (1 - t)) % NZ, axis=1)
        tiles[3 + t] = tiles[3 + t] + jnp.where((lane8 >= 24) & (lane8 < 48), rows, 0.0)
    tiles, scales = _eliminate(tiles, scales, range(24, 48))
    half = jnp.concatenate([t * scales for t in tiles[6:]], 0)
    mix = half + pltpu.roll(half, 48, axis=1)
    mix = jnp.concatenate([mix, gap8], 0)
    high, low = _split(mix)
    coefs = jnp.concatenate([high, low], 0)[:, :96]

    def combine(x, y, _):
        for k in range(3):
            u = jnp.dot(coefs, split[k, x, y], preferred_element_type=jnp.float32)
            u = u[:24] + u[32:56]
            for pz in (0, 1):
                disp[k, pz, x, y] = u[:, pz * NZ : pz * NZ + NZ].reshape(CT, 8, NZ)
        return 0

    _loop2((0, BX + 1), (0, BY + 1), combine, unroll=9, planes=3)

    def s_at(k, pz, x, y, ct):
        return disp[k, pz, x, y, ct]

    for x in range(BX):
        energy[x] = jnp.zeros((BY, 8, NZ), jnp.float32)

    def energies(ct, _):
        for x in range(BX):
            first = _stage(s_at, x, 0, ct)

            def step(y, state, x=x):
                s1 = _stage(s_at, x, y + 1, ct)
                energy[x, y] += _density_of_energy(_modes(dict(zip(KEYS, state)), s1))
                return tuple(s1[key] for key in KEYS)

            lax.fori_loop(0, BY, step, tuple(first[key] for key in KEYS), unroll=2)
        return 0

    lax.fori_loop(0, CT, energies, 0)

    for x in range(BX):
        sens = -3.0 * rho[x] * rho[x] * jnp.sum(energy[x], axis=1) / CASES
        vals[2 + x, BY : 2 * BY] = rho[x] * sens
    group = []
    for n, (dx, dy) in enumerate(NEIGHBOURS):
        at_x, at_y = 2 - BX * dx, BY - BY * dy
        group.append(pltpu.make_async_remote_copy(
            vals.at[2 : 2 + BX, BY : 2 * BY], vals.at[at_x : at_x + BX, at_y : at_y + BY], v_send.at[n], v_recv.at[n],
            device_id=there(dx, dy), device_id_type=MESH))
    for copy in group:
        copy.start()
    for copy in small + near + far + sent:
        copy.wait_send()
    for copy in group:
        copy.wait_recv()
    for p in range(BX + 4):
        for t in range(3):
            rim[p, BY * t : BY * t + BY] = vals[p, BY * t : BY * t + BY] * block(p, t)
    sums = _cone(rim)
    for x in range(BX):
        out[x] = sums[x] / (rho[x] * weights[x])
    for copy in group:
        copy.wait_send()


def _phases(nx, ny):
    core, along_x = [(1, 0)], [(2, 0), (0, 1), (2, 1)]
    along_y = [(4 * o, 0) for o in range(1, nx // 4)]
    along_z = [(0, 2 * o) for o in range(1, ny // 2)]

    def product(fast, slow):
        return [(a ^ c, b ^ d) for c, d in [(0, 0)] + slow for a, b in [(0, 0)] + fast][1:]

    first = [product(core, along_x), along_y, along_z]
    second = [product(core, along_x), product(along_y, along_z)]
    return [g for g in first if g], [g for g in second if g]


def solution(mesh):
    nx, ny = mesh.shape["gx"], mesh.shape["gy"]
    phases, phases2 = _phases(nx, ny)
    slots, slots2 = (sum(len(g) for g in p) for p in (phases, phases2))
    f32 = jnp.float32
    dma = pltpu.SemaphoreType.DMA
    any_space = pl.BlockSpec(memory_space=pl.ANY)

    def local(forces, levels, supports):
        return pl.pallas_call(
            functools.partial(_kernel, nx, ny, phases, phases2),
            out_shape=jax.ShapeDtypeStruct((BX, BY, NZ), f32),
            in_specs=[any_space] * 3,
            out_specs=pl.BlockSpec(memory_space=pltpu.VMEM),
            scratch_shapes=[
                pltpu.VMEM((3 * CASES * BX * BY, NZ), f32),
                pltpu.VMEM((BX + 4, BY + 4, 1, NZ), jnp.int32),
                pltpu.VMEM((BX + 3, BY + 3, 1, NZ), jnp.int32),
                pltpu.VMEM((BX + 4, BY + 4, len(SCALES), 8, NZ), f32),
                pltpu.VMEM((BX + 4, BY + 4, 8, NZ), f32),
                pltpu.VMEM((BX + 3, BY + 3, 8, NZ), f32),
                pltpu.VMEM((BX + 3, BY + 3, 8, NZ), f32),
                pltpu.VMEM((3, BX + 3, BY + 3, CT, 8, NZ), f32),
                pltpu.VMEM((3, BX + 3, BY + 3, CT, 8, NZ), f32),
                pltpu.VMEM((3, 2, BX + 3, BY + 3, CT, 8, NZ), f32),
                pltpu.VMEM((3, 2, BX + 1, BY + 2, CT, 8, NZ), f32),
                pltpu.VMEM((3, 2, BX + 1, BY + 1, CT, 8, NZ), f32),
                pltpu.VMEM((3, 2, BX + 1, BY + 1, CT, 8, NZ), f32),
                pltpu.VMEM((3, BX + 1, BY + 1, 96, 2 * NZ), jnp.bfloat16),
                pltpu.VMEM((3, 2, BX + 1, BY + 1, CT, 8, NZ), f32),
                pltpu.VMEM((BX, BY, 8, NZ), f32),
                pltpu.VMEM((BX + 4, 3 * BY, NZ), f32),
                pltpu.VMEM((BX + 4, 3 * BY, NZ), f32),
                pltpu.VMEM((len(phases), CASES, NZ), f32),
                pltpu.VMEM((slots, CASES, NZ), f32),
                pltpu.VMEM((len(phases2), 8, NZ), f32),
                pltpu.VMEM((slots2, 8, NZ), f32),
                dma((3,)),
                dma((8,)), dma((8,)), dma((8,)), dma((8,)), dma((14,)), dma((14,)), dma((8,)), dma((8,)),
                dma((slots,)), dma((slots,)), dma((slots2,)), dma((slots2,)),
            ],
            compiler_params=pltpu.CompilerParams(collective_id=0, has_side_effects=True),
        )(
            forces.reshape(3 * CASES * BX * BY, NZ),
            levels.reshape(BX, BY, 1, NZ),
            supports.reshape(BX, BY, 1, NZ),
        )

    return jax.shard_map(
        local,
        mesh=mesh,
        in_specs=(P(None, None, "gx", "gy", None), P("gx", "gy", None), P("gx", "gy", None)),
        out_specs=P("gx", "gy", None),
        check_vma=False,
    )
```
